32 devices in a mesh: kstr: 4 (over y, x), pw: 8 (over z, core).
Axes of the slice: x: 2, y: 2, z: 4, core: 2. Of those that a mesh axis runs over, the one named last changes fastest.
Arguments:
- states_re: bfloat16 [4, 256, 16384], P('kstr', None, 'pw'), may hold values from -8 to 8
- states_im: bfloat16 [4, 256, 16384], P('kstr', None, 'pw'), may hold values from -8 to 8
- gmap: int32 [16384], P('pw'), may hold values from 0 to 16383, as said below
Outputs:
- new_re: bfloat16 [4, 256, 16384], P('kstr', None, 'pw')
- new_im: bfloat16 [4, 256, 16384], P('kstr', None, 'pw')
The draws below stay inside these ranges and needn't reach their ends.
Inputs may be any that keep to these rules, and one draw needn't show every extreme that they name: gmap[G] = (G + o) mod 16384 for one offset o with 1 <= o < 16384.
All inputs are finite; a program needn't handle non-finite values.
Results may differ from the reference program's by a relative error of at most 0.008.
Values may be sent and summed in bfloat16 or wider, within the bound.
A program may use at most 64 MiB of HBM per device.

```python
import jax
import jax.numpy as jnp
from jax import lax

NB = 256
NPW = 16384
NEWTON = 4
STEPS = 2
NK = 4


def state_parts(key):
    base_key = jax.random.fold_in(key, 7)
    noise_key = jax.random.fold_in(key, 8)
    kpos = jnp.arange(NK, dtype=jnp.float32) / max(NK - 1, 1)
    base = jax.random.normal(base_key, (2, 1, NB, NPW), jnp.float32) * 0.7071
    noise = jax.random.normal(noise_key, (2, NK, NB, NPW), jnp.float32) * 0.7071
    bands = jnp.ones((1, 1, NB, 1), jnp.float32)
    amplitude = 1.0 / (1.0 + 2.0 * kpos)
    level = (0.15 * (1.0 + 2.0 * kpos))[None, :, None, None]
    gpos = jnp.arange(NPW, dtype=jnp.float32) / NPW
    column = (0.6 + 0.8 * gpos)[None, None, None, :]
    field = jnp.clip(amplitude[None, :, None, None] * (base + level * column * bands * noise), -8.0, 8.0)
    return (field[0], field[1])


def draw_states_re(key, part):
    return state_parts(key)[0].astype(jnp.bfloat16)


def draw_states_im(key, part):
    return state_parts(key)[1].astype(jnp.bfloat16)


def draw_gmap(key, part):
    offset = jax.random.randint(jax.random.fold_in(key, 11), (), 1, NPW)
    index = jnp.arange(NPW, dtype=jnp.int32)
    return jnp.mod(index + offset, NPW).astype(jnp.int32)


def setup_inputs(seed: int = 0) -> dict:
    key_list = jax.random.split(jax.random.key(seed), 4)
    states_re = draw_states_re(jax.random.fold_in(key_list[3], 71), 0)
    states_im = draw_states_im(jax.random.fold_in(key_list[3], 71), 0)
    gmap = draw_gmap(jax.random.fold_in(key_list[3], 71), 0)
    return {"states_re": states_re, "states_im": states_im, "gmap": gmap}


HIGH = lax.Precision.HIGHEST
EPS_SCALE = 1e-06
EPS_NORM = 1e-06
TAU_STEP = 0.25

def complex_mul(a_re, a_im, b_re, b_im):

    def matmul(left, right):
        return jnp.einsum('kij,kjl->kil', left, right, precision=HIGH)
    return (matmul(a_re, b_re) - matmul(a_im, b_im), matmul(a_re, b_im) + matmul(a_im, b_re))

def invert(s_re, s_im):
    magnitude = jnp.sqrt(s_re * s_re + s_im * s_im)
    colmax = lax.optimization_barrier(jnp.max(lax.optimization_barrier(jnp.sum(magnitude, axis=1)), axis=1))
    rowmax = lax.optimization_barrier(jnp.max(lax.optimization_barrier(jnp.sum(magnitude, axis=2)), axis=1))
    factor = (1.0 / (colmax * rowmax + EPS_SCALE))[:, None, None]
    x_re = jnp.swapaxes(s_re, 1, 2) * factor
    x_im = -jnp.swapaxes(s_im, 1, 2) * factor
    for turn in range(NEWTON):
        p_re, p_im = complex_mul(s_re, s_im, x_re, x_im)
        q_re, q_im = complex_mul(x_re, x_im, p_re, p_im)
        x_re = 2.0 * x_re - q_re
        x_im = 2.0 * x_im - q_im
    return (x_re, x_im)

def product(form, left, right):
    return jnp.einsum(form, left.astype(jnp.float32), right.astype(jnp.float32), precision=HIGH)

def reference(states_re, states_im, gmap):
    field_re, field_im = (states_re, states_im)
    for step in range(STEPS):
        next_re = jnp.concatenate([field_re[1:], field_re[:1][:, :, gmap]], 0)
        next_im = jnp.concatenate([field_im[1:], field_im[:1][:, :, gmap]], 0)
        s_re = (product('kmg,kng->kmn', field_re, next_re) + product('kmg,kng->kmn', field_im, next_im)) / NPW
        s_im = (product('kmg,kng->kmn', field_re, next_im) - product('kmg,kng->kmn', field_im, next_re)) / NPW
        x_re, x_im = invert(s_re, s_im)
        xb_re = x_re.astype(jnp.bfloat16)
        xb_im = x_im.astype(jnp.bfloat16)
        a_re = product('kmn,kmg->kng', xb_re, next_re) - product('kmn,kmg->kng', xb_im, next_im)
        a_im = product('kmn,kmg->kng', xb_re, next_im) + product('kmn,kmg->kng', xb_im, next_re)
        c_re = (product('kmn,kmg->kng', xb_re, field_re) + product('kmn,kmg->kng', xb_im, field_im)).astype(jnp.bfloat16)
        c_im = (product('kmn,kmg->kng', xb_re, field_im) - product('kmn,kmg->kng', xb_im, field_re)).astype(jnp.bfloat16)
        head_re = jnp.zeros_like(c_re[-1]).at[:, gmap].set(c_re[-1])
        head_im = jnp.zeros_like(c_im[-1]).at[:, gmap].set(c_im[-1])
        d_re = jnp.concatenate([head_re[None], c_re[:-1]], 0).astype(jnp.float32)
        d_im = jnp.concatenate([head_im[None], c_im[:-1]], 0).astype(jnp.float32)
        g_re = a_im - d_im
        g_im = d_re - a_re
        total = jnp.sum(g_re * g_re + g_im * g_im)
        rms = jnp.sqrt(total / (2 * NK * NB * NPW) + EPS_NORM)
        field_re = (field_re.astype(jnp.float32) + TAU_STEP * g_re / rms).astype(jnp.bfloat16)
        field_im = (field_im.astype(jnp.float32) + TAU_STEP * g_im / rms).astype(jnp.bfloat16)
    return (field_re, field_im)
```

```python
import functools

import jax
import jax.numpy as jnp
from jax import lax
from jax.experimental import pallas as pl
from jax.experimental.pallas import tpu as pltpu
from jax.sharding import PartitionSpec as P

NEWTON = 4
STEPS = 2


HIGH = lax.Precision.HIGHEST
EPS_SCALE = 1e-06
EPS_NORM = 1e-06
TAU_STEP = 0.25


def shifted(value, axis, by):
    count = lax.axis_size(axis)
    return lax.ppermute(value, axis, [(i, (i + by) % count) for i in range(count)])


def padded_2(block, sides, width):
    for axis, dim in sides:
        count = lax.axis_size(axis)
        forward = [(i, i + 1) for i in range(count - 1)]
        forward.append((count - 1, 0))
        backward = [(target, source) for source, target in forward]
        low = lax.ppermute(
            lax.slice_in_dim(block, block.shape[dim] - width, None, axis=dim), axis, forward
        )
        high = lax.ppermute(lax.slice_in_dim(block, 0, width, axis=dim), axis, backward)
        block = jnp.concatenate([low, block, high], axis=dim)
    return block


def complex_mul(left, right):

    def matmul(first, second):
        return jnp.einsum("kij,kjl->kil", first, second, precision=HIGH)

    real = matmul(left[:, 0], right[:, 0]) - matmul(left[:, 1], right[:, 1])
    imag = matmul(left[:, 0], right[:, 1]) + matmul(left[:, 1], right[:, 0])
    return jnp.stack([real, imag], 1)


def start_inverse(whole):
    magnitude = jnp.sqrt(whole[:, 0] * whole[:, 0] + whole[:, 1] * whole[:, 1])
    colmax = jnp.max(jnp.sum(magnitude, axis=1), axis=1)
    rowmax = jnp.max(jnp.sum(magnitude, axis=2), axis=1)
    factor = (1.0 / (colmax * rowmax + EPS_SCALE))[:, None, None]
    return jnp.stack(
        [jnp.swapaxes(whole[:, 0], 1, 2) * factor, -jnp.swapaxes(whole[:, 1], 1, 2) * factor], 1
    )


def newton_full(whole):
    iterate = start_inverse(whole)
    for turn in range(NEWTON):
        iterate = 2.0 * iterate - complex_mul(iterate, complex_mul(whole, iterate))
    return iterate


def bf_product(form, left, right):
    return jnp.einsum(form, left, right, preferred_element_type=jnp.float32)


def dual_terms(rounded, states):
    real = bf_product("kmn,kmg->kng", rounded[:, 0], states[:, 0]) + bf_product(
        "kmn,kmg->kng", rounded[:, 1], states[:, 1]
    )
    imag = bf_product("kmn,kmg->kng", rounded[:, 0], states[:, 1]) - bf_product(
        "kmn,kmg->kng", rounded[:, 1], states[:, 0]
    )
    return jnp.stack([real, imag], 1).astype(jnp.bfloat16)


def rotate_columns(block, amount, width):
    blocks_off = amount // width
    rest = amount % width
    plane_size = lax.axis_size("pw")
    for bit in range((plane_size - 1).bit_length()):
        moved = shifted(block, "pw", -(1 << bit))
        block = jnp.where(jnp.bitwise_and(jnp.right_shift(blocks_off, bit), 1) == 1, moved, block)
    after = shifted(block, "pw", -1)
    joined = jnp.concatenate([block, after], block.ndim - 1)
    return lax.dynamic_slice_in_dim(joined, rest, width, block.ndim - 1)


def general_body(states_re, states_im, gmap):
    kpoints, bands, width = states_re.shape
    string_size = lax.axis_size("kstr")
    plane_size = lax.axis_size("pw")
    string_index = lax.axis_index("kstr")
    total_width = width * plane_size
    offset = jnp.mod(gmap[0] - lax.axis_index("pw") * width, total_width)
    back_offset = jnp.mod(total_width - offset, total_width)
    at_first = string_index == 0
    at_last = string_index == string_size - 1
    count_all = 2 * kpoints * string_size * bands * width * plane_size
    states = jnp.stack([states_re, states_im], 1)
    for step in range(STEPS):
        padded = padded_2(states, (("kstr", 0),), 1)
        ahead = padded[-1:]
        behind = padded[:1]
        turned = rotate_columns(ahead, offset, width)
        ahead = jnp.where(at_last, turned, ahead)
        following = jnp.concatenate([states[1:], ahead], 0)
        s_re = bf_product("kmg,kng->kmn", states[:, 0], following[:, 0]) + bf_product(
            "kmg,kng->kmn", states[:, 1], following[:, 1]
        )
        s_im = bf_product("kmg,kng->kmn", states[:, 0], following[:, 1]) - bf_product(
            "kmg,kng->kmn", states[:, 1], following[:, 0]
        )
        partial_value = jnp.stack([s_re, s_im], 1)
        whole = lax.psum(partial_value, "pw") / (width * plane_size)
        inverse = newton_full(whole)
        rounded = inverse.astype(jnp.bfloat16)
        a_re = bf_product("kmn,kmg->kng", rounded[:, 0], following[:, 0]) - bf_product(
            "kmn,kmg->kng", rounded[:, 1], following[:, 1]
        )
        a_im = bf_product("kmn,kmg->kng", rounded[:, 0], following[:, 1]) + bf_product(
            "kmn,kmg->kng", rounded[:, 1], following[:, 0]
        )
        earlier = dual_terms(rounded[:-1], states[:-1])
        previous_inverse = shifted(rounded, "kstr", 1)
        arrived = dual_terms(previous_inverse, behind)
        placed = rotate_columns(arrived, back_offset, width)
        arrived = jnp.where(at_first, placed, arrived)
        incoming = jnp.concatenate([arrived, earlier], 0).astype(jnp.float32)
        g_re = a_im - incoming[:, 1]
        g_im = incoming[:, 0] - a_re
        total = lax.psum(jnp.sum(g_re * g_re + g_im * g_im), ("kstr", "pw"))
        rms = jnp.sqrt(total / count_all + EPS_NORM)
        new_re = (states[:, 0].astype(jnp.float32) + TAU_STEP * g_re / rms).astype(jnp.bfloat16)
        new_im = (states[:, 1].astype(jnp.float32) + TAU_STEP * g_im / rms).astype(jnp.bfloat16)
        states = jnp.stack([new_re, new_im], 1)
    return (states[:, 0], states[:, 1])


def halves(value):
    high = value.astype(jnp.bfloat16)
    return high, (value - high.astype(jnp.float32)).astype(jnp.bfloat16)


def left_factor(real, imag):
    real_high, real_low = halves(real)
    imag_high, imag_low = halves(imag)
    high = jnp.concatenate([real_high, imag_high], 1)
    return jnp.concatenate([high, high, real_low, imag_low], 1)


def right_factor(real, imag):
    real_high, real_low = halves(real)
    imag_high, imag_low = halves(imag)
    high = [
        jnp.concatenate([real_high, imag_high], 1),
        jnp.concatenate([-imag_high, real_high], 1),
    ]
    low = [
        jnp.concatenate([real_low, imag_low], 1),
        jnp.concatenate([-imag_low, real_low], 1),
    ]
    return jnp.concatenate(high + low + high, 0)


def remote_copy(source, place, send, recv, target):
    return pltpu.make_async_remote_copy(
        src_ref=source,
        dst_ref=place,
        send_sem=send,
        recv_sem=recv,
        device_id=target,
        device_id_type=pl.DeviceIdType.MESH,
    )


def greet_all(greeted, awaited):
    barrier = pltpu.get_barrier_semaphore()
    for peer in greeted:
        pl.semaphore_signal(barrier, inc=1, device_id=peer, device_id_type=pl.DeviceIdType.MESH)
    pl.semaphore_wait(barrier, awaited)


def margin_of(own, ahead):
    left = jnp.concatenate([own[0], own[1]], 1)
    form = (((1,), (1,)), ((), ()))
    real = lax.dot_general(
        left, jnp.concatenate([ahead[0], ahead[1]], 1), form, preferred_element_type=jnp.float32
    )
    imag = lax.dot_general(
        left, jnp.concatenate([ahead[1], -ahead[0]], 1), form, preferred_element_type=jnp.float32
    )
    return real, imag


def whole_step(strings, planes, shift, where, states_re, states_im):
    bands, width = states_re.shape
    piece = width // strings
    total_width = width * planes
    count_all = 2 * strings * bands * total_width
    share, middle, pairs = bands // planes, bands // 2, planes // 2
    chunks = bands // 128
    last_extra = strings + 2 * STEPS
    bf16, f32 = jnp.bfloat16, jnp.float32

    def kernel(where_ref, re_in, im_in, re_ref, im_ref, *scratch):
        chain, joined, chosen, aligned, passing, grad, outgoing = scratch[:7]
        scratch = scratch[1:]
        part, got_pair, half, got_string, summed, got_planes = scratch[6:12]
        block, whole, left, iterate, rounded, inverse = scratch[12:18]
        tile, first, stage, second = scratch[18:22]
        send_base, recv_base, send_join, recv_join, inside = scratch[22:27]
        send_halo, recv_halo, recv_pass, send_pass = scratch[27:31]
        send0, recv0, send1, recv1, send2, recv2, send3, recv3 = scratch[31:39]
        send4, recv4, send5, recv5, send6, recv6, send7, recv7 = scratch[39:47]
        send8, recv8, send9, recv9, kept = scratch[47:]
        k, p = lax.axis_index("kstr"), lax.axis_index("pw")
        inputs = (re_in, im_in)
        forward = (k < STEPS).astype(jnp.int32)
        string_peers = [(lax.rem(k + step, strings), p) for step in range(1, strings)]
        plane_peers = [(k, lax.rem(p + step, planes)) for step in range(1, planes)]
        far_peers = [(k, lax.rem(p + 2 * step, planes)) for step in range(1, pairs)]
        side = lax.rem(p, 2)
        sibling = (k, p + 1 - 2 * side)

        def rows(index, size):
            return pl.ds(pl.multiple_of(index * size, size), size)

        offsets = {(step, 0) for step in range(1, strings)}
        offsets |= {(0, step) for step in range(1, planes)}
        for step in range(strings):
            offsets |= {(step, shift), (step, (planes - shift) % planes)}
        offsets = sorted(offsets - {(0, 0)})
        greet_all(
            [(lax.rem(k + a, strings), lax.rem(p + b, planes)) for a, b in offsets], len(offsets)
        )

        down = lax.rem(p + planes - shift, planes)
        target_plane = forward * down + (1 - forward) * lax.rem(p + shift, planes)
        taker = (k, lax.rem(p + planes + 1 - 2 * forward, planes))
        own_half = rows(1 - forward, width)
        other_half = rows(forward, width)
        mine = rows(k, piece)
        base, joins, insides = [], [], []
        for index, ref in enumerate(inputs):
            joins.append(
                remote_copy(
                    ref, joined.at[index, :, other_half], send_join.at[index],
                    recv_join.at[index], taker,
                )
            )
            insides.append(
                pltpu.make_async_copy(ref, joined.at[index, :, own_half], inside.at[0, index])
            )
            insides.append(
                pltpu.make_async_copy(
                    ref.at[:, mine], chain.at[STEPS + k, index], inside.at[1, index]
                )
            )
            for slot, peer in enumerate(string_peers):
                base.append(
                    remote_copy(
                        ref.at[:, rows(peer[0], piece)], chain.at[STEPS + k, index],
                        send_base.at[slot, index], recv_base.at[slot, index], peer,
                    )
                )
        for copy in base + joins + insides:
            copy.start()
        joined[:, :, 2 * width :] = jnp.zeros((2, bands, piece), bf16)
        row_of = lax.broadcasted_iota(jnp.int32, (2 * piece, piece), 0)
        column_of = lax.broadcasted_iota(jnp.int32, (2 * piece, piece), 1)
        apart = (row_of - column_of).astype(f32) - where_ref[1]
        picked = jnp.maximum(1.0 - jnp.abs(apart), 0.0).astype(bf16)
        weights = [
            jnp.full((64, piece), jnp.maximum(1.0 - jnp.abs(where_ref[0] - h), 0.0), f32)
            for h in range(strings + 1)
        ]
        weights = [weight.astype(bf16) for weight in weights]
        for copy in insides + joins:
            copy.wait()

        def choose(number, carry):
            index = lax.rem(number, 2)
            row = rows(lax.rem(number // 2, bands // 64), 64)
            cut = number // (bands // 32)
            total = joined[index, row, rows(cut, piece)] * weights[0]
            for h in range(1, strings + 1):
                total = total + joined[index, row, rows(cut + h, piece)] * weights[h]
            chosen[index, row, rows(cut, piece)] = total
            return carry

        lax.fori_loop(0, (strings + 1) * (bands // 32), choose, 0)

        def align(cut, carry):
            wide = chosen[:, :, pl.ds(pl.multiple_of(cut * piece, piece), 2 * piece)]
            moved = jnp.dot(
                wide.reshape(2 * bands, 2 * piece), picked, preferred_element_type=f32
            )
            aligned[:, :, rows(cut, piece)] = moved.astype(bf16).reshape(2, bands, piece)
            return carry

        lax.fori_loop(0, strings, align, 0)

        def extra_of(source):
            if isinstance(source, int):
                ahead = int(source < STEPS)
            else:
                ahead = (source < STEPS).astype(jnp.int32)
            return source + ahead * (STEPS + strings) - (1 - ahead) * (strings - STEPS)

        front = STEPS + strings

        def halo_copy(step, index):
            target = lax.rem(k + step, strings)
            return remote_copy(
                aligned.at[index, :, rows(target, piece)], chain.at[extra_of(k), index],
                send_halo.at[step, index], recv_halo.at[k, index], (target, target_plane),
            )

        def pass_first(step, index):
            return remote_copy(
                aligned.at[index, :, rows(step, piece)], passing.at[index],
                send_halo.at[step, index], recv_pass.at[index], (step, p),
            )

        def pass_second(index):
            return remote_copy(
                passing.at[index], chain.at[front, index], send_pass.at[index],
                recv_halo.at[0, index], (k, down),
            )

        def halo_arrival(source, index):
            place = chain.at[extra_of(source), index]
            return remote_copy(
                place, place, send_pass.at[index], recv_halo.at[source, index], sibling
            )

        def own_halo(index):
            return pltpu.make_async_copy(
                aligned.at[index, :, mine], chain.at[extra_of(k), index], recv_halo.at[k, index]
            )

        steps = range(1 if shift == 0 else 0, strings)
        if shift == 0:
            for index in range(2):
                own_halo(index).start()
                for step in steps:
                    halo_copy(step, index).start()
        else:

            @pl.when(k == 0)
            def _():
                for index in range(2):
                    for step in range(1, strings):
                        pass_first(step, index).start()
                    halo_copy(0, index).start()

            @pl.when(k > 0)
            def _():
                for index in range(2):
                    for step in steps:
                        halo_copy(step, index).start()

        for copy in base:
            copy.wait()

        def front_arrives():
            for index in range(2):
                if shift != 0:

                    @pl.when(k > 0)
                    def _():
                        pass_first(0, index).wait_recv()
                        pass_second(index).start()

            for index in range(2):
                halo_arrival(0, index).wait_recv()

        cuts = [pl.ds(chunk * 128, 128) for chunk in range(chunks)]

        def pair_copy(which):
            return remote_copy(
                part.at[which, :, rows(1 - side, middle), :], got_pair.at[which],
                send0.at[which], recv0.at[which], sibling,
            )

        def string_copy(which, slot, chunk):
            cut = cuts[chunk]
            return remote_copy(
                half.at[which, :, :, cut], got_string.at[slot, :, :, cut],
                send1.at[slot, chunk], recv1.at[slot, chunk], (which, p),
            )

        def carry_on(which):
            pair_copy(which).wait()
            both = part[which, :, rows(side, middle), :].astype(f32)
            half[which] = (both + got_pair[which].astype(f32)).astype(bf16)

            @pl.when(which != k)
            def _():
                slot = lax.rem(which - k - 1 + strings, strings)
                for chunk in range(chunks):
                    string_copy(which, slot, chunk).start()

        def find_inverses(turn):
            def margin(which, carry):
                if_front = jnp.logical_and(which == strings - 1, turn == 0)
                pl.when(if_front)(front_arrives)
                real, imag = margin_of(chain[STEPS + which], chain[STEPS + 1 + which])
                part[which, 0] = (real * (1.0 / total_width)).astype(bf16)
                part[which, 1] = (imag * (1.0 / total_width)).astype(bf16)
                pair_copy(which).start()

                @pl.when(which > 0)
                def _():
                    carry_on(which - 1)

                return carry

            lax.fori_loop(0, strings, margin, 0)
            carry_on(strings - 1)

            over_planes = []
            for chunk, cut in enumerate(cuts):
                for slot, peer in enumerate(string_peers):
                    string_copy(peer[0], slot, chunk).wait()
                total = half[k, :, :, cut].astype(f32)
                for slot in range(strings - 1):
                    total = total + got_string[slot, :, :, cut].astype(f32)
                summed[:, :, cut] = total.astype(bf16)
                for slot, peer in enumerate(far_peers):
                    copy = remote_copy(
                        summed.at[:, rows(peer[1] // 2, share), cut],
                        got_planes.at[slot, :, :, cut],
                        send2.at[slot, chunk], recv2.at[slot, chunk], peer,
                    )
                    copy.start()
                    over_planes.append((chunk, copy))
            back, passed = [], []
            place = rows(side * pairs + p // 2, share)
            for chunk, cut in enumerate(cuts):
                for number, copy in over_planes:
                    if number == chunk:
                        copy.wait()
                total = summed[:, rows(p // 2, share), cut].astype(f32)
                for slot in range(pairs - 1):
                    total = total + got_planes[slot, :, :, cut].astype(f32)
                block[:, :, cut] = total.astype(bf16)
                for slot, peer in enumerate(far_peers):
                    copy = remote_copy(
                        block.at[:, :, cut], whole.at[:, place, cut],
                        send3.at[slot, chunk], recv3.at[slot, chunk], peer,
                    )
                    copy.start()
                    back.append((slot, chunk, copy))
                copy = remote_copy(
                    block.at[:, :, cut], whole.at[:, place, cut],
                    send9.at[pairs - 1, chunk], recv9.at[pairs - 1, chunk], sibling,
                )
                copy.start()
                passed.append(copy)
                whole[:, place, cut] = block[:, :, cut]
            for slot, chunk, copy in back:
                copy.wait()
                source = lax.rem(p + planes - 2 * (slot + 1), planes) // 2
                there = whole.at[:, rows(side * pairs + source, share), cuts[chunk]]
                relay = remote_copy(
                    there, there, send9.at[slot, chunk], recv9.at[slot, chunk], sibling
                )
                relay.start()
                passed.append(relay)
            for copy in passed:
                copy.wait()

            real, imag = whole[0].astype(f32), whole[1].astype(f32)
            magnitude = jnp.sqrt(real * real + imag * imag)
            colmax = jnp.max(jnp.sum(magnitude, axis=0, keepdims=True), axis=1, keepdims=True)
            rowmax = jnp.max(jnp.sum(magnitude, axis=1, keepdims=True), axis=0, keepdims=True)
            factor = 1.0 / (colmax * rowmax + EPS_SCALE)
            iterate[0] = real.T * factor
            iterate[1] = -imag.T * factor
            left[...] = left_factor(real, imag)

            def newton(_, carry):
                x_re, x_im = iterate[0], iterate[1]
                product = jnp.dot(
                    left[...], right_factor(x_re, x_im), preferred_element_type=f32
                )
                product = jnp.dot(
                    left_factor(x_re, x_im),
                    right_factor(product[:, :bands], product[:, bands:]),
                    preferred_element_type=f32,
                )
                iterate[0] = 2.0 * x_re - product[:, :bands]
                iterate[1] = 2.0 * x_im - product[:, bands:]
                return carry

            lax.fori_loop(0, NEWTON, newton, 0)
            real, imag = iterate[0].T.astype(bf16), iterate[1].T.astype(bf16)
            rounded[0] = real
            rounded[1] = imag
            mine_rows = rows(side, middle)
            first_hops = []
            for slot, peer in enumerate(string_peers):
                copy = remote_copy(
                    rounded.at[:, mine_rows, :], inverse.at[k, :, mine_rows, :],
                    send4.at[slot], recv4.at[slot], peer,
                )
                copy.start()
                first_hops.append(copy)
            inverse[k, 0] = real
            inverse[k, 1] = imag
            second_hops = []
            for slot, copy in enumerate(first_hops):
                copy.wait()
                source = lax.rem(k + strings - slot - 1, strings)
                relay = remote_copy(
                    inverse.at[source, :, mine_rows, :], inverse.at[source, :, mine_rows, :],
                    send5.at[slot], recv5.at[slot], sibling,
                )
                relay.start()
                second_hops.append(relay)
            for relay in second_hops:
                relay.wait()

        def element(place):
            link = lax.rem(place + 2 * strings - STEPS, strings)
            before = lax.rem(place + 2 * strings - STEPS - 1, strings)

            def product(left_side, right_side):
                return jnp.dot(left_side, right_side, preferred_element_type=f32)

            x_re, x_im = inverse[link, 0], inverse[link, 1]
            next_re, next_im = chain[place + 1, 0], chain[place + 1, 1]
            a_re = product(x_re, next_re) - product(x_im, next_im)
            a_im = product(x_re, next_im) + product(x_im, next_re)
            x_re, x_im = inverse[before, 0], inverse[before, 1]
            last_re, last_im = chain[place - 1, 0], chain[place - 1, 1]
            c_re = (product(x_re, last_re) + product(x_im, last_im)).astype(bf16)
            c_im = (product(x_re, last_im) - product(x_im, last_re)).astype(bf16)
            g_re = a_im - c_im.astype(f32)
            g_im = c_re.astype(f32) - a_re
            grad[place - 1, 0] = g_re
            grad[place - 1, 1] = g_im
            return g_re, g_im

        def inner(place, total):
            g_re, g_im = element(place)
            square = g_re * g_re + g_im * g_im
            lanes = square[:, :128]
            for group in range(1, piece // 128):
                lanes = lanes + square[:, group * 128 : (group + 1) * 128]
            return total + jnp.sum(lanes.reshape(bands // 8, 8, 128), 0)

        def outer(index, carry):
            element(STEPS - 1 + index * (strings + 1))
            return carry

        def find_scale(turn):
            @pl.when(turn == 0)
            def _():
                for index in range(2):
                    halo_arrival(strings - 1, index).wait_recv()

            tile[...] = lax.fori_loop(STEPS, STEPS + strings, inner, jnp.zeros((8, 128), f32))
            copies = [
                remote_copy(tile, first.at[k], send6.at[slot], recv6.at[slot], peer)
                for slot, peer in enumerate(string_peers)
            ]
            for copy in copies:
                copy.start()
            first[k] = tile[...]

            for copy in copies:
                copy.wait()
            stage[...] = jnp.sum(first[...], 0)
            copies = [
                remote_copy(stage, second.at[p], send7.at[slot], recv7.at[slot], peer)
                for slot, peer in enumerate(plane_peers)
            ]
            for copy in copies:
                copy.start()
            second[p] = stage[...]

            @pl.when(turn == 0)
            def _():
                for source in range(1, strings - 1):
                    for index in range(2):
                        halo_arrival(source, index).wait_recv()
                lax.fori_loop(0, 2, outer, 0)

            for copy in copies:
                copy.wait()
            total = jnp.sum(second[...], 0)
            total = jnp.sum(jnp.sum(total, axis=0, keepdims=True), axis=1, keepdims=True)
            return TAU_STEP / jnp.sqrt(total / count_all + EPS_NORM)

        def renewed(place, index, scale):
            old = chain[place, index].astype(f32)
            return (old + grad[place - 1, index] * scale).astype(bf16)

        def renew(scale):
            def one(place, carry):
                chain[place, 0] = renewed(place, 0, scale)
                chain[place, 1] = renewed(place, 1, scale)
                return carry

            lax.fori_loop(STEPS - 1, STEPS + strings + 1, one, 0)

        def finish(scale):
            copies = []
            for slot, peer in enumerate(string_peers):
                for index, ref in enumerate((re_ref, im_ref)):
                    outgoing[slot, index] = renewed(STEPS + peer[0], index, scale)
                    copy = remote_copy(
                        outgoing.at[slot, index], ref.at[:, mine],
                        send8.at[slot, index], recv8.at[slot, index], peer,
                    )
                    copy.start()
                    copies.append(copy)
            for index, ref in enumerate((re_ref, im_ref)):
                outgoing[strings - 1, index] = renewed(STEPS + k, index, scale)
                copy = pltpu.make_async_copy(
                    outgoing.at[strings - 1, index], ref.at[:, mine], kept.at[index]
                )
                copy.start()
                copies.append(copy)
            for copy in copies:
                copy.wait()

        def sent():
            for index in range(2):
                if shift == 0:
                    for step in steps:
                        halo_copy(step, index).wait_send()
                else:

                    @pl.when(k == 0)
                    def _():
                        for step in range(1, strings):
                            pass_first(step, index).wait_send()
                        halo_copy(0, index).wait_send()

                    @pl.when(k > 0)
                    def _():
                        for step in steps:
                            halo_copy(step, index).wait_send()
                        pass_second(index).wait_send()

        def one_step(turn, carry):
            find_inverses(turn)
            scale = find_scale(turn)

            @pl.when(turn < STEPS - 1)
            def _():
                renew(scale)

            @pl.when(turn == STEPS - 1)
            def _():
                finish(scale)

            return carry

        lax.fori_loop(0, STEPS, one_step, 0)
        sent()

    vmem = pl.BlockSpec(memory_space=pltpu.VMEM)
    anywhere = pl.BlockSpec(memory_space=pl.ANY)
    square = (2, bands, bands)
    dma = pltpu.SemaphoreType.DMA
    out = jax.ShapeDtypeStruct((bands, width), bf16)
    return pl.pallas_call(
        kernel,
        out_shape=(out, out),
        in_specs=[pl.BlockSpec(memory_space=pltpu.SMEM), anywhere, anywhere],
        out_specs=(vmem, vmem),
        scratch_shapes=[
            pltpu.VMEM((last_extra, 2, bands, piece), bf16),
            pltpu.VMEM((2, bands, 2 * width + piece), bf16),
            pltpu.VMEM((2, bands, width + piece), bf16),
            pltpu.VMEM((2, bands, width), bf16),
            pltpu.VMEM((2, bands, piece), bf16),
            pltpu.VMEM((strings + 2, 2, bands, piece), f32),
            pltpu.VMEM((strings, 2, bands, piece), bf16),
            pltpu.VMEM((strings,) + square, bf16),
            pltpu.VMEM((strings, 2, middle, bands), bf16),
            pltpu.VMEM((strings, 2, middle, bands), bf16),
            pltpu.VMEM((strings - 1, 2, middle, bands), bf16),
            pltpu.VMEM((2, middle, bands), bf16),
            pltpu.VMEM((pairs - 1, 2, share, bands), bf16),
            pltpu.VMEM((2, share, bands), bf16),
            pltpu.VMEM(square, bf16),
            pltpu.VMEM((bands, 6 * bands), bf16),
            pltpu.VMEM(square, f32),
            pltpu.VMEM(square, bf16),
            pltpu.VMEM((strings,) + square, bf16),
            pltpu.VMEM((8, 128), f32),
            pltpu.VMEM((strings, 8, 128), f32),
            pltpu.VMEM((8, 128), f32),
            pltpu.VMEM((planes, 8, 128), f32),
        ]
        + [dma((strings - 1, 2))] * 2
        + [dma((2,))] * 2
        + [dma((2, 2))]
        + [dma((strings, 2))] * 2
        + [dma((2,))] * 2
        + [dma((strings,))] * 2
        + [dma((strings - 1, chunks))] * 2
        + [dma((pairs - 1, chunks))] * 4
        + [dma((strings - 1,))] * 4
        + [dma((strings - 1,))] * 2
        + [dma((planes - 1,))] * 2
        + [dma((strings - 1, 2))] * 2
        + [dma((pairs, chunks))] * 2
        + [dma((2,))],
        compiler_params=pltpu.CompilerParams(collective_id=20 + shift, has_side_effects=True),
        name=f"steps_{shift}",
    )(where, states_re, states_im)


def spread_body(strings, planes, states_re, states_im, gmap):
    width = states_re.shape[2]
    total_width = width * planes
    offset = jnp.mod(gmap[0] - lax.axis_index("pw") * width, total_width)
    blocks_off, rest = offset // width, jnp.mod(offset, width)
    start = jnp.where(lax.axis_index("kstr") < STEPS, rest, width - rest)
    piece = width // strings
    where = jnp.stack([start // piece, jnp.mod(start, piece)]).astype(jnp.float32)
    new_re, new_im = lax.switch(
        blocks_off,
        [functools.partial(whole_step, strings, planes, shift) for shift in range(planes)],
        where, states_re[0], states_im[0],
    )
    return (new_re[None], new_im[None])


def solution(mesh):
    placed = (P("kstr", None, "pw"), P("kstr", None, "pw"), P("pw"))
    strings, planes = mesh.shape["kstr"], mesh.shape["pw"]

    def body(states_re, states_im, gmap):
        kpoints, bands, width = states_re.shape
        fits = (
            kpoints == 1
            and strings > 1
            and planes > 1
            and width % (strings * 128) == 0
            and bands % (planes * 16) == 0
            and bands % 128 == 0
            and planes % 2 == 0
            and planes > 2
            and strings == 2 * STEPS
        )
        if not fits:
            return general_body(states_re, states_im, gmap)
        return spread_body(strings, planes, states_re, states_im, gmap)

    return jax.shard_map(
        body,
        mesh=mesh,
        in_specs=placed,
        out_specs=(P("kstr", None, "pw"), P("kstr", None, "pw")),
        check_vma=False,
    )
```

```python
import functools

import jax
import jax.numpy as jnp
from jax import lax
from jax.experimental import pallas as pl
from jax.experimental.pallas import tpu as pltpu
from jax.sharding import PartitionSpec as P

NEWTON = 4
STEPS = 2


HIGH = lax.Precision.HIGHEST
EPS_SCALE = 1e-06
EPS_NORM = 1e-06
TAU_STEP = 0.25


def shifted(value, axis, by):
    count = lax.axis_size(axis)
    return lax.ppermute(value, axis, [(i, (i + by) % count) for i in range(count)])


def padded_2(block, sides, width):
    for axis, dim in sides:
        count = lax.axis_size(axis)
        forward = [(i, i + 1) for i in range(count - 1)]
        forward.append((count - 1, 0))
        backward = [(target, source) for source, target in forward]
        low = lax.ppermute(
            lax.slice_in_dim(block, block.shape[dim] - width, None, axis=dim), axis, forward
        )
        high = lax.ppermute(lax.slice_in_dim(block, 0, width, axis=dim), axis, backward)
        block = jnp.concatenate([low, block, high], axis=dim)
    return block


def complex_mul(left, right):

    def matmul(first, second):
        return jnp.einsum("kij,kjl->kil", first, second, precision=HIGH)

    real = matmul(left[:, 0], right[:, 0]) - matmul(left[:, 1], right[:, 1])
    imag = matmul(left[:, 0], right[:, 1]) + matmul(left[:, 1], right[:, 0])
    return jnp.stack([real, imag], 1)


def start_inverse(whole):
    magnitude = jnp.sqrt(whole[:, 0] * whole[:, 0] + whole[:, 1] * whole[:, 1])
    colmax = jnp.max(jnp.sum(magnitude, axis=1), axis=1)
    rowmax = jnp.max(jnp.sum(magnitude, axis=2), axis=1)
    factor = (1.0 / (colmax * rowmax + EPS_SCALE))[:, None, None]
    return jnp.stack(
        [jnp.swapaxes(whole[:, 0], 1, 2) * factor, -jnp.swapaxes(whole[:, 1], 1, 2) * factor], 1
    )


def newton_full(whole):
    iterate = start_inverse(whole)
    for turn in range(NEWTON):
        iterate = 2.0 * iterate - complex_mul(iterate, complex_mul(whole, iterate))
    return iterate


def bf_product(form, left, right):
    return jnp.einsum(form, left, right, preferred_element_type=jnp.float32)


def dual_terms(rounded, states):
    real = bf_product("kmn,kmg->kng", rounded[:, 0], states[:, 0]) + bf_product(
        "kmn,kmg->kng", rounded[:, 1], states[:, 1]
    )
    imag = bf_product("kmn,kmg->kng", rounded[:, 0], states[:, 1]) - bf_product(
        "kmn,kmg->kng", rounded[:, 1], states[:, 0]
    )
    return jnp.stack([real, imag], 1).astype(jnp.bfloat16)


def rotate_columns(block, amount, width):
    blocks_off = amount // width
    rest = amount % width
    plane_size = lax.axis_size("pw")
    for bit in range((plane_size - 1).bit_length()):
        moved = shifted(block, "pw", -(1 << bit))
        block = jnp.where(jnp.bitwise_and(jnp.right_shift(blocks_off, bit), 1) == 1, moved, block)
    after = shifted(block, "pw", -1)
    joined = jnp.concatenate([block, after], block.ndim - 1)
    return lax.dynamic_slice_in_dim(joined, rest, width, block.ndim - 1)


def general_body(states_re, states_im, gmap):
    kpoints, bands, width = states_re.shape
    string_size = lax.axis_size("kstr")
    plane_size = lax.axis_size("pw")
    string_index = lax.axis_index("kstr")
    total_width = width * plane_size
    offset = jnp.mod(gmap[0] - lax.axis_index("pw") * width, total_width)
    back_offset = jnp.mod(total_width - offset, total_width)
    at_first = string_index == 0
    at_last = string_index == string_size - 1
    count_all = 2 * kpoints * string_size * bands * width * plane_size
    states = jnp.stack([states_re, states_im], 1)
    for step in range(STEPS):
        padded = padded_2(states, (("kstr", 0),), 1)
        ahead = padded[-1:]
        behind = padded[:1]
        turned = rotate_columns(ahead, offset, width)
        ahead = jnp.where(at_last, turned, ahead)
        following = jnp.concatenate([states[1:], ahead], 0)
        s_re = bf_product("kmg,kng->kmn", states[:, 0], following[:, 0]) + bf_product(
            "kmg,kng->kmn", states[:, 1], following[:, 1]
        )
        s_im = bf_product("kmg,kng->kmn", states[:, 0], following[:, 1]) - bf_product(
            "kmg,kng->kmn", states[:, 1], following[:, 0]
        )
        partial_value = jnp.stack([s_re, s_im], 1)
        whole = lax.psum(partial_value, "pw") / (width * plane_size)
        inverse = newton_full(whole)
        rounded = inverse.astype(jnp.bfloat16)
        a_re = bf_product("kmn,kmg->kng", rounded[:, 0], following[:, 0]) - bf_product(
            "kmn,kmg->kng", rounded[:, 1], following[:, 1]
        )
        a_im = bf_product("kmn,kmg->kng", rounded[:, 0], following[:, 1]) + bf_product(
            "kmn,kmg->kng", rounded[:, 1], following[:, 0]
        )
        earlier = dual_terms(rounded[:-1], states[:-1])
        previous_inverse = shifted(rounded, "kstr", 1)
        arrived = dual_terms(previous_inverse, behind)
        placed = rotate_columns(arrived, back_offset, width)
        arrived = jnp.where(at_first, placed, arrived)
        incoming = jnp.concatenate([arrived, earlier], 0).astype(jnp.float32)
        g_re = a_im - incoming[:, 1]
        g_im = incoming[:, 0] - a_re
        total = lax.psum(jnp.sum(g_re * g_re + g_im * g_im), ("kstr", "pw"))
        rms = jnp.sqrt(total / count_all + EPS_NORM)
        new_re = (states[:, 0].astype(jnp.float32) + TAU_STEP * g_re / rms).astype(jnp.bfloat16)
        new_im = (states[:, 1].astype(jnp.float32) + TAU_STEP * g_im / rms).astype(jnp.bfloat16)
        states = jnp.stack([new_re, new_im], 1)
    return (states[:, 0], states[:, 1])


def halves(value):
    high = value.astype(jnp.bfloat16)
    return high, (value - high.astype(jnp.float32)).astype(jnp.bfloat16)


def left_factor(real, imag):
    real_high, real_low = halves(real)
    imag_high, imag_low = halves(imag)
    high = jnp.concatenate([real_high, imag_high], 1)
    return jnp.concatenate([high, high, real_low, imag_low], 1)


def right_factor(real, imag):
    real_high, real_low = halves(real)
    imag_high, imag_low = halves(imag)
    high = [
        jnp.concatenate([real_high, imag_high], 1),
        jnp.concatenate([-imag_high, real_high], 1),
    ]
    low = [
        jnp.concatenate([real_low, imag_low], 1),
        jnp.concatenate([-imag_low, real_low], 1),
    ]
    return jnp.concatenate(high + low + high, 0)


def remote_copy(source, place, send, recv, target):
    return pltpu.make_async_remote_copy(
        src_ref=source,
        dst_ref=place,
        send_sem=send,
        recv_sem=recv,
        device_id=target,
        device_id_type=pl.DeviceIdType.MESH,
    )


def greet_all(greeted, awaited):
    barrier = pltpu.get_barrier_semaphore()
    for peer in greeted:
        pl.semaphore_signal(barrier, inc=1, device_id=peer, device_id_type=pl.DeviceIdType.MESH)
    pl.semaphore_wait(barrier, awaited)


def margin_of(own, ahead):
    left = jnp.concatenate([own[0], own[1]], 1)
    form = (((1,), (1,)), ((), ()))
    real = lax.dot_general(
        left, jnp.concatenate([ahead[0], ahead[1]], 1), form, preferred_element_type=jnp.float32
    )
    imag = lax.dot_general(
        left, jnp.concatenate([ahead[1], -ahead[0]], 1), form, preferred_element_type=jnp.float32
    )
    return real, imag


def whole_step(strings, planes, shift, where, states_re, states_im):
    bands, width = states_re.shape
    piece = width // strings
    total_width = width * planes
    count_all = 2 * strings * bands * total_width
    share, middle, pairs = bands // planes, bands // 2, planes // 2
    chunks = bands // 128
    last_extra = strings + 2 * STEPS
    flipped = shift >= planes // 2
    moves = (shift + 1) % planes if flipped else shift
    ahead_rows = bands // 4
    bf16, f32 = jnp.bfloat16, jnp.float32

    def kernel(where_ref, re_in, im_in, re_ref, im_ref, *scratch):
        chain, joined, chosen, aligned, early, slopes, grad, outgoing, picked = scratch[:9]
        early_out, scratch = scratch[9], scratch[4:]
        part, got_pair, half, got_string, summed, got_planes = scratch[6:12]
        block, whole, left, iterate, rounded, inverse = scratch[12:18]
        tile, first, stage, second = scratch[18:22]
        send_base, recv_base, send_join, recv_join, inside = scratch[22:27]
        send_halo, recv_halo = scratch[27:29]
        scratch = scratch[:29] + scratch[27:]
        send0, recv0, send1, recv1, send2, recv2, send3, recv3 = scratch[31:39]
        send4, recv4, send5, recv5, send6, recv6, send7, recv7 = scratch[39:47]
        send8, recv8, send9, recv9, kept, send10, recv10, kept_rest = scratch[47:55]
        send11, recv11 = scratch[55:]
        k, p = lax.axis_index("kstr"), lax.axis_index("pw")
        inputs = (re_in, im_in)
        forward = (k < STEPS).astype(jnp.int32)
        string_peers = [(lax.rem(k + step, strings), p) for step in range(1, strings)]
        plane_peers = [(k, lax.rem(p + step, planes)) for step in range(1, planes)]
        far_peers = [(k, lax.rem(p + 2 * step, planes)) for step in range(1, pairs)]
        side = lax.rem(p, 2)
        sibling = (k, p + 1 - 2 * side)

        def rows(index, size):
            return pl.ds(pl.multiple_of(index * size, size), size)

        offsets = {(step, 0) for step in range(1, strings)}
        offsets |= {(0, step) for step in range(1, planes)}
        for step in range(strings):
            offsets |= {(step, moves), (step, (planes - moves) % planes)}
        offsets = sorted(offsets - {(0, 0)})
        greet_all(
            [(lax.rem(k + a, strings), lax.rem(p + b, planes)) for a, b in offsets], len(offsets)
        )

        down = lax.rem(p + planes - moves, planes)
        target_plane = forward * down + (1 - forward) * lax.rem(p + moves, planes)
        leading = 1 - forward if flipped else forward
        taker = (k, lax.rem(p + planes + 1 - 2 * leading, planes))
        own_half = rows(1 - leading, width)
        other_half = rows(leading, width)
        mine = rows(k, piece)
        base, joins, insides = [], [], []
        for index, ref in enumerate(inputs):
            joins.append(
                remote_copy(
                    ref, joined.at[index, :, other_half], send_join.at[index],
                    recv_join.at[index], taker,
                )
            )
            insides.append(
                pltpu.make_async_copy(ref, joined.at[index, :, own_half], inside.at[0, index])
            )
            insides.append(
                pltpu.make_async_copy(
                    ref.at[:, mine], chain.at[STEPS + k, index], inside.at[1, index]
                )
            )
            for slot, peer in enumerate(string_peers):
                base.append(
                    remote_copy(
                        ref.at[:, rows(peer[0], piece)], chain.at[STEPS + k, index],
                        send_base.at[slot, index], recv_base.at[slot, index], peer,
                    )
                )
        for copy in base + joins + insides:
            copy.start()
        joined[:, :, 2 * width :] = jnp.zeros((2, bands, piece), bf16)
        row_of = lax.broadcasted_iota(jnp.int32, (64, piece), 0)
        column_of = lax.broadcasted_iota(jnp.int32, (64, piece), 1)
        apart = (row_of - column_of).astype(f32) - where_ref[1]

        def pick(number, carry):
            there = apart + (number * 64).astype(f32)
            picked[rows(number, 64)] = jnp.maximum(1.0 - jnp.abs(there), 0.0).astype(bf16)
            return carry

        lax.fori_loop(0, 2 * piece // 64, pick, 0)
        weights = [
            jnp.full((64, piece), jnp.maximum(1.0 - jnp.abs(where_ref[0] - h), 0.0), f32)
            for h in range(strings + 1)
        ]
        weights = [weight.astype(bf16) for weight in weights]
        for copy in insides + joins:
            copy.wait()

        def choose(number, carry):
            index = lax.rem(number, 2)
            row = rows(lax.rem(number // 2, bands // 64), 64)
            cut = number // (bands // 32)
            total = joined[index, row, rows(cut, piece)] * weights[0]
            for h in range(1, strings + 1):
                total = total + joined[index, row, rows(cut + h, piece)] * weights[h]
            chosen[index, row, rows(cut, piece)] = total
            return carry

        lax.fori_loop(0, (strings + 1) * (bands // 32), choose, 0)

        def extra_of(source):
            if isinstance(source, int):
                ahead = int(source < STEPS)
            else:
                ahead = (source < STEPS).astype(jnp.int32)
            return source + ahead * (STEPS + strings) - (1 - ahead) * (strings - STEPS)

        front = STEPS + strings

        def halo_copy(step, index):
            target = lax.rem(k + step, strings)
            return remote_copy(
                aligned.at[index, :, rows(target, piece)], chain.at[extra_of(k), index],
                send_halo.at[step, index], recv_halo.at[k, index], (target, target_plane),
            )

        def halo_arrival(source, index):
            place = chain.at[extra_of(source), index]
            return remote_copy(
                place, place, send_halo.at[0, index], recv_halo.at[source, index], sibling
            )

        def own_halo(index):
            return pltpu.make_async_copy(
                aligned.at[index, :, mine], chain.at[extra_of(k), index], recv_halo.at[k, index]
            )

        def align(step, carry):
            cut = lax.rem(k + step, strings)

            def align_rows(number, carry):
                index = lax.rem(number, 2)
                row = rows(number // 2, 128)
                wide = chosen[index, row, pl.ds(pl.multiple_of(cut * piece, piece), 2 * piece)]
                moved = jnp.dot(wide, picked[...], preferred_element_type=f32)
                aligned[index, row, rows(cut, piece)] = moved.astype(bf16)
                return carry

            lax.fori_loop(0, bands // 64, align_rows, 0)
            for index in range(2):
                if moves == 0:

                    @pl.when(step == strings)
                    def _():
                        own_halo(index).start()

                    @pl.when(step < strings)
                    def _():
                        halo_copy(step, index).start()

                else:
                    halo_copy(step, index).start()
            return carry

        if moves == 0:
            lax.fori_loop(1, strings + 1, align, 0)
        else:
            lax.fori_loop(0, strings, align, 0)

        for copy in base:
            copy.wait()

        def front_arrives():
            for index in range(2):
                halo_arrival(0, index).wait_recv()

        cuts = [pl.ds(chunk * 128, 128) for chunk in range(chunks)]

        def pair_copy(which):
            return remote_copy(
                part.at[which, :, rows(1 - side, middle), :], got_pair.at[which],
                send0.at[which], recv0.at[which], sibling,
            )

        def string_copy(which, slot, chunk):
            cut = cuts[chunk]
            return remote_copy(
                half.at[which, :, :, cut], got_string.at[slot, :, :, cut],
                send1.at[slot, chunk], recv1.at[slot, chunk], (which, p),
            )

        def carry_on(which):
            pair_copy(which).wait()
            both = part[which, :, rows(side, middle), :].astype(f32)
            half[which] = (both + got_pair[which].astype(f32)).astype(bf16)

            @pl.when(which != k)
            def _():
                slot = lax.rem(which - k - 1 + strings, strings)
                for chunk in range(chunks):
                    string_copy(which, slot, chunk).start()

        def find_inverses(turn):
            def margin(which, carry):
                if_front = jnp.logical_and(which == strings - 1, turn == 0)
                pl.when(if_front)(front_arrives)
                real, imag = margin_of(chain[STEPS + which], chain[STEPS + 1 + which])
                part[which, 0] = (real * (1.0 / total_width)).astype(bf16)
                part[which, 1] = (imag * (1.0 / total_width)).astype(bf16)
                pair_copy(which).start()

                @pl.when(which > 0)
                def _():
                    carry_on(which - 1)

                return carry

            lax.fori_loop(0, strings, margin, 0)
            carry_on(strings - 1)


            over_planes = []
            for chunk, cut in enumerate(cuts):
                for slot, peer in enumerate(string_peers):
                    string_copy(peer[0], slot, chunk).wait()
                total = half[k, :, :, cut].astype(f32)
                for slot in range(strings - 1):
                    total = total + got_string[slot, :, :, cut].astype(f32)
                summed[:, :, cut] = total.astype(bf16)
                for slot, peer in enumerate(far_peers):
                    copy = remote_copy(
                        summed.at[:, rows(peer[1] // 2, share), cut],
                        got_planes.at[slot, :, :, cut],
                        send2.at[slot, chunk], recv2.at[slot, chunk], peer,
                    )
                    copy.start()
                    over_planes.append((chunk, copy))

            @pl.when(turn == STEPS - 1)
            def _():
                for slot in range(strings - 1):
                    home_copy(slot).start()
                home_own.start()

            back, passed = [], []
            place = rows(side * pairs + p // 2, share)
            for chunk, cut in enumerate(cuts):
                for number, copy in over_planes:
                    if number == chunk:
                        copy.wait()
                total = summed[:, rows(p // 2, share), cut].astype(f32)
                for slot in range(pairs - 1):
                    total = total + got_planes[slot, :, :, cut].astype(f32)
                block[:, :, cut] = total.astype(bf16)
                for slot, peer in enumerate(far_peers):
                    copy = remote_copy(
                        block.at[:, :, cut], whole.at[:, place, cut],
                        send3.at[slot, chunk], recv3.at[slot, chunk], peer,
                    )
                    copy.start()
                    back.append((slot, chunk, copy))
                copy = remote_copy(
                    block.at[:, :, cut], whole.at[:, place, cut],
                    send9.at[pairs - 1, chunk], recv9.at[pairs - 1, chunk], sibling,
                )
                copy.start()
                passed.append(copy)
                whole[:, place, cut] = block[:, :, cut]
            for slot, chunk, copy in back:
                copy.wait()
                source = lax.rem(p + planes - 2 * (slot + 1), planes) // 2
                there = whole.at[:, rows(side * pairs + source, share), cuts[chunk]]
                relay = remote_copy(
                    there, there, send9.at[slot, chunk], recv9.at[slot, chunk], sibling
                )
                relay.start()
                passed.append(relay)
            for copy in passed:
                copy.wait()

            real, imag = whole[0].astype(f32), whole[1].astype(f32)
            magnitude = jnp.sqrt(real * real + imag * imag)
            colmax = jnp.max(jnp.sum(magnitude, axis=0, keepdims=True), axis=1, keepdims=True)
            rowmax = jnp.max(jnp.sum(magnitude, axis=1, keepdims=True), axis=0, keepdims=True)
            factor = 1.0 / (colmax * rowmax + EPS_SCALE)
            iterate[0] = real.T * factor
            iterate[1] = -imag.T * factor
            left[...] = left_factor(real, imag)

            def newton(_, carry):
                x_re, x_im = iterate[0], iterate[1]
                product = jnp.dot(
                    left[...], right_factor(x_re, x_im), preferred_element_type=f32
                )
                product = jnp.dot(
                    left_factor(x_re, x_im),
                    right_factor(product[:, :bands], product[:, bands:]),
                    preferred_element_type=f32,
                )
                iterate[0] = 2.0 * x_re - product[:, :bands]
                iterate[1] = 2.0 * x_im - product[:, bands:]
                return carry

            lax.fori_loop(0, NEWTON, newton, 0)
            real, imag = iterate[0].T.astype(bf16), iterate[1].T.astype(bf16)
            rounded[0] = real
            rounded[1] = imag
            mine_rows = rows(side, middle)
            first_hops = []
            for slot, peer in enumerate(string_peers):
                copy = remote_copy(
                    rounded.at[:, mine_rows, :], inverse.at[k, :, mine_rows, :],
                    send4.at[slot], recv4.at[slot], peer,
                )
                copy.start()
                first_hops.append(copy)
            inverse[k, 0] = real
            inverse[k, 1] = imag
            second_hops = []
            for slot, copy in enumerate(first_hops):
                copy.wait()
                source = lax.rem(k + strings - slot - 1, strings)
                relay = remote_copy(
                    inverse.at[source, :, mine_rows, :], inverse.at[source, :, mine_rows, :],
                    send5.at[slot], recv5.at[slot], sibling,
                )
                relay.start()
                second_hops.append(relay)
            for relay in second_hops:
                relay.wait()

        def element(place):
            link = lax.rem(place + 2 * strings - STEPS, strings)
            before = lax.rem(place + 2 * strings - STEPS - 1, strings)

            def product(left_side, right_side):
                return jnp.dot(left_side, right_side, preferred_element_type=f32)

            x_re, x_im = inverse[link, 0], inverse[link, 1]
            next_re, next_im = chain[place + 1, 0], chain[place + 1, 1]
            a_re = product(x_re, next_re) - product(x_im, next_im)
            a_im = product(x_re, next_im) + product(x_im, next_re)
            x_re, x_im = inverse[before, 0], inverse[before, 1]
            last_re, last_im = chain[place - 1, 0], chain[place - 1, 1]
            c_re = (product(x_re, last_re) + product(x_im, last_im)).astype(bf16)
            c_im = (product(x_re, last_im) - product(x_im, last_re)).astype(bf16)
            g_re = a_im - c_im.astype(f32)
            g_im = c_re.astype(f32) - a_re
            return g_re, g_im

        def norm_first(slot):
            peer = string_peers[slot]
            return remote_copy(tile, first.at[k], send6.at[slot], recv6.at[slot], peer)

        def norm_second(slot):
            peer = plane_peers[slot]
            return remote_copy(stage, second.at[p], send7.at[slot], recv7.at[slot], peer)

        def begin_norm():
            for slot in range(strings - 1):
                norm_first(slot).start()
            first[k] = tile[...]

        def carry_norm():
            for slot in range(strings - 1):
                norm_first(slot).wait()
            stage[...] = jnp.sum(first[...], 0)
            for slot in range(planes - 1):
                norm_second(slot).start()
            second[p] = stage[...]

        ahead_of = pl.ds(0, ahead_rows)
        rest_of = pl.ds(ahead_rows, bands - ahead_rows)

        def home_copy(slot):
            target = lax.rem(k + 1 + slot, strings)
            return remote_copy(
                chain.at[STEPS + target, :, ahead_of], early.at[:, :, mine],
                send10.at[slot], recv10.at[slot], (target, p),
            )

        home_own = pltpu.make_async_copy(
            chain.at[STEPS + k, :, ahead_of], early.at[:, :, mine], kept.at[0]
        )

        def slope_copy(slot):
            target = lax.rem(k + 1 + slot, strings)
            return remote_copy(
                early_out.at[slot], slopes.at[:, :, mine],
                send8.at[slot], recv8.at[slot], (target, p),
            )

        slope_own = pltpu.make_async_copy(
            early_out.at[strings - 1], slopes.at[:, :, mine], kept.at[1]
        )

        def rest_copy(slot, index):
            target = lax.rem(k + 1 + slot, strings)
            ref = (re_ref, im_ref)[index]
            return remote_copy(
                outgoing.at[slot, index], ref.at[rest_of, mine],
                send11.at[slot, index], recv11.at[slot, index], (target, p),
            )

        def rest_own(index):
            ref = (re_ref, im_ref)[index]
            return pltpu.make_async_copy(
                outgoing.at[strings - 1, index], ref.at[rest_of, mine], kept_rest.at[index]
            )

        def find_scale(turn):
            @pl.when(turn == 0)
            def _():
                for index in range(2):
                    halo_arrival(strings - 1, index).wait_recv()

            tile[...] = jnp.zeros((8, 128), f32)

            def gradient(number, carry):
                @pl.when(number == strings)
                def _():
                    begin_norm()
                    for source in range(1, strings - 1):
                        for index in range(2):
                            halo_arrival(source, index).wait_recv()

                @pl.when(number == strings + 1)
                def _():
                    carry_norm()

                inside_string = (number < strings).astype(jnp.int32)
                place = inside_string * (STEPS + lax.rem(k + 1 + number, strings))
                place += (1 - inside_string) * (
                    STEPS - 1 + (number - strings) * (strings + 1)
                )
                g_re, g_im = element(place)
                grad[place - 1, 0] = g_re
                grad[place - 1, 1] = g_im

                @pl.when(number < strings)
                def _():
                    square = g_re * g_re + g_im * g_im
                    lanes = square[:, :128]
                    for group in range(1, piece // 128):
                        lanes = lanes + square[:, group * 128 : (group + 1) * 128]
                    tile[...] += jnp.sum(lanes.reshape(bands // 8, 8, 128), 0)

                @pl.when(turn == STEPS - 1)
                def _():
                    early_out[number, 0] = g_re[:ahead_rows].astype(bf16)
                    early_out[number, 1] = g_im[:ahead_rows].astype(bf16)

                    @pl.when(number < strings - 1)
                    def _():
                        slope_copy(number).start()

                return carry

            count = strings + 2 * (turn < STEPS - 1).astype(jnp.int32)
            lax.fori_loop(0, count, gradient, 0)

            @pl.when(turn == STEPS - 1)
            def _():
                slope_own.start()
                begin_norm()
                carry_norm()

            for slot in range(planes - 1):
                norm_second(slot).wait()
            total = jnp.sum(second[...], 0)
            total = jnp.sum(jnp.sum(total, axis=0, keepdims=True), axis=1, keepdims=True)
            return TAU_STEP / jnp.sqrt(total / count_all + EPS_NORM)

        def renewed(place, index, scale):
            old = chain[place, index].astype(f32)
            return (old + grad[place - 1, index] * scale).astype(bf16)

        def renew(scale):
            def one(place, carry):
                chain[place, 0] = renewed(place, 0, scale)
                chain[place, 1] = renewed(place, 1, scale)
                return carry

            lax.fori_loop(STEPS - 1, STEPS + strings + 1, one, 0)

        def finish(scale):
            def one(slot, carry):
                place = STEPS + lax.rem(k + 1 + slot, strings)
                for index in range(2):
                    old = chain[place, index, rest_of].astype(f32)
                    fresh = old + grad[place - 1, index, rest_of] * scale
                    outgoing[slot, index] = fresh.astype(bf16)

                    @pl.when(slot < strings - 1)
                    def _():
                        rest_copy(slot, index).start()

                    @pl.when(slot == strings - 1)
                    def _():
                        rest_own(index).start()

                return carry

            lax.fori_loop(0, strings, one, 0)
            for slot in range(strings - 1):
                home_copy(slot).wait()
                slope_copy(slot).wait()
            home_own.wait()
            slope_own.wait()
            for index, ref in enumerate((re_ref, im_ref)):
                fresh = early[index].astype(f32) + slopes[index].astype(f32) * scale
                ref[ahead_of, :] = fresh.astype(bf16)
            for index in range(2):
                for slot in range(strings - 1):
                    rest_copy(slot, index).wait()
                rest_own(index).wait()

        def sent():
            for step in range(1 if moves == 0 else 0, strings):
                for index in range(2):
                    halo_copy(step, index).wait_send()

        def one_step(turn, carry):
            find_inverses(turn)
            scale = find_scale(turn)

            @pl.when(turn < STEPS - 1)
            def _():
                renew(scale)

            @pl.when(turn == STEPS - 1)
            def _():
                finish(scale)

            return carry

        lax.fori_loop(0, STEPS, one_step, 0)
        sent()

    vmem = pl.BlockSpec(memory_space=pltpu.VMEM)
    anywhere = pl.BlockSpec(memory_space=pl.ANY)
    square = (2, bands, bands)
    dma = pltpu.SemaphoreType.DMA
    out = jax.ShapeDtypeStruct((bands, width), bf16)
    return pl.pallas_call(
        kernel,
        out_shape=(out, out),
        in_specs=[pl.BlockSpec(memory_space=pltpu.SMEM), anywhere, anywhere],
        out_specs=(vmem, vmem),
        scratch_shapes=[
            pltpu.VMEM((last_extra, 2, bands, piece), bf16),
            pltpu.VMEM((2, bands, 2 * width + piece), bf16),
            pltpu.VMEM((2, bands, width + piece), bf16),
            pltpu.VMEM((2, bands, width), bf16),
            pltpu.VMEM((2, ahead_rows, width), bf16),
            pltpu.VMEM((2, ahead_rows, width), bf16),
            pltpu.VMEM((strings + 2, 2, bands, piece), f32),
            pltpu.VMEM((strings, 2, bands - ahead_rows, piece), bf16),
            pltpu.VMEM((2 * piece, piece), bf16),
            pltpu.VMEM((strings, 2, ahead_rows, piece), bf16),
            pltpu.VMEM((strings,) + square, bf16),
            pltpu.VMEM((strings, 2, middle, bands), bf16),
            pltpu.VMEM((strings, 2, middle, bands), bf16),
            pltpu.VMEM((strings - 1, 2, middle, bands), bf16),
            pltpu.VMEM((2, middle, bands), bf16),
            pltpu.VMEM((pairs - 1, 2, share, bands), bf16),
            pltpu.VMEM((2, share, bands), bf16),
            pltpu.VMEM(square, bf16),
            pltpu.VMEM((bands, 6 * bands), bf16),
            pltpu.VMEM(square, f32),
            pltpu.VMEM(square, bf16),
            pltpu.VMEM((strings,) + square, bf16),
            pltpu.VMEM((8, 128), f32),
            pltpu.VMEM((strings, 8, 128), f32),
            pltpu.VMEM((8, 128), f32),
            pltpu.VMEM((planes, 8, 128), f32),
        ]
        + [dma((strings - 1, 2))] * 2
        + [dma((2,))] * 2
        + [dma((2, 2))]
        + [dma((strings, 2))] * 2
        + [dma((strings,))] * 2
        + [dma((strings - 1, chunks))] * 2
        + [dma((pairs - 1, chunks))] * 4
        + [dma((strings - 1,))] * 4
        + [dma((strings - 1,))] * 2
        + [dma((planes - 1,))] * 2
        + [dma((strings - 1,))] * 2
        + [dma((pairs, chunks))] * 2
        + [dma((2,))]
        + [dma((strings - 1,))] * 2
        + [dma((2,))]
        + [dma((strings - 1, 2))] * 2,
        compiler_params=pltpu.CompilerParams(collective_id=20 + shift, has_side_effects=True),
        name=f"steps_{shift}",
    )(where, states_re, states_im)


def spread_body(strings, planes, states_re, states_im, gmap):
    width = states_re.shape[2]
    total_width = width * planes
    offset = jnp.mod(gmap[0] - lax.axis_index("pw") * width, total_width)
    blocks_off, rest = offset // width, jnp.mod(offset, width)
    start = jnp.where(lax.axis_index("kstr") < STEPS, rest, width - rest)
    piece = width // strings
    where = jnp.stack([start // piece, jnp.mod(start, piece)]).astype(jnp.float32)
    new_re, new_im = lax.switch(
        blocks_off,
        [functools.partial(whole_step, strings, planes, shift) for shift in range(planes)],
        where, states_re[0], states_im[0],
    )
    return (new_re[None], new_im[None])


def solution(mesh):
    placed = (P("kstr", None, "pw"), P("kstr", None, "pw"), P("pw"))
    strings, planes = mesh.shape["kstr"], mesh.shape["pw"]

    def body(states_re, states_im, gmap):
        kpoints, bands, width = states_re.shape
        fits = (
            kpoints == 1
            and strings > 1
            and planes > 1
            and width % (strings * 128) == 0
            and bands % (planes * 16) == 0
            and bands % 128 == 0
            and planes % 2 == 0
            and planes > 2
            and strings == 2 * STEPS
        )
        if not fits:
            return general_body(states_re, states_im, gmap)
        return spread_body(strings, planes, states_re, states_im, gmap)

    return jax.shard_map(
        body,
        mesh=mesh,
        in_specs=placed,
        out_specs=(P("kstr", None, "pw"), P("kstr", None, "pw")),
        check_vma=False,
    )
```

```python
import functools

import jax
import jax.numpy as jnp
from jax import lax
from jax.experimental import pallas as pl
from jax.experimental.pallas import tpu as pltpu
from jax.sharding import PartitionSpec as P

NEWTON = 4
STEPS = 2


HIGH = lax.Precision.HIGHEST
EPS_SCALE = 1e-06
EPS_NORM = 1e-06
TAU_STEP = 0.25


def shifted(value, axis, by):
    count = lax.axis_size(axis)
    return lax.ppermute(value, axis, [(i, (i + by) % count) for i in range(count)])


def padded_2(block, sides, width):
    for axis, dim in sides:
        count = lax.axis_size(axis)
        forward = [(i, i + 1) for i in range(count - 1)]
        forward.append((count - 1, 0))
        backward = [(target, source) for source, target in forward]
        low = lax.ppermute(
            lax.slice_in_dim(block, block.shape[dim] - width, None, axis=dim), axis, forward
        )
        high = lax.ppermute(lax.slice_in_dim(block, 0, width, axis=dim), axis, backward)
        block = jnp.concatenate([low, block, high], axis=dim)
    return block


def complex_mul(left, right):

    def matmul(first, second):
        return jnp.einsum("kij,kjl->kil", first, second, precision=HIGH)

    real = matmul(left[:, 0], right[:, 0]) - matmul(left[:, 1], right[:, 1])
    imag = matmul(left[:, 0], right[:, 1]) + matmul(left[:, 1], right[:, 0])
    return jnp.stack([real, imag], 1)


def start_inverse(whole):
    magnitude = jnp.sqrt(whole[:, 0] * whole[:, 0] + whole[:, 1] * whole[:, 1])
    colmax = jnp.max(jnp.sum(magnitude, axis=1), axis=1)
    rowmax = jnp.max(jnp.sum(magnitude, axis=2), axis=1)
    factor = (1.0 / (colmax * rowmax + EPS_SCALE))[:, None, None]
    return jnp.stack(
        [jnp.swapaxes(whole[:, 0], 1, 2) * factor, -jnp.swapaxes(whole[:, 1], 1, 2) * factor], 1
    )


def newton_full(whole):
    iterate = start_inverse(whole)
    for turn in range(NEWTON):
        iterate = 2.0 * iterate - complex_mul(iterate, complex_mul(whole, iterate))
    return iterate


def bf_product(form, left, right):
    return jnp.einsum(form, left, right, preferred_element_type=jnp.float32)


def dual_terms(rounded, states):
    real = bf_product("kmn,kmg->kng", rounded[:, 0], states[:, 0]) + bf_product(
        "kmn,kmg->kng", rounded[:, 1], states[:, 1]
    )
    imag = bf_product("kmn,kmg->kng", rounded[:, 0], states[:, 1]) - bf_product(
        "kmn,kmg->kng", rounded[:, 1], states[:, 0]
    )
    return jnp.stack([real, imag], 1).astype(jnp.bfloat16)


def rotate_columns(block, amount, width):
    blocks_off = amount // width
    rest = amount % width
    plane_size = lax.axis_size("pw")
    for bit in range((plane_size - 1).bit_length()):
        moved = shifted(block, "pw", -(1 << bit))
        block = jnp.where(jnp.bitwise_and(jnp.right_shift(blocks_off, bit), 1) == 1, moved, block)
    after = shifted(block, "pw", -1)
    joined = jnp.concatenate([block, after], block.ndim - 1)
    return lax.dynamic_slice_in_dim(joined, rest, width, block.ndim - 1)


def general_body(states_re, states_im, gmap):
    kpoints, bands, width = states_re.shape
    string_size = lax.axis_size("kstr")
    plane_size = lax.axis_size("pw")
    string_index = lax.axis_index("kstr")
    total_width = width * plane_size
    offset = jnp.mod(gmap[0] - lax.axis_index("pw") * width, total_width)
    back_offset = jnp.mod(total_width - offset, total_width)
    at_first = string_index == 0
    at_last = string_index == string_size - 1
    count_all = 2 * kpoints * string_size * bands * width * plane_size
    states = jnp.stack([states_re, states_im], 1)
    for step in range(STEPS):
        padded = padded_2(states, (("kstr", 0),), 1)
        ahead = padded[-1:]
        behind = padded[:1]
        turned = rotate_columns(ahead, offset, width)
        ahead = jnp.where(at_last, turned, ahead)
        following = jnp.concatenate([states[1:], ahead], 0)
        s_re = bf_product("kmg,kng->kmn", states[:, 0], following[:, 0]) + bf_product(
            "kmg,kng->kmn", states[:, 1], following[:, 1]
        )
        s_im = bf_product("kmg,kng->kmn", states[:, 0], following[:, 1]) - bf_product(
            "kmg,kng->kmn", states[:, 1], following[:, 0]
        )
        partial_value = jnp.stack([s_re, s_im], 1)
        whole = lax.psum(partial_value, "pw") / (width * plane_size)
        inverse = newton_full(whole)
        rounded = inverse.astype(jnp.bfloat16)
        a_re = bf_product("kmn,kmg->kng", rounded[:, 0], following[:, 0]) - bf_product(
            "kmn,kmg->kng", rounded[:, 1], following[:, 1]
        )
        a_im = bf_product("kmn,kmg->kng", rounded[:, 0], following[:, 1]) + bf_product(
            "kmn,kmg->kng", rounded[:, 1], following[:, 0]
        )
        earlier = dual_terms(rounded[:-1], states[:-1])
        previous_inverse = shifted(rounded, "kstr", 1)
        arrived = dual_terms(previous_inverse, behind)
        placed = rotate_columns(arrived, back_offset, width)
        arrived = jnp.where(at_first, placed, arrived)
        incoming = jnp.concatenate([arrived, earlier], 0).astype(jnp.float32)
        g_re = a_im - incoming[:, 1]
        g_im = incoming[:, 0] - a_re
        total = lax.psum(jnp.sum(g_re * g_re + g_im * g_im), ("kstr", "pw"))
        rms = jnp.sqrt(total / count_all + EPS_NORM)
        new_re = (states[:, 0].astype(jnp.float32) + TAU_STEP * g_re / rms).astype(jnp.bfloat16)
        new_im = (states[:, 1].astype(jnp.float32) + TAU_STEP * g_im / rms).astype(jnp.bfloat16)
        states = jnp.stack([new_re, new_im], 1)
    return (states[:, 0], states[:, 1])


def halves(value):
    high = value.astype(jnp.bfloat16)
    return high, (value - high.astype(jnp.float32)).astype(jnp.bfloat16)


def left_factor(real, imag):
    real_high, real_low = halves(real)
    imag_high, imag_low = halves(imag)
    high = jnp.concatenate([real_high, imag_high], 1)
    return jnp.concatenate([high, high, real_low, imag_low], 1)


def right_factor(real, imag):
    real_high, real_low = halves(real)
    imag_high, imag_low = halves(imag)
    high = [
        jnp.concatenate([real_high, imag_high], 1),
        jnp.concatenate([-imag_high, real_high], 1),
    ]
    low = [
        jnp.concatenate([real_low, imag_low], 1),
        jnp.concatenate([-imag_low, real_low], 1),
    ]
    return jnp.concatenate(high + low + high, 0)


def remote_copy(source, place, send, recv, target):
    return pltpu.make_async_remote_copy(
        src_ref=source,
        dst_ref=place,
        send_sem=send,
        recv_sem=recv,
        device_id=target,
        device_id_type=pl.DeviceIdType.MESH,
    )


def greet_all(greeted, awaited):
    barrier = pltpu.get_barrier_semaphore()
    for peer in greeted:
        pl.semaphore_signal(barrier, inc=1, device_id=peer, device_id_type=pl.DeviceIdType.MESH)
    pl.semaphore_wait(barrier, awaited)


def margin_of(own, ahead):
    left = jnp.concatenate([own[0], own[1]], 1)
    form = (((1,), (1,)), ((), ()))
    real = lax.dot_general(
        left, jnp.concatenate([ahead[0], ahead[1]], 1), form, preferred_element_type=jnp.float32
    )
    imag = lax.dot_general(
        left, jnp.concatenate([ahead[1], -ahead[0]], 1), form, preferred_element_type=jnp.float32
    )
    return real, imag


def whole_step(strings, planes, shift, where, states_re, states_im):
    bands, width = states_re.shape
    piece = width // strings
    total_width = width * planes
    count_all = 2 * strings * bands * total_width
    share, middle, pairs = bands // planes, bands // 2, planes // 2
    chunks = bands // 128
    last_extra = strings + 2 * STEPS
    flipped = shift >= planes // 2
    moves = (shift + 1) % planes if flipped else shift
    ahead_rows = bands // 4
    blocks = bands // 64
    bf16, f32 = jnp.bfloat16, jnp.float32

    def kernel(where_ref, re_in, im_in, re_ref, im_ref, *scratch):
        chain, joined, chosen, aligned, early, slopes, grad, outgoing, picked = scratch[:9]
        early_out, scratch = scratch[9], scratch[4:]
        part, got_pair, half, got_string, summed, got_planes = scratch[6:12]
        block, whole, left, iterate, rounded, inverse = scratch[12:18]
        tile, first, stage, second = scratch[18:22]
        send_base, recv_base, send_join, recv_join, inside = scratch[22:27]
        send_halo, recv_halo = scratch[27:29]
        scratch = scratch[:29] + scratch[27:]
        send0, recv0, send1, recv1, send2, recv2, send3, recv3 = scratch[31:39]
        send4, recv4, send5, recv5, send6, recv6, send7, recv7 = scratch[39:47]
        send8, recv8, send9, recv9, kept, send10, recv10, kept_rest = scratch[47:55]
        send11, recv11 = scratch[55:]
        k, p = lax.axis_index("kstr"), lax.axis_index("pw")
        inputs = (re_in, im_in)
        forward = (k < STEPS).astype(jnp.int32)
        string_peers = [(lax.rem(k + step, strings), p) for step in range(1, strings)]
        plane_peers = [(k, lax.rem(p + step, planes)) for step in range(1, planes)]
        far_peers = [(k, lax.rem(p + 2 * step, planes)) for step in range(1, pairs)]
        side = lax.rem(p, 2)
        sibling = (k, p + 1 - 2 * side)

        def rows(index, size):
            return pl.ds(pl.multiple_of(index * size, size), size)

        offsets = {(step, 0) for step in range(1, strings)}
        offsets |= {(0, step) for step in range(1, planes)}
        for step in range(strings):
            offsets |= {(step, moves), (step, (planes - moves) % planes)}
        offsets = sorted(offsets - {(0, 0)})
        greet_all(
            [(lax.rem(k + a, strings), lax.rem(p + b, planes)) for a, b in offsets], len(offsets)
        )

        down = lax.rem(p + planes - moves, planes)
        target_plane = forward * down + (1 - forward) * lax.rem(p + moves, planes)
        leading = 1 - forward if flipped else forward
        taker = (k, lax.rem(p + planes + 1 - 2 * leading, planes))
        own_half = rows(1 - leading, width)
        other_half = rows(leading, width)
        mine = rows(k, piece)
        def join(number, index):
            row = rows(number, 64)
            return remote_copy(
                inputs[index].at[row, :], joined.at[index, row, other_half],
                send_join.at[number, index], recv_join.at[number, index], taker,
            )

        def join_own(number, index):
            row = rows(number, 64)
            return pltpu.make_async_copy(
                inputs[index].at[row, :], joined.at[index, row, own_half],
                inside.at[number, index],
            )

        base, insides = [], []
        for index, ref in enumerate(inputs):
            insides.append(
                pltpu.make_async_copy(
                    ref.at[:, mine], chain.at[STEPS + k, index], inside.at[blocks, index]
                )
            )
            for slot, peer in enumerate(string_peers):
                base.append(
                    remote_copy(
                        ref.at[:, rows(peer[0], piece)], chain.at[STEPS + k, index],
                        send_base.at[slot, index], recv_base.at[slot, index], peer,
                    )
                )
        for number in range(blocks):
            for index in range(2):
                join(number, index).start()
                join_own(number, index).start()
        for copy in base + insides:
            copy.start()
        joined[:, :, 2 * width :] = jnp.zeros((2, bands, piece), bf16)
        row_of = lax.broadcasted_iota(jnp.int32, (64, piece), 0)
        column_of = lax.broadcasted_iota(jnp.int32, (64, piece), 1)
        apart = (row_of - column_of).astype(f32) - where_ref[1]

        def pick(number, carry):
            there = apart + (number * 64).astype(f32)
            picked[rows(number, 64)] = jnp.maximum(1.0 - jnp.abs(there), 0.0).astype(bf16)
            return carry

        lax.fori_loop(0, 2 * piece // 64, pick, 0)
        weights = [
            jnp.full((64, piece), jnp.maximum(1.0 - jnp.abs(where_ref[0] - h), 0.0), f32)
            for h in range(strings + 1)
        ]
        weights = [weight.astype(bf16) for weight in weights]
        def extra_of(source):
            if isinstance(source, int):
                ahead = int(source < STEPS)
            else:
                ahead = (source < STEPS).astype(jnp.int32)
            return source + ahead * (STEPS + strings) - (1 - ahead) * (strings - STEPS)

        front = STEPS + strings

        def halo_copy(step, index):
            target = lax.rem(k + step, strings)
            return remote_copy(
                aligned.at[index, :, rows(target, piece)], chain.at[extra_of(k), index],
                send_halo.at[step, index], recv_halo.at[k, index], (target, target_plane),
            )

        def halo_arrival(source, index):
            place = chain.at[extra_of(source), index]
            return remote_copy(
                place, place, send_halo.at[0, index], recv_halo.at[source, index], sibling
            )

        def halo_part(step, index, number):
            target = lax.rem(k + step, strings)
            row = rows(number, 64)
            return remote_copy(
                aligned.at[index, row, rows(target, piece)], chain.at[extra_of(k), index, row],
                send_halo.at[step, index], recv_halo.at[k, index], (target, target_plane),
            )

        def own_part(index, number):
            row = rows(number, 64)
            return pltpu.make_async_copy(
                aligned.at[index, row, mine], chain.at[extra_of(k), index, row],
                recv_halo.at[k, index],
            )

        def send_block(number, carry):
            for index in range(2):
                join_own(number, index).wait()
                join(number, index).wait()
            row = rows(number, 64)

            def choose(place, carry):
                index, cut = lax.rem(place, 2), place // 2
                total = joined[index, row, rows(cut, piece)] * weights[0]
                for h in range(1, strings + 1):
                    total = total + joined[index, row, rows(cut + h, piece)] * weights[h]
                chosen[index, row, rows(cut, piece)] = total
                return carry

            lax.fori_loop(0, 2 * (strings + 1), choose, 0)

            def align(step, carry):
                cut = lax.rem(k + step, strings)
                wide = chosen[:, row, pl.ds(pl.multiple_of(cut * piece, piece), 2 * piece)]
                moved = jnp.dot(
                    wide.reshape(128, 2 * piece), picked[...], preferred_element_type=f32
                )
                moved = moved.astype(bf16).reshape(2, 64, piece)
                aligned[:, row, rows(cut, piece)] = moved
                for index in range(2):
                    if moves == 0:

                        @pl.when(step == strings)
                        def _():
                            own_part(index, number).start()

                        @pl.when(step < strings)
                        def _():
                            halo_part(step, index, number).start()

                    else:
                        halo_part(step, index, number).start()
                return carry

            if moves == 0:
                lax.fori_loop(1, strings + 1, align, 0)
            else:
                lax.fori_loop(0, strings, align, 0)
            return carry

        lax.fori_loop(0, blocks, send_block, 0)

        for copy in insides:
            copy.wait()
        for copy in base:
            copy.wait()

        def front_arrives():
            for index in range(2):
                halo_arrival(0, index).wait_recv()

        cuts = [pl.ds(chunk * 128, 128) for chunk in range(chunks)]

        def pair_copy(which):
            return remote_copy(
                part.at[which, :, rows(1 - side, middle), :], got_pair.at[which],
                send0.at[which], recv0.at[which], sibling,
            )

        def string_copy(which, slot, chunk):
            cut = cuts[chunk]
            return remote_copy(
                half.at[which, :, :, cut], got_string.at[slot, :, :, cut],
                send1.at[slot, chunk], recv1.at[slot, chunk], (which, p),
            )

        def carry_on(which):
            pair_copy(which).wait()
            both = part[which, :, rows(side, middle), :].astype(f32)
            half[which] = (both + got_pair[which].astype(f32)).astype(bf16)

            @pl.when(which != k)
            def _():
                slot = lax.rem(which - k - 1 + strings, strings)
                for chunk in range(chunks):
                    string_copy(which, slot, chunk).start()

        def find_inverses(turn):
            def margin(number, carry):
                later = (turn > 0).astype(jnp.int32)
                which = later * lax.rem(k + 1 + number, strings) + (1 - later) * number
                if_front = jnp.logical_and(which == strings - 1, turn == 0)
                pl.when(if_front)(front_arrives)
                real, imag = margin_of(chain[STEPS + which], chain[STEPS + 1 + which])
                part[which, 0] = (real * (1.0 / total_width)).astype(bf16)
                part[which, 1] = (imag * (1.0 / total_width)).astype(bf16)
                pair_copy(which).start()

                @pl.when(number > 0)
                def _():
                    carry_on(lax.rem(which + strings - 1, strings))

                return carry

            lax.fori_loop(0, strings, margin, 0)
            later = (turn > 0).astype(jnp.int32)
            carry_on(later * k + (1 - later) * (strings - 1))


            over_planes = []
            for chunk, cut in enumerate(cuts):
                for slot, peer in enumerate(string_peers):
                    string_copy(peer[0], slot, chunk).wait()
                total = half[k, :, :, cut].astype(f32)
                for slot in range(strings - 1):
                    total = total + got_string[slot, :, :, cut].astype(f32)
                summed[:, :, cut] = total.astype(bf16)
                for slot, peer in enumerate(far_peers):
                    copy = remote_copy(
                        summed.at[:, rows(peer[1] // 2, share), cut],
                        got_planes.at[slot, :, :, cut],
                        send2.at[slot, chunk], recv2.at[slot, chunk], peer,
                    )
                    copy.start()
                    over_planes.append((chunk, copy))

            @pl.when(turn == STEPS - 1)
            def _():
                for slot in range(strings - 1):
                    home_copy(slot).start()
                home_own.start()

            back, passed = [], []
            place = rows(side * pairs + p // 2, share)
            for chunk, cut in enumerate(cuts):
                for number, copy in over_planes:
                    if number == chunk:
                        copy.wait()
                total = summed[:, rows(p // 2, share), cut].astype(f32)
                for slot in range(pairs - 1):
                    total = total + got_planes[slot, :, :, cut].astype(f32)
                block[:, :, cut] = total.astype(bf16)
                for slot, peer in enumerate(far_peers):
                    copy = remote_copy(
                        block.at[:, :, cut], whole.at[:, place, cut],
                        send3.at[slot, chunk], recv3.at[slot, chunk], peer,
                    )
                    copy.start()
                    back.append((slot, chunk, copy))
                copy = remote_copy(
                    block.at[:, :, cut], whole.at[:, place, cut],
                    send9.at[pairs - 1, chunk], recv9.at[pairs - 1, chunk], sibling,
                )
                copy.start()
                passed.append(copy)
                whole[:, place, cut] = block[:, :, cut]
            for slot, chunk, copy in back:
                copy.wait()
                source = lax.rem(p + planes - 2 * (slot + 1), planes) // 2
                there = whole.at[:, rows(side * pairs + source, share), cuts[chunk]]
                relay = remote_copy(
                    there, there, send9.at[slot, chunk], recv9.at[slot, chunk], sibling
                )
                relay.start()
                passed.append(relay)
            for copy in passed:
                copy.wait()

            real, imag = whole[0].astype(f32), whole[1].astype(f32)
            magnitude = jnp.sqrt(real * real + imag * imag)
            colmax = jnp.max(jnp.sum(magnitude, axis=0, keepdims=True), axis=1, keepdims=True)
            rowmax = jnp.max(jnp.sum(magnitude, axis=1, keepdims=True), axis=0, keepdims=True)
            factor = 1.0 / (colmax * rowmax + EPS_SCALE)
            iterate[0] = real.T * factor
            iterate[1] = -imag.T * factor
            left[...] = left_factor(real, imag)

            def newton(_, carry):
                x_re, x_im = iterate[0], iterate[1]
                product = jnp.dot(
                    left[...], right_factor(x_re, x_im), preferred_element_type=f32
                )
                product = jnp.dot(
                    left_factor(x_re, x_im),
                    right_factor(product[:, :bands], product[:, bands:]),
                    preferred_element_type=f32,
                )
                iterate[0] = 2.0 * x_re - product[:, :bands]
                iterate[1] = 2.0 * x_im - product[:, bands:]
                return carry

            lax.fori_loop(0, NEWTON, newton, 0)
            real, imag = iterate[0].T.astype(bf16), iterate[1].T.astype(bf16)
            rounded[0] = real
            rounded[1] = imag
            mine_rows = rows(side, middle)
            first_hops = []
            for slot, peer in enumerate(string_peers):
                copy = remote_copy(
                    rounded.at[:, mine_rows, :], inverse.at[k, :, mine_rows, :],
                    send4.at[slot], recv4.at[slot], peer,
                )
                copy.start()
                first_hops.append(copy)
            inverse[k, 0] = real
            inverse[k, 1] = imag
            second_hops = []
            for slot, copy in enumerate(first_hops):
                copy.wait()
                source = lax.rem(k + strings - slot - 1, strings)
                relay = remote_copy(
                    inverse.at[source, :, mine_rows, :], inverse.at[source, :, mine_rows, :],
                    send5.at[slot], recv5.at[slot], sibling,
                )
                relay.start()
                second_hops.append(relay)
            for relay in second_hops:
                relay.wait()

        def element(place):
            link = lax.rem(place + 2 * strings - STEPS, strings)
            before = lax.rem(place + 2 * strings - STEPS - 1, strings)

            def product(left_side, right_side):
                return jnp.dot(left_side, right_side, preferred_element_type=f32)

            x_re, x_im = inverse[link, 0], inverse[link, 1]
            next_re, next_im = chain[place + 1, 0], chain[place + 1, 1]
            a_re = product(x_re, next_re) - product(x_im, next_im)
            a_im = product(x_re, next_im) + product(x_im, next_re)
            x_re, x_im = inverse[before, 0], inverse[before, 1]
            last_re, last_im = chain[place - 1, 0], chain[place - 1, 1]
            c_re = (product(x_re, last_re) + product(x_im, last_im)).astype(bf16)
            c_im = (product(x_re, last_im) - product(x_im, last_re)).astype(bf16)
            g_re = a_im - c_im.astype(f32)
            g_im = c_re.astype(f32) - a_re
            return g_re, g_im

        def norm_first(slot):
            peer = string_peers[slot]
            return remote_copy(tile, first.at[k], send6.at[slot], recv6.at[slot], peer)

        def norm_second(slot):
            peer = plane_peers[slot]
            return remote_copy(stage, second.at[p], send7.at[slot], recv7.at[slot], peer)

        def begin_norm():
            for slot in range(strings - 1):
                norm_first(slot).start()
            first[k] = tile[...]

        def carry_norm():
            for slot in range(strings - 1):
                norm_first(slot).wait()
            stage[...] = jnp.sum(first[...], 0)
            for slot in range(planes - 1):
                norm_second(slot).start()
            second[p] = stage[...]

        ahead_of = pl.ds(0, ahead_rows)
        rest_of = pl.ds(ahead_rows, bands - ahead_rows)

        def home_copy(slot):
            target = lax.rem(k + 1 + slot, strings)
            return remote_copy(
                chain.at[STEPS + target, :, ahead_of], early.at[:, :, mine],
                send10.at[slot], recv10.at[slot], (target, p),
            )

        home_own = pltpu.make_async_copy(
            chain.at[STEPS + k, :, ahead_of], early.at[:, :, mine], kept.at[0]
        )

        def slope_copy(slot):
            target = lax.rem(k + 1 + slot, strings)
            return remote_copy(
                early_out.at[slot], slopes.at[:, :, mine],
                send8.at[slot], recv8.at[slot], (target, p),
            )

        slope_own = pltpu.make_async_copy(
            early_out.at[strings - 1], slopes.at[:, :, mine], kept.at[1]
        )

        def rest_copy(slot, index):
            target = lax.rem(k + 1 + slot, strings)
            ref = (re_ref, im_ref)[index]
            return remote_copy(
                outgoing.at[slot, index], ref.at[rest_of, mine],
                send11.at[slot, index], recv11.at[slot, index], (target, p),
            )

        def rest_own(index):
            ref = (re_ref, im_ref)[index]
            return pltpu.make_async_copy(
                outgoing.at[strings - 1, index], ref.at[rest_of, mine], kept_rest.at[index]
            )

        def find_scale(turn):
            @pl.when(turn == 0)
            def _():
                for index in range(2):
                    halo_arrival(strings - 1, index).wait_recv()

            tile[...] = jnp.zeros((8, 128), f32)

            def gradient(number, carry):
                @pl.when(number == strings)
                def _():
                    begin_norm()
                    for source in range(1, strings - 1):
                        for index in range(2):
                            halo_arrival(source, index).wait_recv()

                @pl.when(number == strings + 1)
                def _():
                    carry_norm()

                inside_string = (number < strings).astype(jnp.int32)
                place = inside_string * (STEPS + lax.rem(k + 1 + number, strings))
                place += (1 - inside_string) * (
                    STEPS - 1 + (number - strings) * (strings + 1)
                )
                g_re, g_im = element(place)
                grad[place - 1, 0] = g_re
                grad[place - 1, 1] = g_im

                @pl.when(number < strings)
                def _():
                    square = g_re * g_re + g_im * g_im
                    lanes = square[:, :128]
                    for group in range(1, piece // 128):
                        lanes = lanes + square[:, group * 128 : (group + 1) * 128]
                    tile[...] += jnp.sum(lanes.reshape(bands // 8, 8, 128), 0)

                @pl.when(turn == STEPS - 1)
                def _():
                    early_out[number, 0] = g_re[:ahead_rows].astype(bf16)
                    early_out[number, 1] = g_im[:ahead_rows].astype(bf16)

                    @pl.when(number < strings - 1)
                    def _():
                        slope_copy(number).start()

                return carry

            count = strings + 2 * (turn < STEPS - 1).astype(jnp.int32)
            lax.fori_loop(0, count, gradient, 0)

            @pl.when(turn == STEPS - 1)
            def _():
                slope_own.start()
                begin_norm()
                carry_norm()

            for slot in range(planes - 1):
                norm_second(slot).wait()
            total = jnp.sum(second[...], 0)
            total = jnp.sum(jnp.sum(total, axis=0, keepdims=True), axis=1, keepdims=True)
            return TAU_STEP / jnp.sqrt(total / count_all + EPS_NORM)

        def renewed(place, index, scale):
            old = chain[place, index].astype(f32)
            return (old + grad[place - 1, index] * scale).astype(bf16)

        def renew(scale):
            def one(place, carry):
                chain[place, 0] = renewed(place, 0, scale)
                chain[place, 1] = renewed(place, 1, scale)
                return carry

            lax.fori_loop(STEPS - 1, STEPS + strings + 1, one, 0)

        def finish(scale):
            def one(slot, carry):
                place = STEPS + lax.rem(k + 1 + slot, strings)
                for index in range(2):
                    old = chain[place, index, rest_of].astype(f32)
                    fresh = old + grad[place - 1, index, rest_of] * scale
                    outgoing[slot, index] = fresh.astype(bf16)

                    @pl.when(slot < strings - 1)
                    def _():
                        rest_copy(slot, index).start()

                    @pl.when(slot == strings - 1)
                    def _():
                        rest_own(index).start()

                return carry

            lax.fori_loop(0, strings, one, 0)
            for slot in range(strings - 1):
                home_copy(slot).wait()
                slope_copy(slot).wait()
            home_own.wait()
            slope_own.wait()
            for index, ref in enumerate((re_ref, im_ref)):
                fresh = early[index].astype(f32) + slopes[index].astype(f32) * scale
                ref[ahead_of, :] = fresh.astype(bf16)
            for index in range(2):
                for slot in range(strings - 1):
                    rest_copy(slot, index).wait()
                rest_own(index).wait()

        def sent():
            for step in range(1 if moves == 0 else 0, strings):
                for index in range(2):
                    halo_copy(step, index).wait_send()

        def one_step(turn, carry):
            find_inverses(turn)
            scale = find_scale(turn)

            @pl.when(turn < STEPS - 1)
            def _():
                renew(scale)

            @pl.when(turn == STEPS - 1)
            def _():
                finish(scale)

            return carry

        lax.fori_loop(0, STEPS, one_step, 0)
        sent()

    vmem = pl.BlockSpec(memory_space=pltpu.VMEM)
    anywhere = pl.BlockSpec(memory_space=pl.ANY)
    square = (2, bands, bands)
    dma = pltpu.SemaphoreType.DMA
    out = jax.ShapeDtypeStruct((bands, width), bf16)
    return pl.pallas_call(
        kernel,
        out_shape=(out, out),
        in_specs=[pl.BlockSpec(memory_space=pltpu.SMEM), anywhere, anywhere],
        out_specs=(vmem, vmem),
        scratch_shapes=[
            pltpu.VMEM((last_extra, 2, bands, piece), bf16),
            pltpu.VMEM((2, bands, 2 * width + piece), bf16),
            pltpu.VMEM((2, bands, width + piece), bf16),
            pltpu.VMEM((2, bands, width), bf16),
            pltpu.VMEM((2, ahead_rows, width), bf16),
            pltpu.VMEM((2, ahead_rows, width), bf16),
            pltpu.VMEM((strings + 2, 2, bands, piece), f32),
            pltpu.VMEM((strings, 2, bands - ahead_rows, piece), bf16),
            pltpu.VMEM((2 * piece, piece), bf16),
            pltpu.VMEM((strings, 2, ahead_rows, piece), bf16),
            pltpu.VMEM((strings,) + square, bf16),
            pltpu.VMEM((strings, 2, middle, bands), bf16),
            pltpu.VMEM((strings, 2, middle, bands), bf16),
            pltpu.VMEM((strings - 1, 2, middle, bands), bf16),
            pltpu.VMEM((2, middle, bands), bf16),
            pltpu.VMEM((pairs - 1, 2, share, bands), bf16),
            pltpu.VMEM((2, share, bands), bf16),
            pltpu.VMEM(square, bf16),
            pltpu.VMEM((bands, 6 * bands), bf16),
            pltpu.VMEM(square, f32),
            pltpu.VMEM(square, bf16),
            pltpu.VMEM((strings,) + square, bf16),
            pltpu.VMEM((8, 128), f32),
            pltpu.VMEM((strings, 8, 128), f32),
            pltpu.VMEM((8, 128), f32),
            pltpu.VMEM((planes, 8, 128), f32),
        ]
        + [dma((strings - 1, 2))] * 2
        + [dma((bands // 64, 2))] * 2
        + [dma((bands // 64 + 1, 2))]
        + [dma((strings, 2))] * 2
        + [dma((strings,))] * 2
        + [dma((strings - 1, chunks))] * 2
        + [dma((pairs - 1, chunks))] * 4
        + [dma((strings - 1,))] * 4
        + [dma((strings - 1,))] * 2
        + [dma((planes - 1,))] * 2
        + [dma((strings - 1,))] * 2
        + [dma((pairs, chunks))] * 2
        + [dma((2,))]
        + [dma((strings - 1,))] * 2
        + [dma((2,))]
        + [dma((strings - 1, 2))] * 2,
        compiler_params=pltpu.CompilerParams(collective_id=20 + shift, has_side_effects=True),
        name=f"steps_{shift}",
    )(where, states_re, states_im)


def spread_body(strings, planes, states_re, states_im, gmap):
    width = states_re.shape[2]
    total_width = width * planes
    offset = jnp.mod(gmap[0] - lax.axis_index("pw") * width, total_width)
    blocks_off, rest = offset // width, jnp.mod(offset, width)
    start = jnp.where(lax.axis_index("kstr") < STEPS, rest, width - rest)
    piece = width // strings
    where = jnp.stack([start // piece, jnp.mod(start, piece)]).astype(jnp.float32)
    new_re, new_im = lax.switch(
        blocks_off,
        [functools.partial(whole_step, strings, planes, shift) for shift in range(planes)],
        where, states_re[0], states_im[0],
    )
    return (new_re[None], new_im[None])


def solution(mesh):
    placed = (P("kstr", None, "pw"), P("kstr", None, "pw"), P("pw"))
    strings, planes = mesh.shape["kstr"], mesh.shape["pw"]

    def body(states_re, states_im, gmap):
        kpoints, bands, width = states_re.shape
        fits = (
            kpoints == 1
            and strings > 1
            and planes > 1
            and width % (strings * 128) == 0
            and bands % (planes * 16) == 0
            and bands % 128 == 0
            and planes % 2 == 0
            and planes > 2
            and strings == 2 * STEPS
        )
        if not fits:
            return general_body(states_re, states_im, gmap)
        return spread_body(strings, planes, states_re, states_im, gmap)

    return jax.shard_map(
        body,
        mesh=mesh,
        in_specs=placed,
        out_specs=(P("kstr", None, "pw"), P("kstr", None, "pw")),
        check_vma=False,
    )
```

```python
import functools

import jax
import jax.numpy as jnp
from jax import lax
from jax.experimental import pallas as pl
from jax.experimental.pallas import tpu as pltpu
from jax.sharding import PartitionSpec as P

NEWTON = 4
STEPS = 2


HIGH = lax.Precision.HIGHEST
EPS_SCALE = 1e-06
EPS_NORM = 1e-06
TAU_STEP = 0.25


def shifted(value, axis, by):
    count = lax.axis_size(axis)
    return lax.ppermute(value, axis, [(i, (i + by) % count) for i in range(count)])


def padded_2(block, sides, width):
    for axis, dim in sides:
        count = lax.axis_size(axis)
        forward = [(i, i + 1) for i in range(count - 1)]
        forward.append((count - 1, 0))
        backward = [(target, source) for source, target in forward]
        low = lax.ppermute(
            lax.slice_in_dim(block, block.shape[dim] - width, None, axis=dim), axis, forward
        )
        high = lax.ppermute(lax.slice_in_dim(block, 0, width, axis=dim), axis, backward)
        block = jnp.concatenate([low, block, high], axis=dim)
    return block


def complex_mul(left, right):

    def matmul(first, second):
        return jnp.einsum("kij,kjl->kil", first, second, precision=HIGH)

    real = matmul(left[:, 0], right[:, 0]) - matmul(left[:, 1], right[:, 1])
    imag = matmul(left[:, 0], right[:, 1]) + matmul(left[:, 1], right[:, 0])
    return jnp.stack([real, imag], 1)


def start_inverse(whole):
    magnitude = jnp.sqrt(whole[:, 0] * whole[:, 0] + whole[:, 1] * whole[:, 1])
    colmax = jnp.max(jnp.sum(magnitude, axis=1), axis=1)
    rowmax = jnp.max(jnp.sum(magnitude, axis=2), axis=1)
    factor = (1.0 / (colmax * rowmax + EPS_SCALE))[:, None, None]
    return jnp.stack(
        [jnp.swapaxes(whole[:, 0], 1, 2) * factor, -jnp.swapaxes(whole[:, 1], 1, 2) * factor], 1
    )


def newton_full(whole):
    iterate = start_inverse(whole)
    for turn in range(NEWTON):
        iterate = 2.0 * iterate - complex_mul(iterate, complex_mul(whole, iterate))
    return iterate


def bf_product(form, left, right):
    return jnp.einsum(form, left, right, preferred_element_type=jnp.float32)


def dual_terms(rounded, states):
    real = bf_product("kmn,kmg->kng", rounded[:, 0], states[:, 0]) + bf_product(
        "kmn,kmg->kng", rounded[:, 1], states[:, 1]
    )
    imag = bf_product("kmn,kmg->kng", rounded[:, 0], states[:, 1]) - bf_product(
        "kmn,kmg->kng", rounded[:, 1], states[:, 0]
    )
    return jnp.stack([real, imag], 1).astype(jnp.bfloat16)


def rotate_columns(block, amount, width):
    blocks_off = amount // width
    rest = amount % width
    plane_size = lax.axis_size("pw")
    for bit in range((plane_size - 1).bit_length()):
        moved = shifted(block, "pw", -(1 << bit))
        block = jnp.where(jnp.bitwise_and(jnp.right_shift(blocks_off, bit), 1) == 1, moved, block)
    after = shifted(block, "pw", -1)
    joined = jnp.concatenate([block, after], block.ndim - 1)
    return lax.dynamic_slice_in_dim(joined, rest, width, block.ndim - 1)


def general_body(states_re, states_im, gmap):
    kpoints, bands, width = states_re.shape
    string_size = lax.axis_size("kstr")
    plane_size = lax.axis_size("pw")
    string_index = lax.axis_index("kstr")
    total_width = width * plane_size
    offset = jnp.mod(gmap[0] - lax.axis_index("pw") * width, total_width)
    back_offset = jnp.mod(total_width - offset, total_width)
    at_first = string_index == 0
    at_last = string_index == string_size - 1
    count_all = 2 * kpoints * string_size * bands * width * plane_size
    states = jnp.stack([states_re, states_im], 1)
    for step in range(STEPS):
        padded = padded_2(states, (("kstr", 0),), 1)
        ahead = padded[-1:]
        behind = padded[:1]
        turned = rotate_columns(ahead, offset, width)
        ahead = jnp.where(at_last, turned, ahead)
        following = jnp.concatenate([states[1:], ahead], 0)
        s_re = bf_product("kmg,kng->kmn", states[:, 0], following[:, 0]) + bf_product(
            "kmg,kng->kmn", states[:, 1], following[:, 1]
        )
        s_im = bf_product("kmg,kng->kmn", states[:, 0], following[:, 1]) - bf_product(
            "kmg,kng->kmn", states[:, 1], following[:, 0]
        )
        partial_value = jnp.stack([s_re, s_im], 1)
        whole = lax.psum(partial_value, "pw") / (width * plane_size)
        inverse = newton_full(whole)
        rounded = inverse.astype(jnp.bfloat16)
        a_re = bf_product("kmn,kmg->kng", rounded[:, 0], following[:, 0]) - bf_product(
            "kmn,kmg->kng", rounded[:, 1], following[:, 1]
        )
        a_im = bf_product("kmn,kmg->kng", rounded[:, 0], following[:, 1]) + bf_product(
            "kmn,kmg->kng", rounded[:, 1], following[:, 0]
        )
        earlier = dual_terms(rounded[:-1], states[:-1])
        previous_inverse = shifted(rounded, "kstr", 1)
        arrived = dual_terms(previous_inverse, behind)
        placed = rotate_columns(arrived, back_offset, width)
        arrived = jnp.where(at_first, placed, arrived)
        incoming = jnp.concatenate([arrived, earlier], 0).astype(jnp.float32)
        g_re = a_im - incoming[:, 1]
        g_im = incoming[:, 0] - a_re
        total = lax.psum(jnp.sum(g_re * g_re + g_im * g_im), ("kstr", "pw"))
        rms = jnp.sqrt(total / count_all + EPS_NORM)
        new_re = (states[:, 0].astype(jnp.float32) + TAU_STEP * g_re / rms).astype(jnp.bfloat16)
        new_im = (states[:, 1].astype(jnp.float32) + TAU_STEP * g_im / rms).astype(jnp.bfloat16)
        states = jnp.stack([new_re, new_im], 1)
    return (states[:, 0], states[:, 1])


def halves(value):
    high = value.astype(jnp.bfloat16)
    return high, (value - high.astype(jnp.float32)).astype(jnp.bfloat16)


def left_factor(real, imag):
    real_high, real_low = halves(real)
    imag_high, imag_low = halves(imag)
    high = jnp.concatenate([real_high, imag_high], 1)
    return jnp.concatenate([high, high, real_low, imag_low], 1)


def right_factor(real, imag):
    real_high, real_low = halves(real)
    imag_high, imag_low = halves(imag)
    high = [
        jnp.concatenate([real_high, imag_high], 1),
        jnp.concatenate([-imag_high, real_high], 1),
    ]
    low = [
        jnp.concatenate([real_low, imag_low], 1),
        jnp.concatenate([-imag_low, real_low], 1),
    ]
    return jnp.concatenate(high + low + high, 0)


def remote_copy(source, place, send, recv, target):
    return pltpu.make_async_remote_copy(
        src_ref=source,
        dst_ref=place,
        send_sem=send,
        recv_sem=recv,
        device_id=target,
        device_id_type=pl.DeviceIdType.MESH,
    )


def greet_all(greeted, awaited):
    barrier = pltpu.get_barrier_semaphore()
    for peer in greeted:
        pl.semaphore_signal(barrier, inc=1, device_id=peer, device_id_type=pl.DeviceIdType.MESH)
    pl.semaphore_wait(barrier, awaited)


def margin_of(own, ahead):
    left = jnp.concatenate([own[0], own[1]], 1)
    form = (((1,), (1,)), ((), ()))
    real = lax.dot_general(
        left, jnp.concatenate([ahead[0], ahead[1]], 1), form, preferred_element_type=jnp.float32
    )
    imag = lax.dot_general(
        left, jnp.concatenate([ahead[1], -ahead[0]], 1), form, preferred_element_type=jnp.float32
    )
    return real, imag


def whole_step(strings, planes, shift, where, states_re, states_im):
    bands, width = states_re.shape
    piece = width // strings
    total_width = width * planes
    count_all = 2 * strings * bands * total_width
    share, middle, pairs = bands // planes, bands // 2, planes // 2
    chunks = bands // 128
    last_extra = strings + 2 * STEPS
    flipped = shift >= planes // 2
    moves = (shift + 1) % planes if flipped else shift
    ahead_rows = 3 * bands // 8
    blocks = bands // 64
    bf16, f32 = jnp.bfloat16, jnp.float32

    def kernel(where_ref, re_in, im_in, re_ref, im_ref, *scratch):
        chain, joined, chosen, aligned, early, slopes, grad, outgoing, picked = scratch[:9]
        early_out, scratch = scratch[9], scratch[4:]
        part, got_pair, half, got_string, summed, got_planes = scratch[6:12]
        block, whole, left, iterate, rounded, inverse = scratch[12:18]
        tile, first, stage, second = scratch[18:22]
        send_base, recv_base, send_join, recv_join, inside = scratch[22:27]
        send_halo, recv_halo = scratch[27:29]
        scratch = scratch[:29] + scratch[27:]
        send0, recv0, send1, recv1, send2, recv2, send3, recv3 = scratch[31:39]
        send4, recv4, send5, recv5, send6, recv6, send7, recv7 = scratch[39:47]
        send8, recv8, send9, recv9, kept, send10, recv10, kept_rest = scratch[47:55]
        send11, recv11 = scratch[55:]
        k, p = lax.axis_index("kstr"), lax.axis_index("pw")
        inputs = (re_in, im_in)
        forward = (k < STEPS).astype(jnp.int32)
        string_peers = [(lax.rem(k + step, strings), p) for step in range(1, strings)]
        plane_peers = [(k, lax.rem(p + step, planes)) for step in range(1, planes)]
        far_peers = [(k, lax.rem(p + 2 * step, planes)) for step in range(1, pairs)]
        side = lax.rem(p, 2)
        sibling = (k, p + 1 - 2 * side)

        def rows(index, size):
            return pl.ds(pl.multiple_of(index * size, size), size)

        offsets = {(step, 0) for step in range(1, strings)}
        offsets |= {(0, step) for step in range(1, planes)}
        for step in range(strings):
            offsets |= {(step, moves), (step, (planes - moves) % planes)}
        offsets = sorted(offsets - {(0, 0)})
        greet_all(
            [(lax.rem(k + a, strings), lax.rem(p + b, planes)) for a, b in offsets], len(offsets)
        )

        down = lax.rem(p + planes - moves, planes)
        target_plane = forward * down + (1 - forward) * lax.rem(p + moves, planes)
        leading = 1 - forward if flipped else forward
        taker = (k, lax.rem(p + planes + 1 - 2 * leading, planes))
        own_half = rows(1 - leading, width)
        other_half = rows(leading, width)
        mine = rows(k, piece)
        def join(number, index):
            row = rows(number, 64)
            return remote_copy(
                inputs[index].at[row, :], joined.at[index, row, other_half],
                send_join.at[number, index], recv_join.at[number, index], taker,
            )

        def join_own(number, index):
            row = rows(number, 64)
            return pltpu.make_async_copy(
                inputs[index].at[row, :], joined.at[index, row, own_half],
                inside.at[number, index],
            )

        base, insides = [], []
        for index, ref in enumerate(inputs):
            insides.append(
                pltpu.make_async_copy(
                    ref.at[:, mine], chain.at[STEPS + k, index], inside.at[blocks, index]
                )
            )
            for slot, peer in enumerate(string_peers):
                base.append(
                    remote_copy(
                        ref.at[:, rows(peer[0], piece)], chain.at[STEPS + k, index],
                        send_base.at[slot, index], recv_base.at[slot, index], peer,
                    )
                )
        for number in range(blocks):
            for index in range(2):
                join(number, index).start()
                join_own(number, index).start()
        for copy in base + insides:
            copy.start()
        joined[:, :, 2 * width :] = jnp.zeros((2, bands, piece), bf16)
        row_of = lax.broadcasted_iota(jnp.int32, (64, piece), 0)
        column_of = lax.broadcasted_iota(jnp.int32, (64, piece), 1)
        apart = (row_of - column_of).astype(f32) - where_ref[1]

        def pick(number, carry):
            there = apart + (number * 64).astype(f32)
            picked[rows(number, 64)] = jnp.maximum(1.0 - jnp.abs(there), 0.0).astype(bf16)
            return carry

        lax.fori_loop(0, 2 * piece // 64, pick, 0)
        weights = [
            jnp.full((64, piece), jnp.maximum(1.0 - jnp.abs(where_ref[0] - h), 0.0), f32)
            for h in range(strings + 1)
        ]
        weights = [weight.astype(bf16) for weight in weights]
        def extra_of(source):
            if isinstance(source, int):
                ahead = int(source < STEPS)
            else:
                ahead = (source < STEPS).astype(jnp.int32)
            return source + ahead * (STEPS + strings) - (1 - ahead) * (strings - STEPS)

        front = STEPS + strings

        def halo_copy(step, index):
            target = lax.rem(k + step, strings)
            return remote_copy(
                aligned.at[index, :, rows(target, piece)], chain.at[extra_of(k), index],
                send_halo.at[step, index], recv_halo.at[k, index], (target, target_plane),
            )

        def halo_arrival(source, index):
            place = chain.at[extra_of(source), index]
            return remote_copy(
                place, place, send_halo.at[0, index], recv_halo.at[source, index], sibling
            )

        def halo_part(step, index, number):
            target = lax.rem(k + step, strings)
            row = rows(number, 64)
            return remote_copy(
                aligned.at[index, row, rows(target, piece)], chain.at[extra_of(k), index, row],
                send_halo.at[step, index], recv_halo.at[k, index], (target, target_plane),
            )

        def own_part(index, number):
            row = rows(number, 64)
            return pltpu.make_async_copy(
                aligned.at[index, row, mine], chain.at[extra_of(k), index, row],
                recv_halo.at[k, index],
            )

        def send_block(number, carry):
            for index in range(2):
                join_own(number, index).wait()
                join(number, index).wait()
            row = rows(number, 64)

            def choose(place, carry):
                index, cut = lax.rem(place, 2), place // 2
                total = joined[index, row, rows(cut, piece)] * weights[0]
                for h in range(1, strings + 1):
                    total = total + joined[index, row, rows(cut + h, piece)] * weights[h]
                chosen[index, row, rows(cut, piece)] = total
                return carry

            lax.fori_loop(0, 2 * (strings + 1), choose, 0)

            def align(step, carry):
                cut = lax.rem(k + step, strings)
                wide = chosen[:, row, pl.ds(pl.multiple_of(cut * piece, piece), 2 * piece)]
                moved = jnp.dot(
                    wide.reshape(128, 2 * piece), picked[...], preferred_element_type=f32
                )
                moved = moved.astype(bf16).reshape(2, 64, piece)
                aligned[:, row, rows(cut, piece)] = moved
                for index in range(2):
                    if moves == 0:

                        @pl.when(step == strings)
                        def _():
                            own_part(index, number).start()

                        @pl.when(step < strings)
                        def _():
                            halo_part(step, index, number).start()

                    else:
                        halo_part(step, index, number).start()
                return carry

            if moves == 0:
                lax.fori_loop(1, strings + 1, align, 0)
            else:
                lax.fori_loop(0, strings, align, 0)
            return carry

        lax.fori_loop(0, blocks, send_block, 0)

        for copy in insides:
            copy.wait()
        for copy in base:
            copy.wait()

        def front_arrives():
            for index in range(2):
                halo_arrival(0, index).wait_recv()

        cuts = [pl.ds(chunk * 128, 128) for chunk in range(chunks)]

        def pair_copy(which):
            return remote_copy(
                part.at[which, :, rows(1 - side, middle), :], got_pair.at[which],
                send0.at[which], recv0.at[which], sibling,
            )

        def string_copy(which, slot, chunk):
            cut = cuts[chunk]
            return remote_copy(
                half.at[which, :, :, cut], got_string.at[slot, :, :, cut],
                send1.at[slot, chunk], recv1.at[slot, chunk], (which, p),
            )

        def carry_on(which):
            pair_copy(which).wait()
            both = part[which, :, rows(side, middle), :].astype(f32)
            half[which] = (both + got_pair[which].astype(f32)).astype(bf16)

            @pl.when(which != k)
            def _():
                slot = lax.rem(which - k - 1 + strings, strings)
                for chunk in range(chunks):
                    string_copy(which, slot, chunk).start()

        def find_inverses(turn):
            later = (turn > 0).astype(jnp.int32)
            lag = 1 + later

            def in_turn(number):
                return later * lax.rem(k + 1 + number + strings, strings) + (1 - later) * number

            def margin(number, carry):
                @pl.when(number >= lag)
                def _():
                    carry_on(in_turn(number - lag))

                @pl.when(number < strings)
                def _():
                    which = in_turn(number)
                    if_front = jnp.logical_and(which == strings - 1, turn == 0)
                    pl.when(if_front)(front_arrives)
                    real, imag = margin_of(chain[STEPS + which], chain[STEPS + 1 + which])
                    part[which, 0] = (real * (1.0 / total_width)).astype(bf16)
                    part[which, 1] = (imag * (1.0 / total_width)).astype(bf16)
                    pair_copy(which).start()

                return carry

            lax.fori_loop(0, strings + lag, margin, 0)

            over_planes = []
            for chunk, cut in enumerate(cuts):
                for slot, peer in enumerate(string_peers):
                    string_copy(peer[0], slot, chunk).wait()
                total = half[k, :, :, cut].astype(f32)
                for slot in range(strings - 1):
                    total = total + got_string[slot, :, :, cut].astype(f32)
                summed[:, :, cut] = total.astype(bf16)
                for slot, peer in enumerate(far_peers):
                    copy = remote_copy(
                        summed.at[:, rows(peer[1] // 2, share), cut],
                        got_planes.at[slot, :, :, cut],
                        send2.at[slot, chunk], recv2.at[slot, chunk], peer,
                    )
                    copy.start()
                    over_planes.append((chunk, copy))

            @pl.when(turn == STEPS - 1)
            def _():
                for slot in range(strings - 1):
                    home_copy(slot).start()
                home_own.start()

            back, passed = [], []
            place = rows(side * pairs + p // 2, share)
            for chunk, cut in enumerate(cuts):
                for number, copy in over_planes:
                    if number == chunk:
                        copy.wait()
                total = summed[:, rows(p // 2, share), cut].astype(f32)
                for slot in range(pairs - 1):
                    total = total + got_planes[slot, :, :, cut].astype(f32)
                block[:, :, cut] = total.astype(bf16)
                for slot, peer in enumerate(far_peers):
                    copy = remote_copy(
                        block.at[:, :, cut], whole.at[:, place, cut],
                        send3.at[slot, chunk], recv3.at[slot, chunk], peer,
                    )
                    copy.start()
                    back.append((slot, chunk, copy))
                copy = remote_copy(
                    block.at[:, :, cut], whole.at[:, place, cut],
                    send9.at[pairs - 1, chunk], recv9.at[pairs - 1, chunk], sibling,
                )
                copy.start()
                passed.append(copy)
                whole[:, place, cut] = block[:, :, cut]
            for slot, chunk, copy in back:
                copy.wait()
                source = lax.rem(p + planes - 2 * (slot + 1), planes) // 2
                there = whole.at[:, rows(side * pairs + source, share), cuts[chunk]]
                relay = remote_copy(
                    there, there, send9.at[slot, chunk], recv9.at[slot, chunk], sibling
                )
                relay.start()
                passed.append(relay)
            for copy in passed:
                copy.wait()

            real, imag = whole[0].astype(f32), whole[1].astype(f32)
            magnitude = jnp.sqrt(real * real + imag * imag)
            colmax = jnp.max(jnp.sum(magnitude, axis=0, keepdims=True), axis=1, keepdims=True)
            rowmax = jnp.max(jnp.sum(magnitude, axis=1, keepdims=True), axis=0, keepdims=True)
            factor = 1.0 / (colmax * rowmax + EPS_SCALE)
            iterate[0] = real.T * factor
            iterate[1] = -imag.T * factor
            left[...] = left_factor(real, imag)

            def newton(_, carry):
                x_re, x_im = iterate[0], iterate[1]
                product = jnp.dot(
                    left[...], right_factor(x_re, x_im), preferred_element_type=f32
                )
                product = jnp.dot(
                    left_factor(x_re, x_im),
                    right_factor(product[:, :bands], product[:, bands:]),
                    preferred_element_type=f32,
                )
                iterate[0] = 2.0 * x_re - product[:, :bands]
                iterate[1] = 2.0 * x_im - product[:, bands:]
                return carry

            lax.fori_loop(0, NEWTON, newton, 0)
            real, imag = iterate[0].T.astype(bf16), iterate[1].T.astype(bf16)
            rounded[0] = real
            rounded[1] = imag
            mine_rows = rows(side, middle)
            first_hops = []
            for index in range(2):
                for slot, peer in enumerate(string_peers):
                    copy = remote_copy(
                        rounded.at[index, mine_rows, :], inverse.at[k, index, mine_rows, :],
                        send4.at[slot, index], recv4.at[slot, index], peer,
                    )
                    copy.start()
                    first_hops.append((slot, index, copy))
            inverse[k, 0] = real
            inverse[k, 1] = imag
            second_hops = []
            for slot, index, copy in first_hops:
                copy.wait()
                source = lax.rem(k + strings - slot - 1, strings)
                there = inverse.at[source, index, mine_rows, :]
                relay = remote_copy(
                    there, there, send5.at[slot, index], recv5.at[slot, index], sibling
                )
                relay.start()
                second_hops.append(relay)
            for relay in second_hops:
                relay.wait()

        def element(place):
            link = lax.rem(place + 2 * strings - STEPS, strings)
            before = lax.rem(place + 2 * strings - STEPS - 1, strings)

            x_re, x_im = inverse[link, 0], inverse[link, 1]
            ahead = chain[place + 1].reshape(2 * bands, piece)
            a_re = jnp.dot(
                jnp.concatenate([x_re, -x_im], 1), ahead, preferred_element_type=f32
            )
            a_im = jnp.dot(
                jnp.concatenate([x_im, x_re], 1), ahead, preferred_element_type=f32
            )
            x_re, x_im = inverse[before, 0], inverse[before, 1]
            behind = chain[place - 1].reshape(2 * bands, piece)
            c_re = jnp.dot(
                jnp.concatenate([x_re, x_im], 1), behind, preferred_element_type=f32
            ).astype(bf16)
            c_im = jnp.dot(
                jnp.concatenate([-x_im, x_re], 1), behind, preferred_element_type=f32
            ).astype(bf16)
            g_re = a_im - c_im.astype(f32)
            g_im = c_re.astype(f32) - a_re
            return g_re, g_im

        def norm_first(slot):
            peer = string_peers[slot]
            return remote_copy(tile, first.at[k], send6.at[slot], recv6.at[slot], peer)

        def norm_second(slot):
            peer = plane_peers[slot]
            return remote_copy(stage, second.at[p], send7.at[slot], recv7.at[slot], peer)

        def begin_norm():
            for slot in range(strings - 1):
                norm_first(slot).start()
            first[k] = tile[...]

        def carry_norm():
            for slot in range(strings - 1):
                norm_first(slot).wait()
            stage[...] = jnp.sum(first[...], 0)
            for slot in range(planes - 1):
                norm_second(slot).start()
            second[p] = stage[...]

        ahead_of = pl.ds(0, ahead_rows)
        rest_of = pl.ds(ahead_rows, bands - ahead_rows)

        def home_copy(slot):
            target = lax.rem(k + 1 + slot, strings)
            return remote_copy(
                chain.at[STEPS + target, :, ahead_of], early.at[:, :, mine],
                send10.at[slot], recv10.at[slot], (target, p),
            )

        home_own = pltpu.make_async_copy(
            chain.at[STEPS + k, :, ahead_of], early.at[:, :, mine], kept.at[0]
        )

        def slope_copy(slot):
            target = lax.rem(k + 1 + slot, strings)
            return remote_copy(
                early_out.at[slot], slopes.at[:, :, mine],
                send8.at[slot], recv8.at[slot], (target, p),
            )

        slope_own = pltpu.make_async_copy(
            early_out.at[strings - 1], slopes.at[:, :, mine], kept.at[1]
        )

        def rest_copy(slot, index):
            target = lax.rem(k + 1 + slot, strings)
            ref = (re_ref, im_ref)[index]
            return remote_copy(
                outgoing.at[slot, index], ref.at[rest_of, mine],
                send11.at[slot, index], recv11.at[slot, index], (target, p),
            )

        def rest_own(index):
            ref = (re_ref, im_ref)[index]
            return pltpu.make_async_copy(
                outgoing.at[strings - 1, index], ref.at[rest_of, mine], kept_rest.at[index]
            )

        def find_scale(turn):
            @pl.when(turn == 0)
            def _():
                for index in range(2):
                    halo_arrival(strings - 1, index).wait_recv()

            tile[...] = jnp.zeros((8, 128), f32)

            def gradient(number, carry):
                @pl.when(number == strings)
                def _():
                    begin_norm()
                    for source in range(1, strings - 1):
                        for index in range(2):
                            halo_arrival(source, index).wait_recv()

                @pl.when(number == strings + 1)
                def _():
                    carry_norm()

                inside_string = (number < strings).astype(jnp.int32)
                place = inside_string * (STEPS + lax.rem(k + 1 + number, strings))
                place += (1 - inside_string) * (
                    STEPS - 1 + (number - strings) * (strings + 1)
                )
                g_re, g_im = element(place)
                grad[place - 1, 0] = g_re
                grad[place - 1, 1] = g_im

                @pl.when(number < strings)
                def _():
                    square = g_re * g_re + g_im * g_im
                    lanes = square[:, :128]
                    for group in range(1, piece // 128):
                        lanes = lanes + square[:, group * 128 : (group + 1) * 128]
                    tile[...] += jnp.sum(lanes.reshape(bands // 8, 8, 128), 0)

                @pl.when(turn == STEPS - 1)
                def _():
                    early_out[number, 0] = g_re[:ahead_rows].astype(bf16)
                    early_out[number, 1] = g_im[:ahead_rows].astype(bf16)

                return carry

            count = strings + 2 * (turn < STEPS - 1).astype(jnp.int32)
            lax.fori_loop(0, count, gradient, 0)

            @pl.when(turn == STEPS - 1)
            def _():
                begin_norm()
                for slot in range(strings - 1):
                    slope_copy(slot).start()
                slope_own.start()
                carry_norm()

            for slot in range(planes - 1):
                norm_second(slot).wait()
            total = jnp.sum(second[...], 0)
            total = jnp.sum(jnp.sum(total, axis=0, keepdims=True), axis=1, keepdims=True)
            return TAU_STEP / jnp.sqrt(total / count_all + EPS_NORM)

        def renewed(place, index, scale):
            old = chain[place, index].astype(f32)
            return (old + grad[place - 1, index] * scale).astype(bf16)

        def renew(scale):
            def one(place, carry):
                chain[place, 0] = renewed(place, 0, scale)
                chain[place, 1] = renewed(place, 1, scale)
                return carry

            lax.fori_loop(STEPS - 1, STEPS + strings + 1, one, 0)

        def finish(scale):
            def one(slot, carry):
                place = STEPS + lax.rem(k + 1 + slot, strings)
                for index in range(2):
                    old = chain[place, index, rest_of].astype(f32)
                    fresh = old + grad[place - 1, index, rest_of] * scale
                    outgoing[slot, index] = fresh.astype(bf16)

                    @pl.when(slot < strings - 1)
                    def _():
                        rest_copy(slot, index).start()

                    @pl.when(slot == strings - 1)
                    def _():
                        rest_own(index).start()

                return carry

            lax.fori_loop(0, strings, one, 0)
            for slot in range(strings - 1):
                home_copy(slot).wait()
                slope_copy(slot).wait()
            home_own.wait()
            slope_own.wait()
            for index, ref in enumerate((re_ref, im_ref)):
                fresh = early[index].astype(f32) + slopes[index].astype(f32) * scale
                ref[ahead_of, :] = fresh.astype(bf16)
            for index in range(2):
                for slot in range(strings - 1):
                    rest_copy(slot, index).wait()
                rest_own(index).wait()

        def sent():
            for step in range(1 if moves == 0 else 0, strings):
                for index in range(2):
                    halo_copy(step, index).wait_send()

        def one_step(turn, carry):
            find_inverses(turn)
            scale = find_scale(turn)

            @pl.when(turn < STEPS - 1)
            def _():
                renew(scale)

            @pl.when(turn == STEPS - 1)
            def _():
                finish(scale)

            return carry

        lax.fori_loop(0, STEPS, one_step, 0)
        sent()

    vmem = pl.BlockSpec(memory_space=pltpu.VMEM)
    anywhere = pl.BlockSpec(memory_space=pl.ANY)
    square = (2, bands, bands)
    dma = pltpu.SemaphoreType.DMA
    out = jax.ShapeDtypeStruct((bands, width), bf16)
    return pl.pallas_call(
        kernel,
        out_shape=(out, out),
        in_specs=[pl.BlockSpec(memory_space=pltpu.SMEM), anywhere, anywhere],
        out_specs=(vmem, vmem),
        scratch_shapes=[
            pltpu.VMEM((last_extra, 2, bands, piece), bf16),
            pltpu.VMEM((2, bands, 2 * width + piece), bf16),
            pltpu.VMEM((2, bands, width + piece), bf16),
            pltpu.VMEM((2, bands, width), bf16),
            pltpu.VMEM((2, ahead_rows, width), bf16),
            pltpu.VMEM((2, ahead_rows, width), bf16),
            pltpu.VMEM((strings + 2, 2, bands, piece), f32),
            pltpu.VMEM((strings, 2, bands - ahead_rows, piece), bf16),
            pltpu.VMEM((2 * piece, piece), bf16),
            pltpu.VMEM((strings, 2, ahead_rows, piece), bf16),
            pltpu.VMEM((strings,) + square, bf16),
            pltpu.VMEM((strings, 2, middle, bands), bf16),
            pltpu.VMEM((strings, 2, middle, bands), bf16),
            pltpu.VMEM((strings - 1, 2, middle, bands), bf16),
            pltpu.VMEM((2, middle, bands), bf16),
            pltpu.VMEM((pairs - 1, 2, share, bands), bf16),
            pltpu.VMEM((2, share, bands), bf16),
            pltpu.VMEM(square, bf16),
            pltpu.VMEM((bands, 6 * bands), bf16),
            pltpu.VMEM(square, f32),
            pltpu.VMEM(square, bf16),
            pltpu.VMEM((strings,) + square, bf16),
            pltpu.VMEM((8, 128), f32),
            pltpu.VMEM((strings, 8, 128), f32),
            pltpu.VMEM((8, 128), f32),
            pltpu.VMEM((planes, 8, 128), f32),
        ]
        + [dma((strings - 1, 2))] * 2
        + [dma((bands // 64, 2))] * 2
        + [dma((bands // 64 + 1, 2))]
        + [dma((strings, 2))] * 2
        + [dma((strings,))] * 2
        + [dma((strings - 1, chunks))] * 2
        + [dma((pairs - 1, chunks))] * 4
        + [dma((strings - 1, 2))] * 4
        + [dma((strings - 1,))] * 2
        + [dma((planes - 1,))] * 2
        + [dma((strings - 1,))] * 2
        + [dma((pairs, chunks))] * 2
        + [dma((2,))]
        + [dma((strings - 1,))] * 2
        + [dma((2,))]
        + [dma((strings - 1, 2))] * 2,
        compiler_params=pltpu.CompilerParams(collective_id=20 + shift, has_side_effects=True),
        name=f"steps_{shift}",
    )(where, states_re, states_im)


def spread_body(strings, planes, states_re, states_im, gmap):
    width = states_re.shape[2]
    total_width = width * planes
    offset = jnp.mod(gmap[0] - lax.axis_index("pw") * width, total_width)
    blocks_off, rest = offset // width, jnp.mod(offset, width)
    start = jnp.where(lax.axis_index("kstr") < STEPS, rest, width - rest)
    piece = width // strings
    where = jnp.stack([start // piece, jnp.mod(start, piece)]).astype(jnp.float32)
    new_re, new_im = lax.switch(
        blocks_off,
        [functools.partial(whole_step, strings, planes, shift) for shift in range(planes)],
        where, states_re[0], states_im[0],
    )
    return (new_re[None], new_im[None])


def solution(mesh):
    placed = (P("kstr", None, "pw"), P("kstr", None, "pw"), P("pw"))
    strings, planes = mesh.shape["kstr"], mesh.shape["pw"]

    def body(states_re, states_im, gmap):
        kpoints, bands, width = states_re.shape
        fits = (
            kpoints == 1
            and strings > 1
            and planes > 1
            and width % (strings * 128) == 0
            and bands % (planes * 16) == 0
            and bands % 128 == 0
            and planes % 2 == 0
            and planes > 2
            and strings == 2 * STEPS
        )
        if not fits:
            return general_body(states_re, states_im, gmap)
        return spread_body(strings, planes, states_re, states_im, gmap)

    return jax.shard_map(
        body,
        mesh=mesh,
        in_specs=placed,
        out_specs=(P("kstr", None, "pw"), P("kstr", None, "pw")),
        check_vma=False,
    )
```

```python
import functools

import jax
import jax.numpy as jnp
from jax import lax
from jax.experimental import pallas as pl
from jax.experimental.pallas import tpu as pltpu
from jax.sharding import PartitionSpec as P

NEWTON = 4
STEPS = 2


HIGH = lax.Precision.HIGHEST
EPS_SCALE = 1e-06
EPS_NORM = 1e-06
TAU_STEP = 0.25


def shifted(value, axis, by):
    count = lax.axis_size(axis)
    return lax.ppermute(value, axis, [(i, (i + by) % count) for i in range(count)])


def padded_2(block, sides, width):
    for axis, dim in sides:
        count = lax.axis_size(axis)
        forward = [(i, i + 1) for i in range(count - 1)]
        forward.append((count - 1, 0))
        backward = [(target, source) for source, target in forward]
        low = lax.ppermute(
            lax.slice_in_dim(block, block.shape[dim] - width, None, axis=dim), axis, forward
        )
        high = lax.ppermute(lax.slice_in_dim(block, 0, width, axis=dim), axis, backward)
        block = jnp.concatenate([low, block, high], axis=dim)
    return block


def complex_mul(left, right):

    def matmul(first, second):
        return jnp.einsum("kij,kjl->kil", first, second, precision=HIGH)

    real = matmul(left[:, 0], right[:, 0]) - matmul(left[:, 1], right[:, 1])
    imag = matmul(left[:, 0], right[:, 1]) + matmul(left[:, 1], right[:, 0])
    return jnp.stack([real, imag], 1)


def start_inverse(whole):
    magnitude = jnp.sqrt(whole[:, 0] * whole[:, 0] + whole[:, 1] * whole[:, 1])
    colmax = jnp.max(jnp.sum(magnitude, axis=1), axis=1)
    rowmax = jnp.max(jnp.sum(magnitude, axis=2), axis=1)
    factor = (1.0 / (colmax * rowmax + EPS_SCALE))[:, None, None]
    return jnp.stack(
        [jnp.swapaxes(whole[:, 0], 1, 2) * factor, -jnp.swapaxes(whole[:, 1], 1, 2) * factor], 1
    )


def newton_full(whole):
    iterate = start_inverse(whole)
    for turn in range(NEWTON):
        iterate = 2.0 * iterate - complex_mul(iterate, complex_mul(whole, iterate))
    return iterate


def bf_product(form, left, right):
    return jnp.einsum(form, left, right, preferred_element_type=jnp.float32)


def dual_terms(rounded, states):
    real = bf_product("kmn,kmg->kng", rounded[:, 0], states[:, 0]) + bf_product(
        "kmn,kmg->kng", rounded[:, 1], states[:, 1]
    )
    imag = bf_product("kmn,kmg->kng", rounded[:, 0], states[:, 1]) - bf_product(
        "kmn,kmg->kng", rounded[:, 1], states[:, 0]
    )
    return jnp.stack([real, imag], 1).astype(jnp.bfloat16)


def rotate_columns(block, amount, width):
    blocks_off = amount // width
    rest = amount % width
    plane_size = lax.axis_size("pw")
    for bit in range((plane_size - 1).bit_length()):
        moved = shifted(block, "pw", -(1 << bit))
        block = jnp.where(jnp.bitwise_and(jnp.right_shift(blocks_off, bit), 1) == 1, moved, block)
    after = shifted(block, "pw", -1)
    joined = jnp.concatenate([block, after], block.ndim - 1)
    return lax.dynamic_slice_in_dim(joined, rest, width, block.ndim - 1)


def general_body(states_re, states_im, gmap):
    kpoints, bands, width = states_re.shape
    string_size = lax.axis_size("kstr")
    plane_size = lax.axis_size("pw")
    string_index = lax.axis_index("kstr")
    total_width = width * plane_size
    offset = jnp.mod(gmap[0] - lax.axis_index("pw") * width, total_width)
    back_offset = jnp.mod(total_width - offset, total_width)
    at_first = string_index == 0
    at_last = string_index == string_size - 1
    count_all = 2 * kpoints * string_size * bands * width * plane_size
    states = jnp.stack([states_re, states_im], 1)
    for step in range(STEPS):
        padded = padded_2(states, (("kstr", 0),), 1)
        ahead = padded[-1:]
        behind = padded[:1]
        turned = rotate_columns(ahead, offset, width)
        ahead = jnp.where(at_last, turned, ahead)
        following = jnp.concatenate([states[1:], ahead], 0)
        s_re = bf_product("kmg,kng->kmn", states[:, 0], following[:, 0]) + bf_product(
            "kmg,kng->kmn", states[:, 1], following[:, 1]
        )
        s_im = bf_product("kmg,kng->kmn", states[:, 0], following[:, 1]) - bf_product(
            "kmg,kng->kmn", states[:, 1], following[:, 0]
        )
        partial_value = jnp.stack([s_re, s_im], 1)
        whole = lax.psum(partial_value, "pw") / (width * plane_size)
        inverse = newton_full(whole)
        rounded = inverse.astype(jnp.bfloat16)
        a_re = bf_product("kmn,kmg->kng", rounded[:, 0], following[:, 0]) - bf_product(
            "kmn,kmg->kng", rounded[:, 1], following[:, 1]
        )
        a_im = bf_product("kmn,kmg->kng", rounded[:, 0], following[:, 1]) + bf_product(
            "kmn,kmg->kng", rounded[:, 1], following[:, 0]
        )
        earlier = dual_terms(rounded[:-1], states[:-1])
        previous_inverse = shifted(rounded, "kstr", 1)
        arrived = dual_terms(previous_inverse, behind)
        placed = rotate_columns(arrived, back_offset, width)
        arrived = jnp.where(at_first, placed, arrived)
        incoming = jnp.concatenate([arrived, earlier], 0).astype(jnp.float32)
        g_re = a_im - incoming[:, 1]
        g_im = incoming[:, 0] - a_re
        total = lax.psum(jnp.sum(g_re * g_re + g_im * g_im), ("kstr", "pw"))
        rms = jnp.sqrt(total / count_all + EPS_NORM)
        new_re = (states[:, 0].astype(jnp.float32) + TAU_STEP * g_re / rms).astype(jnp.bfloat16)
        new_im = (states[:, 1].astype(jnp.float32) + TAU_STEP * g_im / rms).astype(jnp.bfloat16)
        states = jnp.stack([new_re, new_im], 1)
    return (states[:, 0], states[:, 1])


def halves(value):
    high = value.astype(jnp.bfloat16)
    return high, (value - high.astype(jnp.float32)).astype(jnp.bfloat16)


def left_factor(real, imag):
    real_high, real_low = halves(real)
    imag_high, imag_low = halves(imag)
    high = jnp.concatenate([real_high, imag_high], 1)
    return jnp.concatenate([high, high, real_low, imag_low], 1)


def right_factor(real, imag):
    real_high, real_low = halves(real)
    imag_high, imag_low = halves(imag)
    high = [
        jnp.concatenate([real_high, imag_high], 1),
        jnp.concatenate([-imag_high, real_high], 1),
    ]
    low = [
        jnp.concatenate([real_low, imag_low], 1),
        jnp.concatenate([-imag_low, real_low], 1),
    ]
    return jnp.concatenate(high + low + high, 0)


def remote_copy(source, place, send, recv, target):
    return pltpu.make_async_remote_copy(
        src_ref=source,
        dst_ref=place,
        send_sem=send,
        recv_sem=recv,
        device_id=target,
        device_id_type=pl.DeviceIdType.MESH,
    )


def greet_all(greeted, awaited):
    barrier = pltpu.get_barrier_semaphore()
    for peer in greeted:
        pl.semaphore_signal(barrier, inc=1, device_id=peer, device_id_type=pl.DeviceIdType.MESH)
    pl.semaphore_wait(barrier, awaited)


def margin_of(own, ahead):
    left = jnp.concatenate([own[0], own[1]], 1)
    form = (((1,), (1,)), ((), ()))
    real = lax.dot_general(
        left, jnp.concatenate([ahead[0], ahead[1]], 1), form, preferred_element_type=jnp.float32
    )
    imag = lax.dot_general(
        left, jnp.concatenate([ahead[1], -ahead[0]], 1), form, preferred_element_type=jnp.float32
    )
    return real, imag


def whole_step(strings, planes, shift, where, states_re, states_im):
    bands, width = states_re.shape
    piece = width // strings
    total_width = width * planes
    count_all = 2 * strings * bands * total_width
    share, middle, pairs = bands // planes, bands // 2, planes // 2
    chunks = bands // 128
    last_extra = strings + 2 * STEPS
    flipped = shift >= planes // 2
    moves = (shift + 1) % planes if flipped else shift
    ahead_rows = 3 * bands // 8
    blocks = bands // 64
    far = min(moves, planes - moves) >= 2
    bf16, f32 = jnp.bfloat16, jnp.float32

    def kernel(where_ref, re_in, im_in, re_ref, im_ref, *scratch):
        chain, joined, chosen, aligned, early, slopes, grad, outgoing, picked = scratch[:9]
        early_out, passing, scratch = scratch[9], scratch[10], scratch[5:]
        part, got_pair, half, got_string, summed, got_planes = scratch[6:12]
        block, whole, left, iterate, rounded, inverse = scratch[12:18]
        tile, first, stage, second = scratch[18:22]
        send_base, recv_base, send_join, recv_join, inside = scratch[22:27]
        send_halo, recv_halo = scratch[27:29]
        scratch = scratch[:29] + scratch[27:]
        send0, recv0, send1, recv1, send2, recv2, send3, recv3 = scratch[31:39]
        send4, recv4, send5, recv5, send6, recv6, send7, recv7 = scratch[39:47]
        send8, recv8, send9, recv9, kept, send10, recv10, kept_rest = scratch[47:55]
        send11, recv11, send_pass, recv_pass = scratch[55:]
        k, p = lax.axis_index("kstr"), lax.axis_index("pw")
        inputs = (re_in, im_in)
        forward = (k < STEPS).astype(jnp.int32)
        string_peers = [(lax.rem(k + step, strings), p) for step in range(1, strings)]
        plane_peers = [(k, lax.rem(p + step, planes)) for step in range(1, planes)]
        far_peers = [(k, lax.rem(p + 2 * step, planes)) for step in range(1, pairs)]
        side = lax.rem(p, 2)
        sibling = (k, p + 1 - 2 * side)

        def rows(index, size):
            return pl.ds(pl.multiple_of(index * size, size), size)

        offsets = {(step, 0) for step in range(1, strings)}
        offsets |= {(0, step) for step in range(1, planes)}
        for step in range(strings):
            offsets |= {(step, moves), (step, (planes - moves) % planes)}
        offsets = sorted(offsets - {(0, 0)})
        greet_all(
            [(lax.rem(k + a, strings), lax.rem(p + b, planes)) for a, b in offsets], len(offsets)
        )

        down = lax.rem(p + planes - moves, planes)
        target_plane = forward * down + (1 - forward) * lax.rem(p + moves, planes)
        leading = 1 - forward if flipped else forward
        taker = (k, lax.rem(p + planes + 1 - 2 * leading, planes))
        own_half = rows(1 - leading, width)
        other_half = rows(leading, width)
        mine = rows(k, piece)
        def join(number, index):
            row = rows(number, 64)
            return remote_copy(
                inputs[index].at[row, :], joined.at[index, row, other_half],
                send_join.at[number, index], recv_join.at[number, index], taker,
            )

        def join_own(number, index):
            row = rows(number, 64)
            return pltpu.make_async_copy(
                inputs[index].at[row, :], joined.at[index, row, own_half],
                inside.at[number, index],
            )

        base, insides = [], []
        for index, ref in enumerate(inputs):
            insides.append(
                pltpu.make_async_copy(
                    ref.at[:, mine], chain.at[STEPS + k, index], inside.at[blocks, index]
                )
            )
            for slot, peer in enumerate(string_peers):
                base.append(
                    remote_copy(
                        ref.at[:, rows(peer[0], piece)], chain.at[STEPS + k, index],
                        send_base.at[slot, index], recv_base.at[slot, index], peer,
                    )
                )
        for number in range(blocks):
            for index in range(2):
                join(number, index).start()
                join_own(number, index).start()
        for copy in base + insides:
            copy.start()
        joined[:, :, 2 * width :] = jnp.zeros((2, bands, piece), bf16)
        row_of = lax.broadcasted_iota(jnp.int32, (64, piece), 0)
        column_of = lax.broadcasted_iota(jnp.int32, (64, piece), 1)
        apart = (row_of - column_of).astype(f32) - where_ref[1]

        def pick(number, carry):
            there = apart + (number * 64).astype(f32)
            picked[rows(number, 64)] = jnp.maximum(1.0 - jnp.abs(there), 0.0).astype(bf16)
            return carry

        lax.fori_loop(0, 2 * piece // 64, pick, 0)
        weights = [
            jnp.full((64, piece), jnp.maximum(1.0 - jnp.abs(where_ref[0] - h), 0.0), f32)
            for h in range(strings + 1)
        ]
        weights = [weight.astype(bf16) for weight in weights]
        def extra_of(source):
            if isinstance(source, int):
                ahead = int(source < STEPS)
            else:
                ahead = (source < STEPS).astype(jnp.int32)
            return source + ahead * (STEPS + strings) - (1 - ahead) * (strings - STEPS)

        front = STEPS + strings

        def halo_copy(step, index):
            target = lax.rem(k + step, strings)
            return remote_copy(
                aligned.at[index, :, rows(target, piece)], chain.at[extra_of(k), index],
                send_halo.at[step, index], recv_halo.at[k, index], (target, target_plane),
            )

        def halo_arrival(source, index):
            place = chain.at[extra_of(source), index]
            return remote_copy(
                place, place, send_halo.at[0, index], recv_halo.at[source, index], sibling
            )

        def halo_part(step, index, number):
            target = lax.rem(k + step, strings)
            row = rows(number, 64)
            return remote_copy(
                aligned.at[index, row, rows(target, piece)], chain.at[extra_of(k), index, row],
                send_halo.at[step, index], recv_halo.at[k, index], (target, target_plane),
            )

        def pass_first(step, index):
            target = lax.rem(k + step, strings)
            return remote_copy(
                aligned.at[index, pl.ds(0, 64), rows(target, piece)], passing.at[index],
                send_halo.at[step, index], recv_pass.at[index], (target, p),
            )

        def pass_arrival(index):
            return remote_copy(
                passing.at[index], passing.at[index], send_pass.at[index],
                recv_pass.at[index], sibling,
            )

        def pass_second(index):
            return remote_copy(
                passing.at[index], chain.at[front, index, pl.ds(0, 64)],
                send_pass.at[index], recv_halo.at[0, index], (k, down),
            )

        def own_part(index, number):
            row = rows(number, 64)
            return pltpu.make_async_copy(
                aligned.at[index, row, mine], chain.at[extra_of(k), index, row],
                recv_halo.at[k, index],
            )

        def send_block(number, carry):
            for index in range(2):
                join_own(number, index).wait()
                join(number, index).wait()
            row = rows(number, 64)

            def choose(place, carry):
                index, cut = lax.rem(place, 2), place // 2
                total = joined[index, row, rows(cut, piece)] * weights[0]
                for h in range(1, strings + 1):
                    total = total + joined[index, row, rows(cut + h, piece)] * weights[h]
                chosen[index, row, rows(cut, piece)] = total
                return carry

            lax.fori_loop(0, 2 * (strings + 1), choose, 0)

            def align(step, carry):
                cut = lax.rem(k + step, strings)
                wide = chosen[:, row, pl.ds(pl.multiple_of(cut * piece, piece), 2 * piece)]
                moved = jnp.dot(
                    wide.reshape(128, 2 * piece), picked[...], preferred_element_type=f32
                )
                moved = moved.astype(bf16).reshape(2, 64, piece)
                aligned[:, row, rows(cut, piece)] = moved
                for index in range(2):
                    if moves == 0:

                        @pl.when(step == strings)
                        def _():
                            own_part(index, number).start()

                        @pl.when(step < strings)
                        def _():
                            halo_part(step, index, number).start()

                    elif not far:
                        halo_part(step, index, number).start()
                    else:
                        first = jnp.logical_and(k == 0, number == 0)
                        passed = jnp.logical_and(first, step > 0)
                        held = jnp.logical_and(k > 0, step == strings - 1)

                        @pl.when(passed)
                        def _():
                            pass_first(step, index).start()

                        @pl.when(jnp.logical_not(jnp.logical_or(passed, held)))
                        def _():
                            halo_part(step, index, number).start()

                return carry

            if moves == 0:
                lax.fori_loop(1, strings + 1, align, 0)
            else:
                lax.fori_loop(0, strings, align, 0)
            return carry

        lax.fori_loop(0, blocks, send_block, 0)

        for copy in insides:
            copy.wait()
        for copy in base:
            copy.wait()

        def front_arrives():
            if far:

                @pl.when(k > 0)
                def _():
                    for index in range(2):
                        pass_arrival(index).wait_recv()
                        pass_second(index).start()

            for index in range(2):
                halo_arrival(0, index).wait_recv()

        cuts = [pl.ds(chunk * 128, 128) for chunk in range(chunks)]

        def pair_copy(which):
            return remote_copy(
                part.at[which, :, rows(1 - side, middle), :], got_pair.at[which],
                send0.at[which], recv0.at[which], sibling,
            )

        def string_copy(which, slot, chunk):
            cut = cuts[chunk]
            return remote_copy(
                half.at[which, :, :, cut], got_string.at[slot, :, :, cut],
                send1.at[slot, chunk], recv1.at[slot, chunk], (which, p),
            )

        def carry_on(which):
            pair_copy(which).wait()
            both = part[which, :, rows(side, middle), :].astype(f32)
            half[which] = (both + got_pair[which].astype(f32)).astype(bf16)

            @pl.when(which != k)
            def _():
                slot = lax.rem(which - k - 1 + strings, strings)
                for chunk in range(chunks):
                    string_copy(which, slot, chunk).start()

        def find_inverses(turn):
            later = (turn > 0).astype(jnp.int32)
            lag = 1 + later

            def in_turn(number):
                return later * lax.rem(k + 1 + number + strings, strings) + (1 - later) * number

            def margin(number, carry):
                @pl.when(number >= lag)
                def _():
                    carry_on(in_turn(number - lag))

                @pl.when(number < strings)
                def _():
                    which = in_turn(number)
                    if_front = jnp.logical_and(which == strings - 1, turn == 0)
                    pl.when(if_front)(front_arrives)
                    real, imag = margin_of(chain[STEPS + which], chain[STEPS + 1 + which])
                    part[which, 0] = (real * (1.0 / total_width)).astype(bf16)
                    part[which, 1] = (imag * (1.0 / total_width)).astype(bf16)
                    pair_copy(which).start()

                return carry

            lax.fori_loop(0, strings + lag, margin, 0)

            over_planes = []
            for chunk, cut in enumerate(cuts):
                for slot, peer in enumerate(string_peers):
                    string_copy(peer[0], slot, chunk).wait()
                total = half[k, :, :, cut].astype(f32)
                for slot in range(strings - 1):
                    total = total + got_string[slot, :, :, cut].astype(f32)
                summed[:, :, cut] = total.astype(bf16)
                for slot, peer in enumerate(far_peers):
                    copy = remote_copy(
                        summed.at[:, rows(peer[1] // 2, share), cut],
                        got_planes.at[slot, :, :, cut],
                        send2.at[slot, chunk], recv2.at[slot, chunk], peer,
                    )
                    copy.start()
                    over_planes.append((chunk, copy))

            @pl.when(turn == STEPS - 1)
            def _():
                for slot in range(strings - 1):
                    home_copy(slot).start()
                home_own.start()

            back, passed = [], []
            place = rows(side * pairs + p // 2, share)
            for chunk, cut in enumerate(cuts):
                for number, copy in over_planes:
                    if number == chunk:
                        copy.wait()
                total = summed[:, rows(p // 2, share), cut].astype(f32)
                for slot in range(pairs - 1):
                    total = total + got_planes[slot, :, :, cut].astype(f32)
                block[:, :, cut] = total.astype(bf16)
                for slot, peer in enumerate(far_peers):
                    copy = remote_copy(
                        block.at[:, :, cut], whole.at[:, place, cut],
                        send3.at[slot, chunk], recv3.at[slot, chunk], peer,
                    )
                    copy.start()
                    back.append((slot, chunk, copy))
                copy = remote_copy(
                    block.at[:, :, cut], whole.at[:, place, cut],
                    send9.at[pairs - 1, chunk], recv9.at[pairs - 1, chunk], sibling,
                )
                copy.start()
                passed.append(copy)
                whole[:, place, cut] = block[:, :, cut]
            for slot, chunk, copy in back:
                copy.wait()
                source = lax.rem(p + planes - 2 * (slot + 1), planes) // 2
                there = whole.at[:, rows(side * pairs + source, share), cuts[chunk]]
                relay = remote_copy(
                    there, there, send9.at[slot, chunk], recv9.at[slot, chunk], sibling
                )
                relay.start()
                passed.append(relay)
            for copy in passed:
                copy.wait()

            if far:

                @pl.when(jnp.logical_and(turn == 0, k > 0))
                def _():
                    for index in range(2):
                        halo_copy(strings - 1, index).start()

            real, imag = whole[0].astype(f32), whole[1].astype(f32)
            magnitude = jnp.sqrt(real * real + imag * imag)
            colmax = jnp.max(jnp.sum(magnitude, axis=0, keepdims=True), axis=1, keepdims=True)
            rowmax = jnp.max(jnp.sum(magnitude, axis=1, keepdims=True), axis=0, keepdims=True)
            factor = 1.0 / (colmax * rowmax + EPS_SCALE)
            iterate[0] = real.T * factor
            iterate[1] = -imag.T * factor
            left[...] = left_factor(real, imag)

            def newton(_, carry):
                x_re, x_im = iterate[0], iterate[1]
                product = jnp.dot(
                    left[...], right_factor(x_re, x_im), preferred_element_type=f32
                )
                product = jnp.dot(
                    left_factor(x_re, x_im),
                    right_factor(product[:, :bands], product[:, bands:]),
                    preferred_element_type=f32,
                )
                iterate[0] = 2.0 * x_re - product[:, :bands]
                iterate[1] = 2.0 * x_im - product[:, bands:]
                return carry

            lax.fori_loop(0, NEWTON, newton, 0)
            real, imag = iterate[0].T.astype(bf16), iterate[1].T.astype(bf16)
            rounded[0] = real
            rounded[1] = imag
            mine_rows = rows(side, middle)
            first_hops = []
            for index in range(2):
                for slot, peer in enumerate(string_peers):
                    copy = remote_copy(
                        rounded.at[index, mine_rows, :], inverse.at[k, index, mine_rows, :],
                        send4.at[slot, index], recv4.at[slot, index], peer,
                    )
                    copy.start()
                    first_hops.append((slot, index, copy))
            inverse[k, 0] = real
            inverse[k, 1] = imag
            second_hops = []
            for slot, index, copy in first_hops:
                copy.wait()
                source = lax.rem(k + strings - slot - 1, strings)
                there = inverse.at[source, index, mine_rows, :]
                relay = remote_copy(
                    there, there, send5.at[slot, index], recv5.at[slot, index], sibling
                )
                relay.start()
                second_hops.append(relay)
            for relay in second_hops:
                relay.wait()

        def element(place):
            link = lax.rem(place + 2 * strings - STEPS, strings)
            before = lax.rem(place + 2 * strings - STEPS - 1, strings)

            x_re, x_im = inverse[link, 0], inverse[link, 1]
            ahead = chain[place + 1].reshape(2 * bands, piece)
            a_re = jnp.dot(
                jnp.concatenate([x_re, -x_im], 1), ahead, preferred_element_type=f32
            )
            a_im = jnp.dot(
                jnp.concatenate([x_im, x_re], 1), ahead, preferred_element_type=f32
            )
            x_re, x_im = inverse[before, 0], inverse[before, 1]
            behind = chain[place - 1].reshape(2 * bands, piece)
            c_re = jnp.dot(
                jnp.concatenate([x_re, x_im], 1), behind, preferred_element_type=f32
            ).astype(bf16)
            c_im = jnp.dot(
                jnp.concatenate([-x_im, x_re], 1), behind, preferred_element_type=f32
            ).astype(bf16)
            g_re = a_im - c_im.astype(f32)
            g_im = c_re.astype(f32) - a_re
            return g_re, g_im

        def norm_first(slot):
            peer = string_peers[slot]
            return remote_copy(tile, first.at[k], send6.at[slot], recv6.at[slot], peer)

        def norm_second(slot):
            peer = plane_peers[slot]
            return remote_copy(stage, second.at[p], send7.at[slot], recv7.at[slot], peer)

        def begin_norm():
            for slot in range(strings - 1):
                norm_first(slot).start()
            first[k] = tile[...]

        def carry_norm():
            for slot in range(strings - 1):
                norm_first(slot).wait()
            stage[...] = jnp.sum(first[...], 0)
            for slot in range(planes - 1):
                norm_second(slot).start()
            second[p] = stage[...]

        ahead_of = pl.ds(0, ahead_rows)
        rest_of = pl.ds(ahead_rows, bands - ahead_rows)

        def home_copy(slot):
            target = lax.rem(k + 1 + slot, strings)
            return remote_copy(
                chain.at[STEPS + target, :, ahead_of], early.at[:, :, mine],
                send10.at[slot], recv10.at[slot], (target, p),
            )

        home_own = pltpu.make_async_copy(
            chain.at[STEPS + k, :, ahead_of], early.at[:, :, mine], kept.at[0]
        )

        def slope_copy(slot):
            target = lax.rem(k + 1 + slot, strings)
            return remote_copy(
                early_out.at[slot], slopes.at[:, :, mine],
                send8.at[slot], recv8.at[slot], (target, p),
            )

        slope_own = pltpu.make_async_copy(
            early_out.at[strings - 1], slopes.at[:, :, mine], kept.at[1]
        )

        def rest_copy(slot, index):
            target = lax.rem(k + 1 + slot, strings)
            ref = (re_ref, im_ref)[index]
            return remote_copy(
                outgoing.at[slot, index], ref.at[rest_of, mine],
                send11.at[slot, index], recv11.at[slot, index], (target, p),
            )

        def rest_own(index):
            ref = (re_ref, im_ref)[index]
            return pltpu.make_async_copy(
                outgoing.at[strings - 1, index], ref.at[rest_of, mine], kept_rest.at[index]
            )

        def find_scale(turn):
            @pl.when(turn == 0)
            def _():
                for index in range(2):
                    halo_arrival(strings - 1, index).wait_recv()

            tile[...] = jnp.zeros((8, 128), f32)

            def gradient(number, carry):
                @pl.when(number == strings)
                def _():
                    begin_norm()
                    for source in range(1, strings - 1):
                        for index in range(2):
                            halo_arrival(source, index).wait_recv()

                @pl.when(number == strings + 1)
                def _():
                    carry_norm()

                inside_string = (number < strings).astype(jnp.int32)
                place = inside_string * (STEPS + lax.rem(k + 1 + number, strings))
                place += (1 - inside_string) * (
                    STEPS - 1 + (number - strings) * (strings + 1)
                )
                g_re, g_im = element(place)
                grad[place - 1, 0] = g_re
                grad[place - 1, 1] = g_im

                @pl.when(number < strings)
                def _():
                    square = g_re * g_re + g_im * g_im
                    lanes = square[:, :128]
                    for group in range(1, piece // 128):
                        lanes = lanes + square[:, group * 128 : (group + 1) * 128]
                    tile[...] += jnp.sum(lanes.reshape(bands // 8, 8, 128), 0)

                @pl.when(turn == STEPS - 1)
                def _():
                    early_out[number, 0] = g_re[:ahead_rows].astype(bf16)
                    early_out[number, 1] = g_im[:ahead_rows].astype(bf16)

                return carry

            count = strings + 2 * (turn < STEPS - 1).astype(jnp.int32)
            lax.fori_loop(0, count, gradient, 0)

            @pl.when(turn == STEPS - 1)
            def _():
                begin_norm()
                for slot in range(strings - 1):
                    slope_copy(slot).start()
                slope_own.start()
                carry_norm()

            for slot in range(planes - 1):
                norm_second(slot).wait()
            total = jnp.sum(second[...], 0)
            total = jnp.sum(jnp.sum(total, axis=0, keepdims=True), axis=1, keepdims=True)
            return TAU_STEP / jnp.sqrt(total / count_all + EPS_NORM)

        def renewed(place, index, scale):
            old = chain[place, index].astype(f32)
            return (old + grad[place - 1, index] * scale).astype(bf16)

        def renew(scale):
            def one(place, carry):
                chain[place, 0] = renewed(place, 0, scale)
                chain[place, 1] = renewed(place, 1, scale)
                return carry

            lax.fori_loop(STEPS - 1, STEPS + strings + 1, one, 0)

        def finish(scale):
            def one(slot, carry):
                place = STEPS + lax.rem(k + 1 + slot, strings)
                for index in range(2):
                    old = chain[place, index, rest_of].astype(f32)
                    fresh = old + grad[place - 1, index, rest_of] * scale
                    outgoing[slot, index] = fresh.astype(bf16)

                    @pl.when(slot < strings - 1)
                    def _():
                        rest_copy(slot, index).start()

                    @pl.when(slot == strings - 1)
                    def _():
                        rest_own(index).start()

                return carry

            lax.fori_loop(0, strings, one, 0)
            for slot in range(strings - 1):
                home_copy(slot).wait()
                slope_copy(slot).wait()
            home_own.wait()
            slope_own.wait()
            for index, ref in enumerate((re_ref, im_ref)):
                fresh = early[index].astype(f32) + slopes[index].astype(f32) * scale
                ref[ahead_of, :] = fresh.astype(bf16)
            for index in range(2):
                for slot in range(strings - 1):
                    rest_copy(slot, index).wait()
                rest_own(index).wait()

        def sent():
            for step in range(1 if moves == 0 else 0, strings):
                for index in range(2):
                    halo_copy(step, index).wait_send()
            if far:

                @pl.when(k > 0)
                def _():
                    for index in range(2):
                        pass_second(index).wait_send()

        def one_step(turn, carry):
            find_inverses(turn)
            scale = find_scale(turn)

            @pl.when(turn < STEPS - 1)
            def _():
                renew(scale)

            @pl.when(turn == STEPS - 1)
            def _():
                finish(scale)

            return carry

        lax.fori_loop(0, STEPS, one_step, 0)
        sent()

    vmem = pl.BlockSpec(memory_space=pltpu.VMEM)
    anywhere = pl.BlockSpec(memory_space=pl.ANY)
    square = (2, bands, bands)
    dma = pltpu.SemaphoreType.DMA
    out = jax.ShapeDtypeStruct((bands, width), bf16)
    return pl.pallas_call(
        kernel,
        out_shape=(out, out),
        in_specs=[pl.BlockSpec(memory_space=pltpu.SMEM), anywhere, anywhere],
        out_specs=(vmem, vmem),
        scratch_shapes=[
            pltpu.VMEM((last_extra, 2, bands, piece), bf16),
            pltpu.VMEM((2, bands, 2 * width + piece), bf16),
            pltpu.VMEM((2, bands, width + piece), bf16),
            pltpu.VMEM((2, bands, width), bf16),
            pltpu.VMEM((2, ahead_rows, width), bf16),
            pltpu.VMEM((2, ahead_rows, width), bf16),
            pltpu.VMEM((strings + 2, 2, bands, piece), f32),
            pltpu.VMEM((strings, 2, bands - ahead_rows, piece), bf16),
            pltpu.VMEM((2 * piece, piece), bf16),
            pltpu.VMEM((strings, 2, ahead_rows, piece), bf16),
            pltpu.VMEM((2, 64, piece), bf16),
            pltpu.VMEM((strings,) + square, bf16),
            pltpu.VMEM((strings, 2, middle, bands), bf16),
            pltpu.VMEM((strings, 2, middle, bands), bf16),
            pltpu.VMEM((strings - 1, 2, middle, bands), bf16),
            pltpu.VMEM((2, middle, bands), bf16),
            pltpu.VMEM((pairs - 1, 2, share, bands), bf16),
            pltpu.VMEM((2, share, bands), bf16),
            pltpu.VMEM(square, bf16),
            pltpu.VMEM((bands, 6 * bands), bf16),
            pltpu.VMEM(square, f32),
            pltpu.VMEM(square, bf16),
            pltpu.VMEM((strings,) + square, bf16),
            pltpu.VMEM((8, 128), f32),
            pltpu.VMEM((strings, 8, 128), f32),
            pltpu.VMEM((8, 128), f32),
            pltpu.VMEM((planes, 8, 128), f32),
        ]
        + [dma((strings - 1, 2))] * 2
        + [dma((bands // 64, 2))] * 2
        + [dma((bands // 64 + 1, 2))]
        + [dma((strings, 2))] * 2
        + [dma((strings,))] * 2
        + [dma((strings - 1, chunks))] * 2
        + [dma((pairs - 1, chunks))] * 4
        + [dma((strings - 1, 2))] * 4
        + [dma((strings - 1,))] * 2
        + [dma((planes - 1,))] * 2
        + [dma((strings - 1,))] * 2
        + [dma((pairs, chunks))] * 2
        + [dma((2,))]
        + [dma((strings - 1,))] * 2
        + [dma((2,))]
        + [dma((strings - 1, 2))] * 2
        + [dma((2,))] * 2,
        compiler_params=pltpu.CompilerParams(collective_id=20 + shift, has_side_effects=True),
        name=f"steps_{shift}",
    )(where, states_re, states_im)


def spread_body(strings, planes, states_re, states_im, gmap):
    width = states_re.shape[2]
    total_width = width * planes
    offset = jnp.mod(gmap[0] - lax.axis_index("pw") * width, total_width)
    blocks_off, rest = offset // width, jnp.mod(offset, width)
    start = jnp.where(lax.axis_index("kstr") < STEPS, rest, width - rest)
    piece = width // strings
    where = jnp.stack([start // piece, jnp.mod(start, piece)]).astype(jnp.float32)
    new_re, new_im = lax.switch(
        blocks_off,
        [functools.partial(whole_step, strings, planes, shift) for shift in range(planes)],
        where, states_re[0], states_im[0],
    )
    return (new_re[None], new_im[None])


def solution(mesh):
    placed = (P("kstr", None, "pw"), P("kstr", None, "pw"), P("pw"))
    strings, planes = mesh.shape["kstr"], mesh.shape["pw"]

    def body(states_re, states_im, gmap):
        kpoints, bands, width = states_re.shape
        fits = (
            kpoints == 1
            and strings > 1
            and planes > 1
            and width % (strings * 128) == 0
            and bands % (planes * 16) == 0
            and bands % 128 == 0
            and planes % 2 == 0
            and planes > 2
            and strings == 2 * STEPS
        )
        if not fits:
            return general_body(states_re, states_im, gmap)
        return spread_body(strings, planes, states_re, states_im, gmap)

    return jax.shard_map(
        body,
        mesh=mesh,
        in_specs=placed,
        out_specs=(P("kstr", None, "pw"), P("kstr", None, "pw")),
        check_vma=False,
    )
```

```python
import functools

import jax
import jax.numpy as jnp
from jax import lax
from jax.experimental import pallas as pl
from jax.experimental.pallas import tpu as pltpu
from jax.sharding import PartitionSpec as P

NEWTON = 4
STEPS = 2


HIGH = lax.Precision.HIGHEST
EPS_SCALE = 1e-06
EPS_NORM = 1e-06
TAU_STEP = 0.25


def shifted(value, axis, by):
    count = lax.axis_size(axis)
    return lax.ppermute(value, axis, [(i, (i + by) % count) for i in range(count)])


def padded_2(block, sides, width):
    for axis, dim in sides:
        count = lax.axis_size(axis)
        forward = [(i, i + 1) for i in range(count - 1)]
        forward.append((count - 1, 0))
        backward = [(target, source) for source, target in forward]
        low = lax.ppermute(
            lax.slice_in_dim(block, block.shape[dim] - width, None, axis=dim), axis, forward
        )
        high = lax.ppermute(lax.slice_in_dim(block, 0, width, axis=dim), axis, backward)
        block = jnp.concatenate([low, block, high], axis=dim)
    return block


def complex_mul(left, right):

    def matmul(first, second):
        return jnp.einsum("kij,kjl->kil", first, second, precision=HIGH)

    real = matmul(left[:, 0], right[:, 0]) - matmul(left[:, 1], right[:, 1])
    imag = matmul(left[:, 0], right[:, 1]) + matmul(left[:, 1], right[:, 0])
    return jnp.stack([real, imag], 1)


def start_inverse(whole):
    magnitude = jnp.sqrt(whole[:, 0] * whole[:, 0] + whole[:, 1] * whole[:, 1])
    colmax = jnp.max(jnp.sum(magnitude, axis=1), axis=1)
    rowmax = jnp.max(jnp.sum(magnitude, axis=2), axis=1)
    factor = (1.0 / (colmax * rowmax + EPS_SCALE))[:, None, None]
    return jnp.stack(
        [jnp.swapaxes(whole[:, 0], 1, 2) * factor, -jnp.swapaxes(whole[:, 1], 1, 2) * factor], 1
    )


def newton_full(whole):
    iterate = start_inverse(whole)
    for turn in range(NEWTON):
        iterate = 2.0 * iterate - complex_mul(iterate, complex_mul(whole, iterate))
    return iterate


def bf_product(form, left, right):
    return jnp.einsum(form, left, right, preferred_element_type=jnp.float32)


def dual_terms(rounded, states):
    real = bf_product("kmn,kmg->kng", rounded[:, 0], states[:, 0]) + bf_product(
        "kmn,kmg->kng", rounded[:, 1], states[:, 1]
    )
    imag = bf_product("kmn,kmg->kng", rounded[:, 0], states[:, 1]) - bf_product(
        "kmn,kmg->kng", rounded[:, 1], states[:, 0]
    )
    return jnp.stack([real, imag], 1).astype(jnp.bfloat16)


def rotate_columns(block, amount, width):
    blocks_off = amount // width
    rest = amount % width
    plane_size = lax.axis_size("pw")
    for bit in range((plane_size - 1).bit_length()):
        moved = shifted(block, "pw", -(1 << bit))
        block = jnp.where(jnp.bitwise_and(jnp.right_shift(blocks_off, bit), 1) == 1, moved, block)
    after = shifted(block, "pw", -1)
    joined = jnp.concatenate([block, after], block.ndim - 1)
    return lax.dynamic_slice_in_dim(joined, rest, width, block.ndim - 1)


def general_body(states_re, states_im, gmap):
    kpoints, bands, width = states_re.shape
    string_size = lax.axis_size("kstr")
    plane_size = lax.axis_size("pw")
    string_index = lax.axis_index("kstr")
    total_width = width * plane_size
    offset = jnp.mod(gmap[0] - lax.axis_index("pw") * width, total_width)
    back_offset = jnp.mod(total_width - offset, total_width)
    at_first = string_index == 0
    at_last = string_index == string_size - 1
    count_all = 2 * kpoints * string_size * bands * width * plane_size
    states = jnp.stack([states_re, states_im], 1)
    for step in range(STEPS):
        padded = padded_2(states, (("kstr", 0),), 1)
        ahead = padded[-1:]
        behind = padded[:1]
        turned = rotate_columns(ahead, offset, width)
        ahead = jnp.where(at_last, turned, ahead)
        following = jnp.concatenate([states[1:], ahead], 0)
        s_re = bf_product("kmg,kng->kmn", states[:, 0], following[:, 0]) + bf_product(
            "kmg,kng->kmn", states[:, 1], following[:, 1]
        )
        s_im = bf_product("kmg,kng->kmn", states[:, 0], following[:, 1]) - bf_product(
            "kmg,kng->kmn", states[:, 1], following[:, 0]
        )
        partial_value = jnp.stack([s_re, s_im], 1)
        whole = lax.psum(partial_value, "pw") / (width * plane_size)
        inverse = newton_full(whole)
        rounded = inverse.astype(jnp.bfloat16)
        a_re = bf_product("kmn,kmg->kng", rounded[:, 0], following[:, 0]) - bf_product(
            "kmn,kmg->kng", rounded[:, 1], following[:, 1]
        )
        a_im = bf_product("kmn,kmg->kng", rounded[:, 0], following[:, 1]) + bf_product(
            "kmn,kmg->kng", rounded[:, 1], following[:, 0]
        )
        earlier = dual_terms(rounded[:-1], states[:-1])
        previous_inverse = shifted(rounded, "kstr", 1)
        arrived = dual_terms(previous_inverse, behind)
        placed = rotate_columns(arrived, back_offset, width)
        arrived = jnp.where(at_first, placed, arrived)
        incoming = jnp.concatenate([arrived, earlier], 0).astype(jnp.float32)
        g_re = a_im - incoming[:, 1]
        g_im = incoming[:, 0] - a_re
        total = lax.psum(jnp.sum(g_re * g_re + g_im * g_im), ("kstr", "pw"))
        rms = jnp.sqrt(total / count_all + EPS_NORM)
        new_re = (states[:, 0].astype(jnp.float32) + TAU_STEP * g_re / rms).astype(jnp.bfloat16)
        new_im = (states[:, 1].astype(jnp.float32) + TAU_STEP * g_im / rms).astype(jnp.bfloat16)
        states = jnp.stack([new_re, new_im], 1)
    return (states[:, 0], states[:, 1])


def halves(value):
    high = value.astype(jnp.bfloat16)
    return high, (value - high.astype(jnp.float32)).astype(jnp.bfloat16)


def left_factor(real, imag):
    real_high, real_low = halves(real)
    imag_high, imag_low = halves(imag)
    high = jnp.concatenate([real_high, imag_high], 1)
    return jnp.concatenate([high, high, real_low, imag_low], 1)


def right_factor(real, imag):
    real_high, real_low = halves(real)
    imag_high, imag_low = halves(imag)
    high = [
        jnp.concatenate([real_high, imag_high], 1),
        jnp.concatenate([-imag_high, real_high], 1),
    ]
    low = [
        jnp.concatenate([real_low, imag_low], 1),
        jnp.concatenate([-imag_low, real_low], 1),
    ]
    return jnp.concatenate(high + low + high, 0)


def remote_copy(source, place, send, recv, target):
    return pltpu.make_async_remote_copy(
        src_ref=source,
        dst_ref=place,
        send_sem=send,
        recv_sem=recv,
        device_id=target,
        device_id_type=pl.DeviceIdType.MESH,
    )


def greet_all(greeted, awaited):
    barrier = pltpu.get_barrier_semaphore()
    for peer in greeted:
        pl.semaphore_signal(barrier, inc=1, device_id=peer, device_id_type=pl.DeviceIdType.MESH)
    pl.semaphore_wait(barrier, awaited)


def margin_of(own, ahead):
    left = jnp.concatenate([own[0], own[1]], 1)
    form = (((1,), (1,)), ((), ()))
    real = lax.dot_general(
        left, jnp.concatenate([ahead[0], ahead[1]], 1), form, preferred_element_type=jnp.float32
    )
    imag = lax.dot_general(
        left, jnp.concatenate([ahead[1], -ahead[0]], 1), form, preferred_element_type=jnp.float32
    )
    return real, imag


def whole_step(strings, planes, shift, where, states_re, states_im):
    bands, width = states_re.shape
    piece = width // strings
    total_width = width * planes
    count_all = 2 * strings * bands * total_width
    share, middle, pairs = bands // planes, bands // 2, planes // 2
    chunks = bands // 128
    last_extra = strings + 2 * STEPS
    flipped = shift >= planes // 2
    moves = (shift + 1) % planes if flipped else shift
    ahead_rows = 3 * bands // 8
    blocks = bands // 64
    far = min(moves, planes - moves) >= 2
    late_parts = (1,) if min(moves, planes - moves) == 2 else (0, 1)
    bf16, f32 = jnp.bfloat16, jnp.float32

    def kernel(where_ref, re_in, im_in, re_ref, im_ref, *scratch):
        chain, joined, chosen, aligned, early, slopes, grad, outgoing, picked = scratch[:9]
        early_out, passing, scratch = scratch[9], scratch[10], scratch[5:]
        part, got_pair, half, got_string, summed, got_planes = scratch[6:12]
        block, whole, left, iterate, rounded, inverse = scratch[12:18]
        tile, first, stage, second = scratch[18:22]
        send_base, recv_base, send_join, recv_join, inside = scratch[22:27]
        send_halo, recv_halo = scratch[27:29]
        scratch = scratch[:29] + scratch[27:]
        send0, recv0, send1, recv1, send2, recv2, send3, recv3 = scratch[31:39]
        send4, recv4, send5, recv5, send6, recv6, send7, recv7 = scratch[39:47]
        send8, recv8, send9, recv9, kept, send10, recv10, kept_rest = scratch[47:55]
        send11, recv11, send_pass, recv_pass = scratch[55:]
        k, p = lax.axis_index("kstr"), lax.axis_index("pw")
        inputs = (re_in, im_in)
        forward = (k < STEPS).astype(jnp.int32)
        string_peers = [(lax.rem(k + step, strings), p) for step in range(1, strings)]
        plane_peers = [(k, lax.rem(p + step, planes)) for step in range(1, planes)]
        far_peers = [(k, lax.rem(p + 2 * step, planes)) for step in range(1, pairs)]
        side = lax.rem(p, 2)
        sibling = (k, p + 1 - 2 * side)

        def rows(index, size):
            return pl.ds(pl.multiple_of(index * size, size), size)

        offsets = {(step, 0) for step in range(1, strings)}
        offsets |= {(0, step) for step in range(1, planes)}
        for step in range(strings):
            offsets |= {(step, moves), (step, (planes - moves) % planes)}
        offsets = sorted(offsets - {(0, 0)})
        greet_all(
            [(lax.rem(k + a, strings), lax.rem(p + b, planes)) for a, b in offsets], len(offsets)
        )

        down = lax.rem(p + planes - moves, planes)
        target_plane = forward * down + (1 - forward) * lax.rem(p + moves, planes)
        leading = 1 - forward if flipped else forward
        taker = (k, lax.rem(p + planes + 1 - 2 * leading, planes))
        own_half = rows(1 - leading, width)
        other_half = rows(leading, width)
        mine = rows(k, piece)
        def join(number, index):
            row = rows(number, 64)
            return remote_copy(
                inputs[index].at[row, :], joined.at[index, row, other_half],
                send_join.at[number, index], recv_join.at[number, index], taker,
            )

        def join_own(number, index):
            row = rows(number, 64)
            return pltpu.make_async_copy(
                inputs[index].at[row, :], joined.at[index, row, own_half],
                inside.at[number, index],
            )

        base, insides = [], []
        for index, ref in enumerate(inputs):
            insides.append(
                pltpu.make_async_copy(
                    ref.at[:, mine], chain.at[STEPS + k, index], inside.at[blocks, index]
                )
            )
            for slot, peer in enumerate(string_peers):
                base.append(
                    remote_copy(
                        ref.at[:, rows(peer[0], piece)], chain.at[STEPS + k, index],
                        send_base.at[slot, index], recv_base.at[slot, index], peer,
                    )
                )
        for number in range(blocks):
            for index in range(2):
                join(number, index).start()
                join_own(number, index).start()
        for copy in base + insides:
            copy.start()
        joined[:, :, 2 * width :] = jnp.zeros((2, bands, piece), bf16)
        row_of = lax.broadcasted_iota(jnp.int32, (64, piece), 0)
        column_of = lax.broadcasted_iota(jnp.int32, (64, piece), 1)
        apart = (row_of - column_of).astype(f32) - where_ref[1]

        def pick(number, carry):
            there = apart + (number * 64).astype(f32)
            picked[rows(number, 64)] = jnp.maximum(1.0 - jnp.abs(there), 0.0).astype(bf16)
            return carry

        lax.fori_loop(0, 2 * piece // 64, pick, 0)
        weights = [
            jnp.full((64, piece), jnp.maximum(1.0 - jnp.abs(where_ref[0] - h), 0.0), f32)
            for h in range(strings + 1)
        ]
        weights = [weight.astype(bf16) for weight in weights]
        def extra_of(source):
            if isinstance(source, int):
                ahead = int(source < STEPS)
            else:
                ahead = (source < STEPS).astype(jnp.int32)
            return source + ahead * (STEPS + strings) - (1 - ahead) * (strings - STEPS)

        front = STEPS + strings

        def halo_copy(step, index):
            target = lax.rem(k + step, strings)
            return remote_copy(
                aligned.at[index, :, rows(target, piece)], chain.at[extra_of(k), index],
                send_halo.at[step, index], recv_halo.at[k, index], (target, target_plane),
            )

        def halo_arrival(source, index):
            place = chain.at[extra_of(source), index]
            return remote_copy(
                place, place, send_halo.at[0, index], recv_halo.at[source, index], sibling
            )

        def halo_part(step, index, number):
            target = lax.rem(k + step, strings)
            row = rows(number, 64)
            return remote_copy(
                aligned.at[index, row, rows(target, piece)], chain.at[extra_of(k), index, row],
                send_halo.at[step, index], recv_halo.at[k, index], (target, target_plane),
            )

        def pass_first(step, index):
            target = lax.rem(k + step, strings)
            return remote_copy(
                aligned.at[index, pl.ds(0, 64), rows(target, piece)], passing.at[index],
                send_halo.at[step, index], recv_pass.at[index], (target, p),
            )

        def pass_arrival(index):
            return remote_copy(
                passing.at[index], passing.at[index], send_pass.at[index],
                recv_pass.at[index], sibling,
            )

        def pass_second(index):
            return remote_copy(
                passing.at[index], chain.at[front, index, pl.ds(0, 64)],
                send_pass.at[index], recv_halo.at[0, index], (k, down),
            )

        def own_part(index, number):
            row = rows(number, 64)
            return pltpu.make_async_copy(
                aligned.at[index, row, mine], chain.at[extra_of(k), index, row],
                recv_halo.at[k, index],
            )

        def send_block(number, carry):
            for index in range(2):
                join_own(number, index).wait()
                join(number, index).wait()
            row = rows(number, 64)

            def choose(place, carry):
                index, cut = lax.rem(place, 2), place // 2
                total = joined[index, row, rows(cut, piece)] * weights[0]
                for h in range(1, strings + 1):
                    total = total + joined[index, row, rows(cut + h, piece)] * weights[h]
                chosen[index, row, rows(cut, piece)] = total
                return carry

            lax.fori_loop(0, 2 * (strings + 1), choose, 0)

            def align(step, carry):
                cut = lax.rem(k + step, strings)
                wide = chosen[:, row, pl.ds(pl.multiple_of(cut * piece, piece), 2 * piece)]
                moved = jnp.dot(
                    wide.reshape(128, 2 * piece), picked[...], preferred_element_type=f32
                )
                moved = moved.astype(bf16).reshape(2, 64, piece)
                aligned[:, row, rows(cut, piece)] = moved
                for index in range(2):
                    if moves == 0:

                        @pl.when(step == strings)
                        def _():
                            own_part(index, number).start()

                        @pl.when(step < strings)
                        def _():
                            halo_part(step, index, number).start()

                    elif not far:
                        halo_part(step, index, number).start()
                    else:
                        first = jnp.logical_and(k == 0, number == 0)
                        passed = jnp.logical_and(first, step > 0)
                        last_step = step == strings - 1 if index in late_parts else step < 0
                        held = jnp.logical_and(k > 0, last_step)

                        @pl.when(passed)
                        def _():
                            pass_first(step, index).start()

                        @pl.when(jnp.logical_not(jnp.logical_or(passed, held)))
                        def _():
                            halo_part(step, index, number).start()

                return carry

            if moves == 0:
                lax.fori_loop(1, strings + 1, align, 0)
            else:
                lax.fori_loop(0, strings, align, 0)
            return carry

        lax.fori_loop(0, blocks, send_block, 0)

        for copy in insides:
            copy.wait()
        for copy in base:
            copy.wait()

        def front_arrives():
            if far:

                @pl.when(k > 0)
                def _():
                    for index in range(2):
                        pass_arrival(index).wait_recv()
                        pass_second(index).start()

            for index in range(2):
                halo_arrival(0, index).wait_recv()

        cuts = [pl.ds(chunk * 128, 128) for chunk in range(chunks)]

        def pair_copy(which):
            return remote_copy(
                part.at[which, :, rows(1 - side, middle), :], got_pair.at[which],
                send0.at[which], recv0.at[which], sibling,
            )

        def string_copy(which, slot, chunk):
            cut = cuts[chunk]
            return remote_copy(
                half.at[which, :, :, cut], got_string.at[slot, :, :, cut],
                send1.at[slot, chunk], recv1.at[slot, chunk], (which, p),
            )

        def carry_on(which):
            pair_copy(which).wait()
            both = part[which, :, rows(side, middle), :].astype(f32)
            half[which] = (both + got_pair[which].astype(f32)).astype(bf16)

            @pl.when(which != k)
            def _():
                slot = lax.rem(which - k - 1 + strings, strings)
                for chunk in range(chunks):
                    string_copy(which, slot, chunk).start()

        def find_inverses(turn):
            later = (turn > 0).astype(jnp.int32)
            lag = 1 + later

            def in_turn(number):
                return later * lax.rem(k + 1 + number + strings, strings) + (1 - later) * number

            def margin(number, carry):
                @pl.when(number >= lag)
                def _():
                    carry_on(in_turn(number - lag))

                @pl.when(number < strings)
                def _():
                    which = in_turn(number)
                    if_front = jnp.logical_and(which == strings - 1, turn == 0)
                    pl.when(if_front)(front_arrives)
                    real, imag = margin_of(chain[STEPS + which], chain[STEPS + 1 + which])
                    part[which, 0] = (real * (1.0 / total_width)).astype(bf16)
                    part[which, 1] = (imag * (1.0 / total_width)).astype(bf16)
                    pair_copy(which).start()

                return carry

            lax.fori_loop(0, strings + lag, margin, 0)

            over_planes = []
            for chunk, cut in enumerate(cuts):
                for slot, peer in enumerate(string_peers):
                    string_copy(peer[0], slot, chunk).wait()
                total = half[k, :, :, cut].astype(f32)
                for slot in range(strings - 1):
                    total = total + got_string[slot, :, :, cut].astype(f32)
                summed[:, :, cut] = total.astype(bf16)
                for slot, peer in enumerate(far_peers):
                    copy = remote_copy(
                        summed.at[:, rows(peer[1] // 2, share), cut],
                        got_planes.at[slot, :, :, cut],
                        send2.at[slot, chunk], recv2.at[slot, chunk], peer,
                    )
                    copy.start()
                    over_planes.append((chunk, copy))

            @pl.when(turn == STEPS - 1)
            def _():
                for slot in range(strings - 1):
                    home_copy(slot).start()
                home_own.start()

            back, passed = [], []
            place = rows(side * pairs + p // 2, share)
            for chunk, cut in enumerate(cuts):
                for number, copy in over_planes:
                    if number == chunk:
                        copy.wait()
                total = summed[:, rows(p // 2, share), cut].astype(f32)
                for slot in range(pairs - 1):
                    total = total + got_planes[slot, :, :, cut].astype(f32)
                block[:, :, cut] = total.astype(bf16)
                for slot, peer in enumerate(far_peers):
                    copy = remote_copy(
                        block.at[:, :, cut], whole.at[:, place, cut],
                        send3.at[slot, chunk], recv3.at[slot, chunk], peer,
                    )
                    copy.start()
                    back.append((slot, chunk, copy))
                copy = remote_copy(
                    block.at[:, :, cut], whole.at[:, place, cut],
                    send9.at[pairs - 1, chunk], recv9.at[pairs - 1, chunk], sibling,
                )
                copy.start()
                passed.append(copy)
                whole[:, place, cut] = block[:, :, cut]
            for slot, chunk, copy in back:
                copy.wait()
                source = lax.rem(p + planes - 2 * (slot + 1), planes) // 2
                there = whole.at[:, rows(side * pairs + source, share), cuts[chunk]]
                relay = remote_copy(
                    there, there, send9.at[slot, chunk], recv9.at[slot, chunk], sibling
                )
                relay.start()
                passed.append(relay)
            for copy in passed:
                copy.wait()

            if far:

                @pl.when(jnp.logical_and(turn == 0, k > 0))
                def _():
                    for index in late_parts:
                        halo_copy(strings - 1, index).start()

            real, imag = whole[0].astype(f32), whole[1].astype(f32)
            magnitude = jnp.sqrt(real * real + imag * imag)
            colmax = jnp.max(jnp.sum(magnitude, axis=0, keepdims=True), axis=1, keepdims=True)
            rowmax = jnp.max(jnp.sum(magnitude, axis=1, keepdims=True), axis=0, keepdims=True)
            factor = 1.0 / (colmax * rowmax + EPS_SCALE)
            iterate[0] = real.T * factor
            iterate[1] = -imag.T * factor
            left[...] = left_factor(real, imag)

            def newton(_, carry):
                x_re, x_im = iterate[0], iterate[1]
                product = jnp.dot(
                    left[...], right_factor(x_re, x_im), preferred_element_type=f32
                )
                product = jnp.dot(
                    left_factor(x_re, x_im),
                    right_factor(product[:, :bands], product[:, bands:]),
                    preferred_element_type=f32,
                )
                iterate[0] = 2.0 * x_re - product[:, :bands]
                iterate[1] = 2.0 * x_im - product[:, bands:]
                return carry

            lax.fori_loop(0, NEWTON, newton, 0)
            real, imag = iterate[0].T.astype(bf16), iterate[1].T.astype(bf16)
            rounded[0] = real
            rounded[1] = imag
            mine_rows = rows(side, middle)
            first_hops = []
            for index in range(2):
                for slot, peer in enumerate(string_peers):
                    copy = remote_copy(
                        rounded.at[index, mine_rows, :], inverse.at[k, index, mine_rows, :],
                        send4.at[slot, index], recv4.at[slot, index], peer,
                    )
                    copy.start()
                    first_hops.append((slot, index, copy))
            inverse[k, 0] = real
            inverse[k, 1] = imag
            second_hops = []
            for slot, index, copy in first_hops:
                copy.wait()
                source = lax.rem(k + strings - slot - 1, strings)
                there = inverse.at[source, index, mine_rows, :]
                relay = remote_copy(
                    there, there, send5.at[slot, index], recv5.at[slot, index], sibling
                )
                relay.start()
                second_hops.append(relay)
            for relay in second_hops:
                relay.wait()

        def element(place):
            link = lax.rem(place + 2 * strings - STEPS, strings)
            before = lax.rem(place + 2 * strings - STEPS - 1, strings)

            x_re, x_im = inverse[link, 0], inverse[link, 1]
            ahead = chain[place + 1].reshape(2 * bands, piece)
            a_re = jnp.dot(
                jnp.concatenate([x_re, -x_im], 1), ahead, preferred_element_type=f32
            )
            a_im = jnp.dot(
                jnp.concatenate([x_im, x_re], 1), ahead, preferred_element_type=f32
            )
            x_re, x_im = inverse[before, 0], inverse[before, 1]
            behind = chain[place - 1].reshape(2 * bands, piece)
            c_re = jnp.dot(
                jnp.concatenate([x_re, x_im], 1), behind, preferred_element_type=f32
            ).astype(bf16)
            c_im = jnp.dot(
                jnp.concatenate([-x_im, x_re], 1), behind, preferred_element_type=f32
            ).astype(bf16)
            g_re = a_im - c_im.astype(f32)
            g_im = c_re.astype(f32) - a_re
            return g_re, g_im

        def norm_first(slot):
            peer = string_peers[slot]
            return remote_copy(tile, first.at[k], send6.at[slot], recv6.at[slot], peer)

        def norm_second(slot):
            peer = plane_peers[slot]
            return remote_copy(stage, second.at[p], send7.at[slot], recv7.at[slot], peer)

        def begin_norm():
            for slot in range(strings - 1):
                norm_first(slot).start()
            first[k] = tile[...]

        def carry_norm():
            for slot in range(strings - 1):
                norm_first(slot).wait()
            stage[...] = jnp.sum(first[...], 0)
            for slot in range(planes - 1):
                norm_second(slot).start()
            second[p] = stage[...]

        ahead_of = pl.ds(0, ahead_rows)
        rest_of = pl.ds(ahead_rows, bands - ahead_rows)

        def home_copy(slot):
            target = lax.rem(k + 1 + slot, strings)
            return remote_copy(
                chain.at[STEPS + target, :, ahead_of], early.at[:, :, mine],
                send10.at[slot], recv10.at[slot], (target, p),
            )

        home_own = pltpu.make_async_copy(
            chain.at[STEPS + k, :, ahead_of], early.at[:, :, mine], kept.at[0]
        )

        def slope_copy(slot):
            target = lax.rem(k + 1 + slot, strings)
            return remote_copy(
                early_out.at[slot], slopes.at[:, :, mine],
                send8.at[slot], recv8.at[slot], (target, p),
            )

        slope_own = pltpu.make_async_copy(
            early_out.at[strings - 1], slopes.at[:, :, mine], kept.at[1]
        )

        def rest_copy(slot, index):
            target = lax.rem(k + 1 + slot, strings)
            ref = (re_ref, im_ref)[index]
            return remote_copy(
                outgoing.at[slot, index], ref.at[rest_of, mine],
                send11.at[slot, index], recv11.at[slot, index], (target, p),
            )

        def rest_own(index):
            ref = (re_ref, im_ref)[index]
            return pltpu.make_async_copy(
                outgoing.at[strings - 1, index], ref.at[rest_of, mine], kept_rest.at[index]
            )

        def find_scale(turn):
            @pl.when(turn == 0)
            def _():
                for index in range(2):
                    halo_arrival(strings - 1, index).wait_recv()

            tile[...] = jnp.zeros((8, 128), f32)

            def gradient(number, carry):
                @pl.when(number == strings)
                def _():
                    begin_norm()
                    for source in range(1, strings - 1):
                        for index in range(2):
                            halo_arrival(source, index).wait_recv()

                @pl.when(number == strings + 1)
                def _():
                    carry_norm()

                inside_string = (number < strings).astype(jnp.int32)
                place = inside_string * (STEPS + lax.rem(k + 1 + number, strings))
                place += (1 - inside_string) * (
                    STEPS - 1 + (number - strings) * (strings + 1)
                )
                g_re, g_im = element(place)
                grad[place - 1, 0] = g_re
                grad[place - 1, 1] = g_im

                @pl.when(number < strings)
                def _():
                    square = g_re * g_re + g_im * g_im
                    lanes = square[:, :128]
                    for group in range(1, piece // 128):
                        lanes = lanes + square[:, group * 128 : (group + 1) * 128]
                    tile[...] += jnp.sum(lanes.reshape(bands // 8, 8, 128), 0)

                @pl.when(turn == STEPS - 1)
                def _():
                    early_out[number, 0] = g_re[:ahead_rows].astype(bf16)
                    early_out[number, 1] = g_im[:ahead_rows].astype(bf16)

                return carry

            count = strings + 2 * (turn < STEPS - 1).astype(jnp.int32)
            lax.fori_loop(0, count, gradient, 0)

            @pl.when(turn == STEPS - 1)
            def _():
                begin_norm()
                for slot in range(strings - 1):
                    slope_copy(slot).start()
                slope_own.start()
                carry_norm()

            for slot in range(planes - 1):
                norm_second(slot).wait()
            total = jnp.sum(second[...], 0)
            total = jnp.sum(jnp.sum(total, axis=0, keepdims=True), axis=1, keepdims=True)
            return TAU_STEP / jnp.sqrt(total / count_all + EPS_NORM)

        def renewed(place, index, scale):
            old = chain[place, index].astype(f32)
            return (old + grad[place - 1, index] * scale).astype(bf16)

        def renew(scale):
            def one(place, carry):
                chain[place, 0] = renewed(place, 0, scale)
                chain[place, 1] = renewed(place, 1, scale)
                return carry

            lax.fori_loop(STEPS - 1, STEPS + strings + 1, one, 0)

        def finish(scale):
            def one(slot, carry):
                place = STEPS + lax.rem(k + 1 + slot, strings)
                for index in range(2):
                    old = chain[place, index, rest_of].astype(f32)
                    fresh = old + grad[place - 1, index, rest_of] * scale
                    outgoing[slot, index] = fresh.astype(bf16)

                    @pl.when(slot < strings - 1)
                    def _():
                        rest_copy(slot, index).start()

                    @pl.when(slot == strings - 1)
                    def _():
                        rest_own(index).start()

                return carry

            lax.fori_loop(0, strings, one, 0)
            for slot in range(strings - 1):
                home_copy(slot).wait()
                slope_copy(slot).wait()
            home_own.wait()
            slope_own.wait()
            for index, ref in enumerate((re_ref, im_ref)):
                fresh = early[index].astype(f32) + slopes[index].astype(f32) * scale
                ref[ahead_of, :] = fresh.astype(bf16)
            for index in range(2):
                for slot in range(strings - 1):
                    rest_copy(slot, index).wait()
                rest_own(index).wait()

        def sent():
            for step in range(1 if moves == 0 else 0, strings):
                for index in range(2):
                    halo_copy(step, index).wait_send()
            if far:

                @pl.when(k > 0)
                def _():
                    for index in range(2):
                        pass_second(index).wait_send()

        def one_step(turn, carry):
            find_inverses(turn)
            scale = find_scale(turn)

            @pl.when(turn < STEPS - 1)
            def _():
                renew(scale)

            @pl.when(turn == STEPS - 1)
            def _():
                finish(scale)

            return carry

        lax.fori_loop(0, STEPS, one_step, 0)
        sent()

    vmem = pl.BlockSpec(memory_space=pltpu.VMEM)
    anywhere = pl.BlockSpec(memory_space=pl.ANY)
    square = (2, bands, bands)
    dma = pltpu.SemaphoreType.DMA
    out = jax.ShapeDtypeStruct((bands, width), bf16)
    return pl.pallas_call(
        kernel,
        out_shape=(out, out),
        in_specs=[pl.BlockSpec(memory_space=pltpu.SMEM), anywhere, anywhere],
        out_specs=(vmem, vmem),
        scratch_shapes=[
            pltpu.VMEM((last_extra, 2, bands, piece), bf16),
            pltpu.VMEM((2, bands, 2 * width + piece), bf16),
            pltpu.VMEM((2, bands, width + piece), bf16),
            pltpu.VMEM((2, bands, width), bf16),
            pltpu.VMEM((2, ahead_rows, width), bf16),
            pltpu.VMEM((2, ahead_rows, width), bf16),
            pltpu.VMEM((strings + 2, 2, bands, piece), f32),
            pltpu.VMEM((strings, 2, bands - ahead_rows, piece), bf16),
            pltpu.VMEM((2 * piece, piece), bf16),
            pltpu.VMEM((strings, 2, ahead_rows, piece), bf16),
            pltpu.VMEM((2, 64, piece), bf16),
            pltpu.VMEM((strings,) + square, bf16),
            pltpu.VMEM((strings, 2, middle, bands), bf16),
            pltpu.VMEM((strings, 2, middle, bands), bf16),
            pltpu.VMEM((strings - 1, 2, middle, bands), bf16),
            pltpu.VMEM((2, middle, bands), bf16),
            pltpu.VMEM((pairs - 1, 2, share, bands), bf16),
            pltpu.VMEM((2, share, bands), bf16),
            pltpu.VMEM(square, bf16),
            pltpu.VMEM((bands, 6 * bands), bf16),
            pltpu.VMEM(square, f32),
            pltpu.VMEM(square, bf16),
            pltpu.VMEM((strings,) + square, bf16),
            pltpu.VMEM((8, 128), f32),
            pltpu.VMEM((strings, 8, 128), f32),
            pltpu.VMEM((8, 128), f32),
            pltpu.VMEM((planes, 8, 128), f32),
        ]
        + [dma((strings - 1, 2))] * 2
        + [dma((bands // 64, 2))] * 2
        + [dma((bands // 64 + 1, 2))]
        + [dma((strings, 2))] * 2
        + [dma((strings,))] * 2
        + [dma((strings - 1, chunks))] * 2
        + [dma((pairs - 1, chunks))] * 4
        + [dma((strings - 1, 2))] * 4
        + [dma((strings - 1,))] * 2
        + [dma((planes - 1,))] * 2
        + [dma((strings - 1,))] * 2
        + [dma((pairs, chunks))] * 2
        + [dma((2,))]
        + [dma((strings - 1,))] * 2
        + [dma((2,))]
        + [dma((strings - 1, 2))] * 2
        + [dma((2,))] * 2,
        compiler_params=pltpu.CompilerParams(collective_id=20 + shift, has_side_effects=True),
        name=f"steps_{shift}",
    )(where, states_re, states_im)


def spread_body(strings, planes, states_re, states_im, gmap):
    width = states_re.shape[2]
    total_width = width * planes
    offset = jnp.mod(gmap[0] - lax.axis_index("pw") * width, total_width)
    blocks_off, rest = offset // width, jnp.mod(offset, width)
    start = jnp.where(lax.axis_index("kstr") < STEPS, rest, width - rest)
    piece = width // strings
    where = jnp.stack([start // piece, jnp.mod(start, piece)]).astype(jnp.float32)
    new_re, new_im = lax.switch(
        blocks_off,
        [functools.partial(whole_step, strings, planes, shift) for shift in range(planes)],
        where, states_re[0], states_im[0],
    )
    return (new_re[None], new_im[None])


def solution(mesh):
    placed = (P("kstr", None, "pw"), P("kstr", None, "pw"), P("pw"))
    strings, planes = mesh.shape["kstr"], mesh.shape["pw"]

    def body(states_re, states_im, gmap):
        kpoints, bands, width = states_re.shape
        fits = (
            kpoints == 1
            and strings > 1
            and planes > 1
            and width % (strings * 128) == 0
            and bands % (planes * 16) == 0
            and bands % 128 == 0
            and planes % 2 == 0
            and planes > 2
            and strings == 2 * STEPS
        )
        if not fits:
            return general_body(states_re, states_im, gmap)
        return spread_body(strings, planes, states_re, states_im, gmap)

    return jax.shard_map(
        body,
        mesh=mesh,
        in_specs=placed,
        out_specs=(P("kstr", None, "pw"), P("kstr", None, "pw")),
        check_vma=False,
    )
```

```python
import functools

import jax
import jax.numpy as jnp
from jax import lax
from jax.experimental import pallas as pl
from jax.experimental.pallas import tpu as pltpu
from jax.sharding import PartitionSpec as P

NEWTON = 4
STEPS = 2


HIGH = lax.Precision.HIGHEST
EPS_SCALE = 1e-06
EPS_NORM = 1e-06
TAU_STEP = 0.25


def shifted(value, axis, by):
    count = lax.axis_size(axis)
    return lax.ppermute(value, axis, [(i, (i + by) % count) for i in range(count)])


def padded_2(block, sides, width):
    for axis, dim in sides:
        count = lax.axis_size(axis)
        forward = [(i, i + 1) for i in range(count - 1)]
        forward.append((count - 1, 0))
        backward = [(target, source) for source, target in forward]
        low = lax.ppermute(
            lax.slice_in_dim(block, block.shape[dim] - width, None, axis=dim), axis, forward
        )
        high = lax.ppermute(lax.slice_in_dim(block, 0, width, axis=dim), axis, backward)
        block = jnp.concatenate([low, block, high], axis=dim)
    return block


def complex_mul(left, right):

    def matmul(first, second):
        return jnp.einsum("kij,kjl->kil", first, second, precision=HIGH)

    real = matmul(left[:, 0], right[:, 0]) - matmul(left[:, 1], right[:, 1])
    imag = matmul(left[:, 0], right[:, 1]) + matmul(left[:, 1], right[:, 0])
    return jnp.stack([real, imag], 1)


def start_inverse(whole):
    magnitude = jnp.sqrt(whole[:, 0] * whole[:, 0] + whole[:, 1] * whole[:, 1])
    colmax = jnp.max(jnp.sum(magnitude, axis=1), axis=1)
    rowmax = jnp.max(jnp.sum(magnitude, axis=2), axis=1)
    factor = (1.0 / (colmax * rowmax + EPS_SCALE))[:, None, None]
    return jnp.stack(
        [jnp.swapaxes(whole[:, 0], 1, 2) * factor, -jnp.swapaxes(whole[:, 1], 1, 2) * factor], 1
    )


def newton_full(whole):
    iterate = start_inverse(whole)
    for turn in range(NEWTON):
        iterate = 2.0 * iterate - complex_mul(iterate, complex_mul(whole, iterate))
    return iterate


def bf_product(form, left, right):
    return jnp.einsum(form, left, right, preferred_element_type=jnp.float32)


def dual_terms(rounded, states):
    real = bf_product("kmn,kmg->kng", rounded[:, 0], states[:, 0]) + bf_product(
        "kmn,kmg->kng", rounded[:, 1], states[:, 1]
    )
    imag = bf_product("kmn,kmg->kng", rounded[:, 0], states[:, 1]) - bf_product(
        "kmn,kmg->kng", rounded[:, 1], states[:, 0]
    )
    return jnp.stack([real, imag], 1).astype(jnp.bfloat16)


def rotate_columns(block, amount, width):
    blocks_off = amount // width
    rest = amount % width
    plane_size = lax.axis_size("pw")
    for bit in range((plane_size - 1).bit_length()):
        moved = shifted(block, "pw", -(1 << bit))
        block = jnp.where(jnp.bitwise_and(jnp.right_shift(blocks_off, bit), 1) == 1, moved, block)
    after = shifted(block, "pw", -1)
    joined = jnp.concatenate([block, after], block.ndim - 1)
    return lax.dynamic_slice_in_dim(joined, rest, width, block.ndim - 1)


def general_body(states_re, states_im, gmap):
    kpoints, bands, width = states_re.shape
    string_size = lax.axis_size("kstr")
    plane_size = lax.axis_size("pw")
    string_index = lax.axis_index("kstr")
    total_width = width * plane_size
    offset = jnp.mod(gmap[0] - lax.axis_index("pw") * width, total_width)
    back_offset = jnp.mod(total_width - offset, total_width)
    at_first = string_index == 0
    at_last = string_index == string_size - 1
    count_all = 2 * kpoints * string_size * bands * width * plane_size
    states = jnp.stack([states_re, states_im], 1)
    for step in range(STEPS):
        padded = padded_2(states, (("kstr", 0),), 1)
        ahead = padded[-1:]
        behind = padded[:1]
        turned = rotate_columns(ahead, offset, width)
        ahead = jnp.where(at_last, turned, ahead)
        following = jnp.concatenate([states[1:], ahead], 0)
        s_re = bf_product("kmg,kng->kmn", states[:, 0], following[:, 0]) + bf_product(
            "kmg,kng->kmn", states[:, 1], following[:, 1]
        )
        s_im = bf_product("kmg,kng->kmn", states[:, 0], following[:, 1]) - bf_product(
            "kmg,kng->kmn", states[:, 1], following[:, 0]
        )
        partial_value = jnp.stack([s_re, s_im], 1)
        whole = lax.psum(partial_value, "pw") / (width * plane_size)
        inverse = newton_full(whole)
        rounded = inverse.astype(jnp.bfloat16)
        a_re = bf_product("kmn,kmg->kng", rounded[:, 0], following[:, 0]) - bf_product(
            "kmn,kmg->kng", rounded[:, 1], following[:, 1]
        )
        a_im = bf_product("kmn,kmg->kng", rounded[:, 0], following[:, 1]) + bf_product(
            "kmn,kmg->kng", rounded[:, 1], following[:, 0]
        )
        earlier = dual_terms(rounded[:-1], states[:-1])
        previous_inverse = shifted(rounded, "kstr", 1)
        arrived = dual_terms(previous_inverse, behind)
        placed = rotate_columns(arrived, back_offset, width)
        arrived = jnp.where(at_first, placed, arrived)
        incoming = jnp.concatenate([arrived, earlier], 0).astype(jnp.float32)
        g_re = a_im - incoming[:, 1]
        g_im = incoming[:, 0] - a_re
        total = lax.psum(jnp.sum(g_re * g_re + g_im * g_im), ("kstr", "pw"))
        rms = jnp.sqrt(total / count_all + EPS_NORM)
        new_re = (states[:, 0].astype(jnp.float32) + TAU_STEP * g_re / rms).astype(jnp.bfloat16)
        new_im = (states[:, 1].astype(jnp.float32) + TAU_STEP * g_im / rms).astype(jnp.bfloat16)
        states = jnp.stack([new_re, new_im], 1)
    return (states[:, 0], states[:, 1])


def halves(value):
    high = value.astype(jnp.bfloat16)
    return high, (value - high.astype(jnp.float32)).astype(jnp.bfloat16)


def left_factor(real, imag):
    real_high, real_low = halves(real)
    imag_high, imag_low = halves(imag)
    high = jnp.concatenate([real_high, imag_high], 1)
    return jnp.concatenate([high, high, real_low, imag_low], 1)


def right_factor(real, imag):
    real_high, real_low = halves(real)
    imag_high, imag_low = halves(imag)
    high = [
        jnp.concatenate([real_high, imag_high], 1),
        jnp.concatenate([-imag_high, real_high], 1),
    ]
    low = [
        jnp.concatenate([real_low, imag_low], 1),
        jnp.concatenate([-imag_low, real_low], 1),
    ]
    return jnp.concatenate(high + low + high, 0)


def remote_copy(source, place, send, recv, target):
    return pltpu.make_async_remote_copy(
        src_ref=source,
        dst_ref=place,
        send_sem=send,
        recv_sem=recv,
        device_id=target,
        device_id_type=pl.DeviceIdType.MESH,
    )


def greet_all(greeted, awaited):
    barrier = pltpu.get_barrier_semaphore()
    for peer in greeted:
        pl.semaphore_signal(barrier, inc=1, device_id=peer, device_id_type=pl.DeviceIdType.MESH)
    pl.semaphore_wait(barrier, awaited)


def margin_of(own, ahead):
    left = jnp.concatenate([own[0], own[1]], 1)
    form = (((1,), (1,)), ((), ()))
    real = lax.dot_general(
        left, jnp.concatenate([ahead[0], ahead[1]], 1), form, preferred_element_type=jnp.float32
    )
    imag = lax.dot_general(
        left, jnp.concatenate([ahead[1], -ahead[0]], 1), form, preferred_element_type=jnp.float32
    )
    return real, imag


def whole_step(strings, planes, shift, where, states_re, states_im):
    bands, width = states_re.shape
    piece = width // strings
    total_width = width * planes
    count_all = 2 * strings * bands * total_width
    share, middle, pairs = bands // planes, bands // 2, planes // 2
    chunks = bands // 128
    last_extra = strings + 2 * STEPS
    flipped = shift >= planes // 2
    moves = (shift + 1) % planes if flipped else shift
    ahead_rows = 3 * bands // 8
    blocks = bands // 64
    far = min(moves, planes - moves) >= 2
    late_parts = (1,) if min(moves, planes - moves) == 2 else (0, 1)
    bf16, f32 = jnp.bfloat16, jnp.float32

    def kernel(where_ref, re_in, im_in, re_ref, im_ref, *scratch):
        chain, joined, chosen, aligned, early, slopes, grad, outgoing, picked = scratch[:9]
        early_out, passing, scratch = scratch[9], scratch[10], scratch[5:]
        part, got_pair, half, got_string, summed, got_planes = scratch[6:12]
        block, whole, left, iterate, rounded, inverse = scratch[12:18]
        tile, first, stage, second = scratch[18:22]
        send_base, recv_base, send_join, recv_join, inside = scratch[22:27]
        send_halo, recv_halo = scratch[27:29]
        scratch = scratch[:29] + scratch[27:]
        send0, recv0, send1, recv1, send2, recv2, send3, recv3 = scratch[31:39]
        send4, recv4, send5, recv5, send6, recv6, send7, recv7 = scratch[39:47]
        send8, recv8, send9, recv9, kept, send10, recv10, kept_rest = scratch[47:55]
        send11, recv11, send_pass, recv_pass = scratch[55:]
        k, p = lax.axis_index("kstr"), lax.axis_index("pw")
        inputs = (re_in, im_in)
        forward = (k < STEPS).astype(jnp.int32)
        string_peers = [(lax.rem(k + step, strings), p) for step in range(1, strings)]
        plane_peers = [(k, lax.rem(p + step, planes)) for step in range(1, planes)]
        far_peers = [(k, lax.rem(p + 2 * step, planes)) for step in range(1, pairs)]
        side = lax.rem(p, 2)
        sibling = (k, p + 1 - 2 * side)

        def rows(index, size):
            return pl.ds(pl.multiple_of(index * size, size), size)

        offsets = {(step, 0) for step in range(1, strings)}
        offsets |= {(0, step) for step in range(1, planes)}
        for step in range(strings):
            offsets |= {(step, moves), (step, (planes - moves) % planes)}
        offsets = sorted(offsets - {(0, 0)})
        greet_all(
            [(lax.rem(k + a, strings), lax.rem(p + b, planes)) for a, b in offsets], len(offsets)
        )

        down = lax.rem(p + planes - moves, planes)
        target_plane = forward * down + (1 - forward) * lax.rem(p + moves, planes)
        leading = 1 - forward if flipped else forward
        taker = (k, lax.rem(p + planes + 1 - 2 * leading, planes))
        own_half = rows(1 - leading, width)
        other_half = rows(leading, width)
        mine = rows(k, piece)
        def join(number, index):
            row = rows(number, 64)
            return remote_copy(
                inputs[index].at[row, :], joined.at[index, row, other_half],
                send_join.at[number, index], recv_join.at[number, index], taker,
            )

        def join_own(number, index):
            row = rows(number, 64)
            return pltpu.make_async_copy(
                inputs[index].at[row, :], joined.at[index, row, own_half],
                inside.at[number, index],
            )

        base, insides = [], []
        for index, ref in enumerate(inputs):
            insides.append(
                pltpu.make_async_copy(
                    ref.at[:, mine], chain.at[STEPS + k, index], inside.at[blocks, index]
                )
            )
            for slot, peer in enumerate(string_peers):
                base.append(
                    remote_copy(
                        ref.at[:, rows(peer[0], piece)], chain.at[STEPS + k, index],
                        send_base.at[slot, index], recv_base.at[slot, index], peer,
                    )
                )
        for number in range(blocks):
            for index in range(2):
                join(number, index).start()
                join_own(number, index).start()
        for copy in base + insides:
            copy.start()
        joined[:, :, 2 * width :] = jnp.zeros((2, bands, piece), bf16)
        row_of = lax.broadcasted_iota(jnp.int32, (64, piece // 2), 0)
        column_of = lax.broadcasted_iota(jnp.int32, (64, piece // 2), 1)
        apart = (row_of - column_of).astype(f32) - where_ref[1]

        def pick(number, carry):
            there = apart + (number * 64).astype(f32)
            picked[rows(number, 64)] = jnp.maximum(1.0 - jnp.abs(there), 0.0).astype(bf16)
            return carry

        lax.fori_loop(0, 3 * piece // 128, pick, 0)
        weights = [
            jnp.full((64, piece), jnp.maximum(1.0 - jnp.abs(where_ref[0] - h), 0.0), f32)
            for h in range(strings + 1)
        ]
        weights = [weight.astype(bf16) for weight in weights]
        def extra_of(source):
            if isinstance(source, int):
                ahead = int(source < STEPS)
            else:
                ahead = (source < STEPS).astype(jnp.int32)
            return source + ahead * (STEPS + strings) - (1 - ahead) * (strings - STEPS)

        front = STEPS + strings

        def halo_copy(step, index):
            target = lax.rem(k + step, strings)
            return remote_copy(
                aligned.at[index, :, rows(target, piece)], chain.at[extra_of(k), index],
                send_halo.at[step, index], recv_halo.at[k, index], (target, target_plane),
            )

        def halo_arrival(source, index):
            place = chain.at[extra_of(source), index]
            return remote_copy(
                place, place, send_halo.at[0, index], recv_halo.at[source, index], sibling
            )

        def halo_part(step, index, number):
            target = lax.rem(k + step, strings)
            row = rows(number, 64)
            return remote_copy(
                aligned.at[index, row, rows(target, piece)], chain.at[extra_of(k), index, row],
                send_halo.at[step, index], recv_halo.at[k, index], (target, target_plane),
            )

        def pass_first(step, index):
            target = lax.rem(k + step, strings)
            return remote_copy(
                aligned.at[index, pl.ds(0, 64), rows(target, piece)], passing.at[index],
                send_halo.at[step, index], recv_pass.at[index], (target, p),
            )

        def pass_arrival(index):
            return remote_copy(
                passing.at[index], passing.at[index], send_pass.at[index],
                recv_pass.at[index], sibling,
            )

        def pass_second(index):
            return remote_copy(
                passing.at[index], chain.at[front, index, pl.ds(0, 64)],
                send_pass.at[index], recv_halo.at[0, index], (k, down),
            )

        def own_part(index, number):
            row = rows(number, 64)
            return pltpu.make_async_copy(
                aligned.at[index, row, mine], chain.at[extra_of(k), index, row],
                recv_halo.at[k, index],
            )

        def send_block(number, carry):
            for index in range(2):
                join_own(number, index).wait()
                join(number, index).wait()
            row = rows(number, 64)

            def choose(place, carry):
                index, cut = lax.rem(place, 2), place // 2
                total = joined[index, row, rows(cut, piece)] * weights[0]
                for h in range(1, strings + 1):
                    total = total + joined[index, row, rows(cut + h, piece)] * weights[h]
                chosen[index, row, rows(cut, piece)] = total
                return carry

            lax.fori_loop(0, 2 * (strings + 1), choose, 0)

            def align(step, carry):
                cut = lax.rem(k + step, strings)
                start = pl.multiple_of(cut * piece, piece)
                for side_of in range(2):
                    begin = pl.multiple_of(start + side_of * (piece // 2), piece // 2)
                    wide = chosen[:, row, pl.ds(begin, 3 * piece // 2)]
                    moved = jnp.dot(
                        wide.reshape(128, 3 * piece // 2), picked[...], preferred_element_type=f32
                    )
                    moved = moved.astype(bf16).reshape(2, 64, piece // 2)
                    aligned[:, row, pl.ds(begin, piece // 2)] = moved
                for index in range(2):
                    if moves == 0:

                        @pl.when(step == strings)
                        def _():
                            own_part(index, number).start()

                        @pl.when(step < strings)
                        def _():
                            halo_part(step, index, number).start()

                    elif not far:
                        halo_part(step, index, number).start()
                    else:
                        first = jnp.logical_and(k == 0, number == 0)
                        passed = jnp.logical_and(first, step > 0)
                        last_step = step == strings - 1 if index in late_parts else step < 0
                        held = jnp.logical_and(k > 0, last_step)

                        @pl.when(passed)
                        def _():
                            pass_first(step, index).start()

                        @pl.when(jnp.logical_not(jnp.logical_or(passed, held)))
                        def _():
                            halo_part(step, index, number).start()

                return carry

            if moves == 0:
                lax.fori_loop(1, strings + 1, align, 0)
            else:
                lax.fori_loop(0, strings, align, 0)
            return carry

        lax.fori_loop(0, blocks, send_block, 0)

        for copy in insides:
            copy.wait()
        for copy in base:
            copy.wait()

        def front_arrives():
            if far:

                @pl.when(k > 0)
                def _():
                    for index in range(2):
                        pass_arrival(index).wait_recv()
                        pass_second(index).start()

            for index in range(2):
                halo_arrival(0, index).wait_recv()

        cuts = [pl.ds(chunk * 128, 128) for chunk in range(chunks)]

        def pair_copy(which):
            return remote_copy(
                part.at[which, :, rows(1 - side, middle), :], got_pair.at[which],
                send0.at[which], recv0.at[which], sibling,
            )

        def string_copy(which, slot, chunk):
            cut = cuts[chunk]
            return remote_copy(
                half.at[which, :, :, cut], got_string.at[slot, :, :, cut],
                send1.at[slot, chunk], recv1.at[slot, chunk], (which, p),
            )

        def carry_on(which):
            pair_copy(which).wait()
            both = part[which, :, rows(side, middle), :].astype(f32)
            half[which] = (both + got_pair[which].astype(f32)).astype(bf16)

            @pl.when(which != k)
            def _():
                slot = lax.rem(which - k - 1 + strings, strings)
                for chunk in range(chunks):
                    string_copy(which, slot, chunk).start()

        def find_inverses(turn):
            later = (turn > 0).astype(jnp.int32)
            lag = 1 + later

            def in_turn(number):
                return later * lax.rem(k + 1 + number + strings, strings) + (1 - later) * number

            def margin(number, carry):
                @pl.when(number >= lag)
                def _():
                    carry_on(in_turn(number - lag))

                @pl.when(number < strings)
                def _():
                    which = in_turn(number)
                    if_front = jnp.logical_and(which == strings - 1, turn == 0)
                    pl.when(if_front)(front_arrives)
                    real, imag = margin_of(chain[STEPS + which], chain[STEPS + 1 + which])
                    part[which, 0] = (real * (1.0 / total_width)).astype(bf16)
                    part[which, 1] = (imag * (1.0 / total_width)).astype(bf16)
                    pair_copy(which).start()

                return carry

            lax.fori_loop(0, strings + lag, margin, 0)

            over_planes = []
            for chunk, cut in enumerate(cuts):
                for slot, peer in enumerate(string_peers):
                    string_copy(peer[0], slot, chunk).wait()
                total = half[k, :, :, cut].astype(f32)
                for slot in range(strings - 1):
                    total = total + got_string[slot, :, :, cut].astype(f32)
                summed[:, :, cut] = total.astype(bf16)
                for slot, peer in enumerate(far_peers):
                    copy = remote_copy(
                        summed.at[:, rows(peer[1] // 2, share), cut],
                        got_planes.at[slot, :, :, cut],
                        send2.at[slot, chunk], recv2.at[slot, chunk], peer,
                    )
                    copy.start()
                    over_planes.append((chunk, copy))

            @pl.when(turn == STEPS - 1)
            def _():
                for slot in range(strings - 1):
                    home_copy(slot).start()
                home_own.start()

            back, passed = [], []
            place = rows(side * pairs + p // 2, share)
            for chunk, cut in enumerate(cuts):
                for number, copy in over_planes:
                    if number == chunk:
                        copy.wait()
                total = summed[:, rows(p // 2, share), cut].astype(f32)
                for slot in range(pairs - 1):
                    total = total + got_planes[slot, :, :, cut].astype(f32)
                block[:, :, cut] = total.astype(bf16)
                for slot, peer in enumerate(far_peers):
                    copy = remote_copy(
                        block.at[:, :, cut], whole.at[:, place, cut],
                        send3.at[slot, chunk], recv3.at[slot, chunk], peer,
                    )
                    copy.start()
                    back.append((slot, chunk, copy))
                copy = remote_copy(
                    block.at[:, :, cut], whole.at[:, place, cut],
                    send9.at[pairs - 1, chunk], recv9.at[pairs - 1, chunk], sibling,
                )
                copy.start()
                passed.append(copy)
                whole[:, place, cut] = block[:, :, cut]
            for slot, chunk, copy in back:
                copy.wait()
                source = lax.rem(p + planes - 2 * (slot + 1), planes) // 2
                there = whole.at[:, rows(side * pairs + source, share), cuts[chunk]]
                relay = remote_copy(
                    there, there, send9.at[slot, chunk], recv9.at[slot, chunk], sibling
                )
                relay.start()
                passed.append(relay)
            for copy in passed:
                copy.wait()

            if far:

                @pl.when(jnp.logical_and(turn == 0, k > 0))
                def _():
                    for index in late_parts:
                        halo_copy(strings - 1, index).start()

            real, imag = whole[0].astype(f32), whole[1].astype(f32)
            magnitude = jnp.sqrt(real * real + imag * imag)
            colmax = jnp.max(jnp.sum(magnitude, axis=0, keepdims=True), axis=1, keepdims=True)
            rowmax = jnp.max(jnp.sum(magnitude, axis=1, keepdims=True), axis=0, keepdims=True)
            factor = 1.0 / (colmax * rowmax + EPS_SCALE)
            iterate[0] = real.T * factor
            iterate[1] = -imag.T * factor
            left[...] = left_factor(real, imag)

            def newton(_, carry):
                x_re, x_im = iterate[0], iterate[1]
                product = jnp.dot(
                    left[...], right_factor(x_re, x_im), preferred_element_type=f32
                )
                product = jnp.dot(
                    left_factor(x_re, x_im),
                    right_factor(product[:, :bands], product[:, bands:]),
                    preferred_element_type=f32,
                )
                iterate[0] = 2.0 * x_re - product[:, :bands]
                iterate[1] = 2.0 * x_im - product[:, bands:]
                return carry

            lax.fori_loop(0, NEWTON, newton, 0)
            real, imag = iterate[0].T.astype(bf16), iterate[1].T.astype(bf16)
            rounded[0] = real
            rounded[1] = imag
            mine_rows = rows(side, middle)
            first_hops = []
            for index in range(2):
                for slot, peer in enumerate(string_peers):
                    copy = remote_copy(
                        rounded.at[index, mine_rows, :], inverse.at[k, index, mine_rows, :],
                        send4.at[slot, index], recv4.at[slot, index], peer,
                    )
                    copy.start()
                    first_hops.append((slot, index, copy))
            inverse[k, 0] = real
            inverse[k, 1] = imag
            second_hops = []
            for slot, index, copy in first_hops:
                copy.wait()
                source = lax.rem(k + strings - slot - 1, strings)
                there = inverse.at[source, index, mine_rows, :]
                relay = remote_copy(
                    there, there, send5.at[slot, index], recv5.at[slot, index], sibling
                )
                relay.start()
                second_hops.append(relay)
            for relay in second_hops:
                relay.wait()

        def element(place):
            link = lax.rem(place + 2 * strings - STEPS, strings)
            before = lax.rem(place + 2 * strings - STEPS - 1, strings)

            x_re, x_im = inverse[link, 0], inverse[link, 1]
            ahead = chain[place + 1].reshape(2 * bands, piece)
            a_re = jnp.dot(
                jnp.concatenate([x_re, -x_im], 1), ahead, preferred_element_type=f32
            )
            a_im = jnp.dot(
                jnp.concatenate([x_im, x_re], 1), ahead, preferred_element_type=f32
            )
            x_re, x_im = inverse[before, 0], inverse[before, 1]
            behind = chain[place - 1].reshape(2 * bands, piece)
            c_re = jnp.dot(
                jnp.concatenate([x_re, x_im], 1), behind, preferred_element_type=f32
            ).astype(bf16)
            c_im = jnp.dot(
                jnp.concatenate([-x_im, x_re], 1), behind, preferred_element_type=f32
            ).astype(bf16)
            g_re = a_im - c_im.astype(f32)
            g_im = c_re.astype(f32) - a_re
            return g_re, g_im

        def norm_first(slot):
            peer = string_peers[slot]
            return remote_copy(tile, first.at[k], send6.at[slot], recv6.at[slot], peer)

        def norm_second(slot):
            peer = plane_peers[slot]
            return remote_copy(stage, second.at[p], send7.at[slot], recv7.at[slot], peer)

        def begin_norm():
            for slot in range(strings - 1):
                norm_first(slot).start()
            first[k] = tile[...]

        def carry_norm():
            for slot in range(strings - 1):
                norm_first(slot).wait()
            stage[...] = jnp.sum(first[...], 0)
            for slot in range(planes - 1):
                norm_second(slot).start()
            second[p] = stage[...]

        ahead_of = pl.ds(0, ahead_rows)
        rest_of = pl.ds(ahead_rows, bands - ahead_rows)

        def home_copy(slot):
            target = lax.rem(k + 1 + slot, strings)
            return remote_copy(
                chain.at[STEPS + target, :, ahead_of], early.at[:, :, mine],
                send10.at[slot], recv10.at[slot], (target, p),
            )

        home_own = pltpu.make_async_copy(
            chain.at[STEPS + k, :, ahead_of], early.at[:, :, mine], kept.at[0]
        )

        def slope_copy(slot):
            target = lax.rem(k + 1 + slot, strings)
            return remote_copy(
                early_out.at[slot], slopes.at[:, :, mine],
                send8.at[slot], recv8.at[slot], (target, p),
            )

        slope_own = pltpu.make_async_copy(
            early_out.at[strings - 1], slopes.at[:, :, mine], kept.at[1]
        )

        def rest_copy(slot, index):
            target = lax.rem(k + 1 + slot, strings)
            ref = (re_ref, im_ref)[index]
            return remote_copy(
                outgoing.at[slot, index], ref.at[rest_of, mine],
                send11.at[slot, index], recv11.at[slot, index], (target, p),
            )

        def rest_own(index):
            ref = (re_ref, im_ref)[index]
            return pltpu.make_async_copy(
                outgoing.at[strings - 1, index], ref.at[rest_of, mine], kept_rest.at[index]
            )

        def find_scale(turn):
            @pl.when(turn == 0)
            def _():
                for index in range(2):
                    halo_arrival(strings - 1, index).wait_recv()

            tile[...] = jnp.zeros((8, 128), f32)

            def gradient(number, carry):
                @pl.when(number == strings)
                def _():
                    begin_norm()
                    for source in range(1, strings - 1):
                        for index in range(2):
                            halo_arrival(source, index).wait_recv()

                @pl.when(number == strings + 1)
                def _():
                    carry_norm()

                inside_string = (number < strings).astype(jnp.int32)
                place = inside_string * (STEPS + lax.rem(k + 1 + number, strings))
                place += (1 - inside_string) * (
                    STEPS - 1 + (number - strings) * (strings + 1)
                )
                g_re, g_im = element(place)
                grad[place - 1, 0] = g_re
                grad[place - 1, 1] = g_im

                @pl.when(number < strings)
                def _():
                    square = g_re * g_re + g_im * g_im
                    lanes = square[:, :128]
                    for group in range(1, piece // 128):
                        lanes = lanes + square[:, group * 128 : (group + 1) * 128]
                    tile[...] += jnp.sum(lanes.reshape(bands // 8, 8, 128), 0)

                @pl.when(turn == STEPS - 1)
                def _():
                    early_out[number, 0] = g_re[:ahead_rows].astype(bf16)
                    early_out[number, 1] = g_im[:ahead_rows].astype(bf16)

                return carry

            count = strings + 2 * (turn < STEPS - 1).astype(jnp.int32)
            lax.fori_loop(0, count, gradient, 0)

            @pl.when(turn == STEPS - 1)
            def _():
                begin_norm()
                for slot in range(strings - 1):
                    slope_copy(slot).start()
                slope_own.start()
                carry_norm()

            for slot in range(planes - 1):
                norm_second(slot).wait()
            total = jnp.sum(second[...], 0)
            total = jnp.sum(jnp.sum(total, axis=0, keepdims=True), axis=1, keepdims=True)
            return TAU_STEP / jnp.sqrt(total / count_all + EPS_NORM)

        def renewed(place, index, scale):
            old = chain[place, index].astype(f32)
            return (old + grad[place - 1, index] * scale).astype(bf16)

        def renew(scale):
            def one(place, carry):
                chain[place, 0] = renewed(place, 0, scale)
                chain[place, 1] = renewed(place, 1, scale)
                return carry

            lax.fori_loop(STEPS - 1, STEPS + strings + 1, one, 0)

        def finish(scale):
            def one(slot, carry):
                place = STEPS + lax.rem(k + 1 + slot, strings)
                for index in range(2):
                    old = chain[place, index, rest_of].astype(f32)
                    fresh = old + grad[place - 1, index, rest_of] * scale
                    outgoing[slot, index] = fresh.astype(bf16)

                    @pl.when(slot < strings - 1)
                    def _():
                        rest_copy(slot, index).start()

                    @pl.when(slot == strings - 1)
                    def _():
                        rest_own(index).start()

                return carry

            lax.fori_loop(0, strings, one, 0)
            for slot in range(strings - 1):
                home_copy(slot).wait()
                slope_copy(slot).wait()
            home_own.wait()
            slope_own.wait()
            for index, ref in enumerate((re_ref, im_ref)):
                fresh = early[index].astype(f32) + slopes[index].astype(f32) * scale
                ref[ahead_of, :] = fresh.astype(bf16)
            for index in range(2):
                for slot in range(strings - 1):
                    rest_copy(slot, index).wait()
                rest_own(index).wait()

        def sent():
            for step in range(1 if moves == 0 else 0, strings):
                for index in range(2):
                    halo_copy(step, index).wait_send()
            if far:

                @pl.when(k > 0)
                def _():
                    for index in range(2):
                        pass_second(index).wait_send()

        def one_step(turn, carry):
            find_inverses(turn)
            scale = find_scale(turn)

            @pl.when(turn < STEPS - 1)
            def _():
                renew(scale)

            @pl.when(turn == STEPS - 1)
            def _():
                finish(scale)

            return carry

        lax.fori_loop(0, STEPS, one_step, 0)
        sent()

    vmem = pl.BlockSpec(memory_space=pltpu.VMEM)
    anywhere = pl.BlockSpec(memory_space=pl.ANY)
    square = (2, bands, bands)
    dma = pltpu.SemaphoreType.DMA
    out = jax.ShapeDtypeStruct((bands, width), bf16)
    return pl.pallas_call(
        kernel,
        out_shape=(out, out),
        in_specs=[pl.BlockSpec(memory_space=pltpu.SMEM), anywhere, anywhere],
        out_specs=(vmem, vmem),
        scratch_shapes=[
            pltpu.VMEM((last_extra, 2, bands, piece), bf16),
            pltpu.VMEM((2, bands, 2 * width + piece), bf16),
            pltpu.VMEM((2, bands, width + piece), bf16),
            pltpu.VMEM((2, bands, width), bf16),
            pltpu.VMEM((2, ahead_rows, width), bf16),
            pltpu.VMEM((2, ahead_rows, width), bf16),
            pltpu.VMEM((strings + 2, 2, bands, piece), f32),
            pltpu.VMEM((strings, 2, bands - ahead_rows, piece), bf16),
            pltpu.VMEM((3 * piece // 2, piece // 2), bf16),
            pltpu.VMEM((strings, 2, ahead_rows, piece), bf16),
            pltpu.VMEM((2, 64, piece), bf16),
            pltpu.VMEM((strings,) + square, bf16),
            pltpu.VMEM((strings, 2, middle, bands), bf16),
            pltpu.VMEM((strings, 2, middle, bands), bf16),
            pltpu.VMEM((strings - 1, 2, middle, bands), bf16),
            pltpu.VMEM((2, middle, bands), bf16),
            pltpu.VMEM((pairs - 1, 2, share, bands), bf16),
            pltpu.VMEM((2, share, bands), bf16),
            pltpu.VMEM(square, bf16),
            pltpu.VMEM((bands, 6 * bands), bf16),
            pltpu.VMEM(square, f32),
            pltpu.VMEM(square, bf16),
            pltpu.VMEM((strings,) + square, bf16),
            pltpu.VMEM((8, 128), f32),
            pltpu.VMEM((strings, 8, 128), f32),
            pltpu.VMEM((8, 128), f32),
            pltpu.VMEM((planes, 8, 128), f32),
        ]
        + [dma((strings - 1, 2))] * 2
        + [dma((bands // 64, 2))] * 2
        + [dma((bands // 64 + 1, 2))]
        + [dma((strings, 2))] * 2
        + [dma((strings,))] * 2
        + [dma((strings - 1, chunks))] * 2
        + [dma((pairs - 1, chunks))] * 4
        + [dma((strings - 1, 2))] * 4
        + [dma((strings - 1,))] * 2
        + [dma((planes - 1,))] * 2
        + [dma((strings - 1,))] * 2
        + [dma((pairs, chunks))] * 2
        + [dma((2,))]
        + [dma((strings - 1,))] * 2
        + [dma((2,))]
        + [dma((strings - 1, 2))] * 2
        + [dma((2,))] * 2,
        compiler_params=pltpu.CompilerParams(collective_id=20 + shift, has_side_effects=True),
        name=f"steps_{shift}",
    )(where, states_re, states_im)


def spread_body(strings, planes, states_re, states_im, gmap):
    width = states_re.shape[2]
    total_width = width * planes
    offset = jnp.mod(gmap[0] - lax.axis_index("pw") * width, total_width)
    blocks_off, rest = offset // width, jnp.mod(offset, width)
    start = jnp.where(lax.axis_index("kstr") < STEPS, rest, width - rest)
    piece = width // strings
    where = jnp.stack([start // piece, jnp.mod(start, piece)]).astype(jnp.float32)
    new_re, new_im = lax.switch(
        blocks_off,
        [functools.partial(whole_step, strings, planes, shift) for shift in range(planes)],
        where, states_re[0], states_im[0],
    )
    return (new_re[None], new_im[None])


def solution(mesh):
    placed = (P("kstr", None, "pw"), P("kstr", None, "pw"), P("pw"))
    strings, planes = mesh.shape["kstr"], mesh.shape["pw"]

    def body(states_re, states_im, gmap):
        kpoints, bands, width = states_re.shape
        fits = (
            kpoints == 1
            and strings > 1
            and planes > 1
            and width % (strings * 256) == 0
            and bands % (planes * 16) == 0
            and bands % 128 == 0
            and planes % 2 == 0
            and planes > 2
            and strings == 2 * STEPS
        )
        if not fits:
            return general_body(states_re, states_im, gmap)
        return spread_body(strings, planes, states_re, states_im, gmap)

    return jax.shard_map(
        body,
        mesh=mesh,
        in_specs=placed,
        out_specs=(P("kstr", None, "pw"), P("kstr", None, "pw")),
        check_vma=False,
    )
```
